32 devices in a mesh: stream: 2 (over y), dp: 8 (over z, x), head: 2 (over core).
Axes of the slice: x: 2, y: 2, z: 4, core: 2. Of those that a mesh axis runs over, the one named last changes fastest.
Arguments:
- patches: bfloat16 [32, 512, 768], P(('dp', 'head')), may hold values from -6 to 6
- order: int32 [32, 512], P(('dp', 'head')), may hold values from 0 to 511, each once within a row
- cotangent: bfloat16 [2, 32, 256, 768], P('stream', ('dp', 'head')), may hold values from -6 to 6
- norm_gains: float32 [2, 2, 768], P('stream'), may hold values from 0.5 to 1.5
- norm_biases: float32 [2, 2, 768], P('stream'), may hold values from -3 to 3
- layer_scales: float32 [2, 2, 768], P('stream'), may hold values from 0.5 to 1.5
- qkv_weight: bfloat16 [2, 3, 768, 768], P('stream', None, None, 'head'), may hold values from -0.21875 to 0.21875
- out_weight: bfloat16 [2, 768, 768], P('stream', 'head'), may hold values from -2.5 to 2.5
- up_weight: bfloat16 [2, 768, 3072], P('stream', None, 'head'), may hold values from -0.21875 to 0.21875
- up_bias: bfloat16 [2, 3072], P('stream', 'head'), may hold values from -3 to 3
- down_weight: bfloat16 [2, 3072, 768], P('stream', 'head'), may hold values from -0.109375 to 0.109375
- down_bias: float32 [2, 768], P('stream'), may hold values from -2 to 2
- mask_token: float32 [768], replicated, may hold values from -6 to 6
Outputs:
- latents: bfloat16 [32, 256, 768], P(('dp', 'head'))
- features: bfloat16 [2, 32, 256, 768], P('stream', ('dp', 'head'))
- input_grads: float32 [2, 32, 512, 768], P('stream', ('dp', 'head'))
- norm_gains_grad: float32 [2, 2, 768], P('stream')
- norm_biases_grad: float32 [2, 2, 768], P('stream')
- layer_scales_grad: float32 [2, 2, 768], P('stream')
- qkv_grad: float32 [2, 3, 768, 768], P('stream', None, None, 'head')
- out_grad: float32 [2, 768, 768], P('stream', 'head')
- up_grad: float32 [2, 768, 3072], P('stream', None, 'head')
- up_bias_grad: float32 [2, 3072], P('stream', 'head')
- down_grad: float32 [2, 3072, 768], P('stream', 'head')
- down_bias_grad: float32 [2, 768], P('stream')
- mask_token_grad: float32 [768], replicated
The draws below stay inside these ranges and needn't reach their ends.
Inputs may be any that keep to these rules, and one draw needn't show every extreme that they name: `order`: each row holds every patch position of its image once; the first half of a row are the visible patches, the second half the masked ones.
All inputs are finite; a program needn't handle non-finite values.
Results may differ from the reference program's by a relative error of at most 0.014.
Values may be sent and summed in bfloat16 or wider, within the bound.
A program may use at most 192 MiB of HBM per device.

```python
import functools
import math
import jax
import jax.numpy as jnp
from jax import lax

D = 768
FF = 3072
HEADS = 12
PATCHES = 512
IMG_DEV = 4
IMAGES = 32


def steps_of(rng, shape, pieces, low, largest):
    def one(axis_at, blocks):
        draws = jax.random.uniform(jax.random.fold_in(jax.random.fold_in(rng, 6), axis_at), (blocks,), jnp.float32, low / len(pieces), largest / len(pieces))
        return jnp.repeat(jnp.exp(draws), shape[axis_at] // blocks).reshape((-1,) + (1,) * (len(shape) - axis_at - 1))

    gain = one(*pieces[0])
    for cut in pieces[1:]:
        gain = gain * one(*cut)
    return gain


def gaussian(rng, shape, width, bound, split=(), held_as=jnp.bfloat16):
    gain = steps_of(rng, shape, split, -0.22, 0.18) if split else 1.0
    drawn = jax.random.normal(rng, shape, jnp.float32) * width * gain
    return jnp.minimum(jnp.maximum(drawn, -bound), bound).astype(held_as)


def setup_inputs(seed: int = 0) -> dict:
    streams_of = jax.random.split(jax.random.key(seed), 14)
    return {
        "patches": gaussian(streams_of[0], (IMAGES, PATCHES, D), 1.0, 6.0, ((0, 16),)),
        "order": jax.vmap(lambda own: jax.random.permutation(own, PATCHES))(jax.random.split(streams_of[1], IMAGES)).reshape((IMAGES, PATCHES)).astype(jnp.int32),
        "cotangent": gaussian(streams_of[2], (2, IMAGES, PATCHES // 2, D), 1.0, 6.0, ((0, 2), (1, 16))),
        "norm_gains": jnp.clip(1.0 + 0.1 * jax.random.normal(streams_of[3], (2, 2, D), jnp.float32), 0.5, 1.5),
        "norm_biases": gaussian(streams_of[4], (2, 2, D), 0.5, 3.0, ((0, 2),), jnp.float32),
        "layer_scales": jnp.clip(jnp.exp(math.log(1.5) - 1.0986123 * jax.random.uniform(streams_of[5], (2, 2, D), jnp.float32) ** steps_of(streams_of[5], (2, 2, D), ((0, 2),), -0.2, 0.2)), 0.5, 1.5),
        "qkv_weight": gaussian(streams_of[6], (2, 3, D, D), D ** -0.5, 0.21875, ((0, 2), (3, 2))),
        "out_weight": gaussian(streams_of[7], (2, D, D), (max(D // 128, 1)) ** -0.5, 2.5, ((0, 2), (1, 2))),
        "up_weight": gaussian(streams_of[8], (2, D, FF), D ** -0.5, 0.21875, ((0, 2), (2, 2))),
        "up_bias": gaussian(streams_of[9], (2, FF), 0.5, 3.0, ((0, 2), (1, 2))),
        "down_weight": gaussian(streams_of[10], (2, FF, D), FF ** -0.5, 0.109375, ((0, 2), (1, 2))),
        "down_bias": gaussian(streams_of[11], (2, D), 0.3, 2.0, ((0, 2),), jnp.float32),
        "mask_token": gaussian(streams_of[12], (D,), 1.0, 6.0, (), jnp.float32),
    }


@jax.custom_vjp
def low(v):
    return lax.optimization_barrier(v.astype(jnp.bfloat16)).astype(jnp.float32)

@jax.custom_vjp
def low_back(v):
    return v

def low_keep(v):
    return (low(v), None)

def low_pass(kept, grad):
    return (grad,)

def back_keep(v):
    return (v, None)

def back_low(kept, grad):
    return (low(grad),)
low.defvjp(low_keep, low_pass)
low_back.defvjp(back_keep, back_low)

def matmul_hi(form, left, right):
    return jnp.einsum(form, left, right, precision=lax.Precision.HIGHEST)

def layer_norm(values, norm_gain, norm_bias):
    row_mean = lax.optimization_barrier(jnp.mean(values, -1, keepdims=True))
    centred = values - row_mean
    variance = lax.optimization_barrier(jnp.mean(centred * centred, -1, keepdims=True))
    return centred * lax.rsqrt(variance + 1e-06) * norm_gain + norm_bias

def place_code(positions, model_width):
    half_width = model_width // 2
    frequency = jnp.exp(jnp.arange(half_width, dtype=jnp.float32) * (-math.log(10000.0) / half_width))
    angles = positions.astype(jnp.float32)[..., None] * frequency
    return jnp.concatenate([jnp.sin(angles), jnp.cos(angles)], -1)

def vit_block(rows_query, rows_context, params):
    gain_rows, biases, scales, qkv_weight, out_weight, up_weight, up_bias, down_weight, down_bias = params
    ctx_count = rows_context.shape[1]
    rows_all = jnp.concatenate([rows_context, rows_query], 1)
    images, key_count, model_width = rows_all.shape
    row_count = key_count - ctx_count
    head_dim = model_width // HEADS
    normed = low(layer_norm(rows_all, gain_rows[0], biases[0]))
    queries = low_back(low(matmul_hi('ikd,de->ike', normed[:, ctx_count:], qkv_weight[0])))
    key_rows = low_back(low(matmul_hi('ikd,de->ike', normed, qkv_weight[1])))
    value_rows = low_back(low(matmul_hi('ikd,de->ike', normed, qkv_weight[2])))
    scores = matmul_hi('iqhe,ikhe->ihqk', queries.reshape(images, row_count, HEADS, head_dim), key_rows.reshape(images, key_count, HEADS, head_dim))
    scores = low_back(scores * head_dim ** (-0.5))
    attention = low(jax.nn.softmax(scores, -1))
    mixture = matmul_hi('ihqk,ikhe->iqhe', attention, value_rows.reshape(images, key_count, HEADS, head_dim))
    mixture = low_back(low(mixture.reshape(images, row_count, model_width)))
    attended = low_back(matmul_hi('iqe,ed->iqd', mixture, out_weight))
    hidden = rows_query + scales[0] * attended
    normed_two = low(layer_norm(hidden, gain_rows[1], biases[1]))
    pre_act = low_back(matmul_hi('iqd,df->iqf', normed_two, up_weight)) + up_bias
    activation = low(jax.nn.gelu(pre_act, approximate=False))
    branch_out = low_back(matmul_hi('iqf,fd->iqd', activation, down_weight)) + down_bias
    return hidden + scales[1] * branch_out

def forward_group(enc_params, reg_params, patch_rows, token, shift_context, shift_query, visible, masked):
    model_width = patch_rows.shape[2]
    seen_rows = jnp.take_along_axis(patch_rows, visible[..., None], 1)
    latent = low(vit_block(seen_rows, seen_rows[:, :0], enc_params))
    context = low_back(latent) + place_code(visible, model_width) + shift_context
    queries = token + place_code(masked, model_width) + shift_query
    predicted = low(vit_block(queries, context, reg_params))
    return (latent, predicted)

def reference(patches, order, cotangent, norm_gains, norm_biases, layer_scales, qkv_weight, out_weight, up_weight, up_bias, down_weight, down_bias, mask_token):
    stacks = tuple((tensor.astype(jnp.float32) for tensor in (norm_gains, norm_biases, layer_scales, qkv_weight, out_weight, up_weight, up_bias, down_weight, down_bias)))
    enc_params = tuple((tensor[0] for tensor in stacks))
    reg_params = tuple((tensor[1] for tensor in stacks))
    token = mask_token.astype(jnp.float32)
    images, npatch, model_width = patches.shape
    visible_count = npatch // 2
    groups = images // IMG_DEV

    def one_group(totals, group_index):
        first_row = (group_index * IMG_DEV).astype(jnp.int32)
        patch_rows = lax.dynamic_slice_in_dim(patches, first_row, IMG_DEV, 0).astype(jnp.float32)
        group_order = lax.dynamic_slice_in_dim(order, first_row, IMG_DEV, 0)
        visible = group_order[:, :visible_count]
        masked = group_order[:, visible_count:]
        output_grads = lax.dynamic_slice_in_dim(cotangent, first_row, IMG_DEV, 1).astype(jnp.float32)
        zero_shift = jnp.zeros((IMG_DEV, visible_count, model_width), jnp.float32)
        forward = functools.partial(forward_group, visible=visible, masked=masked)
        (latent, predicted), pullback = jax.vjp(forward, enc_params, reg_params, patch_rows, token, zero_shift, zero_shift)
        enc_grads, reg_grads, rows_grad, token_grad, context_grad, query_grad = pullback((output_grads[0], output_grads[1]))
        masked_rows = jnp.take_along_axis(patch_rows, masked[..., None], 1)
        targets = low(vit_block(masked_rows, masked_rows[:, :0], enc_params))
        totals = jax.tree.map(jnp.add, totals, (enc_grads, reg_grads, token_grad))
        return (totals, (latent, targets, predicted, rows_grad, jnp.concatenate([context_grad, query_grad], 1)))
    zero_totals = jax.tree.map(jnp.zeros_like, (enc_params, reg_params, token))
    totals, stacked = lax.scan(one_group, zero_totals, jnp.arange(groups, dtype=jnp.int32))
    latent, targets, predicted, rows_grad, regressor_rows = stacked

    def flatten(tensor):
        return tensor.reshape((images,) + tensor.shape[2:])
    enc_grads, reg_grads, token_grad = totals
    grads = tuple((jnp.stack([enc_value, reg_value]) for enc_value, reg_value in zip(enc_grads, reg_grads)))
    latents = flatten(latent).astype(jnp.bfloat16)
    features = jnp.stack([flatten(targets), flatten(predicted)]).astype(jnp.bfloat16)
    input_grads = jnp.stack([flatten(rows_grad), flatten(regressor_rows)])
    return (latents, features, input_grads, grads[0], grads[1], grads[2], grads[3], grads[4], grads[5], grads[6], grads[7], grads[8], token_grad)
```

```python
import functools
import math

import jax
import jax.numpy as jnp
from jax import lax
from jax.experimental import pallas as pl
from jax.experimental.pallas import tpu as pltpu
from jax.sharding import PartitionSpec as P

HEADS = 12
EPSILON = 1e-06
BF = jnp.bfloat16
F32 = jnp.float32
ROWS_AT_ONCE = 64
NN = ((1,), (0,))
NT = ((1,), (1,))
TN = ((0,), (0,))
SWAP = ((0, 1), (1, 0))
VMEM_BYTES = 60 * 1024 * 1024


def dot(left, right, dims=NN):
    return lax.dot_general(left, right, (dims, ((), ())), preferred_element_type=F32)


def row_loop(rows, body):
    def step(index, carry):
        body(pl.ds(pl.multiple_of(index * ROWS_AT_ONCE, ROWS_AT_ONCE), ROWS_AT_ONCE))
        return carry

    lax.fori_loop(0, rows // ROWS_AT_ONCE, step, 0)


def standardize(values):
    centred = values - jnp.mean(values, -1, keepdims=True)
    inv_std = lax.rsqrt(jnp.mean(centred * centred, -1, keepdims=True) + EPSILON)
    return centred * inv_std, inv_std


def norm_into(source, target, gain, bias):
    def body(rows):
        scaled, _ = standardize(source[rows, :])
        target[rows, :] = (scaled * gain + bias).astype(BF)

    row_loop(source.shape[0], body)


def fold_rows(values):
    return jnp.sum(values.reshape(-1, 8, values.shape[-1]), 0)


def norm_back(grad, scaled, inv_std, gain):
    scaled_grad = grad * gain
    return inv_std * (
        scaled_grad
        - jnp.mean(scaled_grad, -1, keepdims=True)
        - scaled * jnp.mean(scaled_grad * scaled, -1, keepdims=True)
    )


class Weights:
    NAMES = ("qkv", "out", "up", "down")

    def __init__(self, sources, buffers, sems, names=NAMES):
        self.buffers = dict(zip(self.NAMES, buffers))
        self.copies = {}
        for at, name in enumerate(self.NAMES):
            if name not in names:
                continue
            for half in range(2):
                self.copies[name, half] = pltpu.make_async_copy(
                    sources[2 * at + half], self.buffers[name].at[half], sems.at[at, half]
                )

    def start(self, order):
        for name in order:
            for half in range(2):
                self.copies[name, half].start()

    def wait(self, name):
        for half in range(2):
            self.copies[name, half].wait()

    def __getitem__(self, name):
        return self.buffers[name]


def weight_scratch(width, local, hidden):
    return [
        pltpu.VMEM((2, 3, width, local), BF),
        pltpu.VMEM((2, local, width), BF),
        pltpu.VMEM((2, width, hidden), BF),
        pltpu.VMEM((2, hidden, width), BF),
        pltpu.SemaphoreType.DMA((4, 2)),
    ]


def head_masks():
    lanes = lax.broadcasted_iota(jnp.int32, (1, 128), 1)
    low = (lanes < 64).astype(F32)
    return low.astype(BF), (1.0 - low).astype(BF)


def forward(rows_all, ctx, vec, up_bias, weights, keep, result_fn):
    width = rows_all.shape[1]
    row_count = rows_all.shape[0] - ctx
    normed, queries, keys, values, probs, mixed = (
        keep[name] for name in ("N", "Q", "K", "V", "P", "O")
    )
    norm_into(rows_all, normed, vec[0:1, :], vec[2:3, :])
    weights.wait("qkv")
    local = weights["qkv"].shape[3]
    for half in range(2):
        cols = slice(half * local, (half + 1) * local)
        queries[:, cols] = (dot(normed[ctx:, :], weights["qkv"][half, 0]) * 0.125).astype(BF)
        keys[:, cols] = dot(normed[...], weights["qkv"][half, 1]).astype(BF)
        values[:, cols] = dot(normed[...], weights["qkv"][half, 2]).astype(BF)
    masks = head_masks()

    def attend(pair, carry):
        cols = pl.ds(pl.multiple_of(pair * 128, 128), 128)
        query, key = queries[:, cols], keys[:, cols]
        value_t = values[:, cols].T
        outs = []
        for at in range(2):
            scores = dot(key, query * masks[at], NT)
            weight = jnp.exp(scores - jnp.max(scores, 0, keepdims=True))
            prob = (weight * (1.0 / jnp.sum(weight, 0, keepdims=True))).astype(BF)
            probs[2 * pair + at] = prob
            outs.append(dot(value_t[64 * at : 64 * at + 64], prob))
        mixed[:, cols] = jnp.concatenate(outs, 0).T.astype(BF)
        return carry

    lax.fori_loop(0, HEADS // 2, attend, 0)
    weights.wait("out")
    attended = dot(mixed[:, :local], weights["out"][0]) + dot(mixed[:, local:], weights["out"][1])
    hidden, normed_two = keep["H"], keep["M"]
    keep["A"][...] = attended.astype(keep["A"].dtype)
    hidden[...] = rows_all[ctx:, :] + vec[4:5, :] * attended
    norm_into(hidden, normed_two, vec[1:2, :], vec[3:4, :])
    weights.wait("up")
    weights.wait("down")
    fed = keep["F"]
    fed[...] = jnp.broadcast_to(vec[6:7, :], fed.shape)
    step = 512
    per_half = weights["up"].shape[2] // step
    for half in range(2):

        def feed(chunk, carry):
            cols = pl.ds(pl.multiple_of(chunk * step, step), step)
            pre = dot(normed_two[...], weights["up"][half, :, cols]) + up_bias[half, :, cols]
            phi = 0.5 + 0.5 * lax.erf(pre * math.sqrt(0.5))
            act = (pre * phi).astype(BF)
            if "G" in keep:
                keep["G"][half, :, cols] = act
                density = jnp.exp(pre * pre * -0.5) * (1.0 / math.sqrt(2.0 * math.pi))
                keep["D"][half, :, cols] = (phi + pre * density).astype(BF)
            fed[...] += dot(act, weights["down"][half, cols, :])
            return carry

        lax.fori_loop(0, per_half, feed, 0)

    def finish(rows):
        result_fn(rows, hidden[rows, :] + vec[5:6, :] * fed[rows, :])

    row_loop(row_count, finish)


def backward(rows_all, ctx, out_grad_fn, vec, weights, keep, grads, work, sums, up_bias_grad):
    width = rows_all.shape[1]
    row_count = rows_all.shape[0] - ctx
    local = width // 2
    grad_in = work["dH"]
    for at in range(8):
        sums[at] = jnp.zeros((8, width), F32)

    def enter(rows):
        grad = out_grad_fn(rows)
        grad_in[rows, :] = grad
        branch = vec[5:6, :] * grad
        sums[5] += fold_rows(grad * keep["F"][rows, :].astype(F32))
        sums[6] += fold_rows(branch)
        grads["dF"][rows, :] = branch.astype(BF)

    row_loop(row_count, enter)
    weights.wait("down")
    weights.wait("up")
    grad_mid = work["dM"]
    grad_mid[...] = jnp.zeros_like(grad_mid)
    step = 512
    per_half = weights["up"].shape[2] // step
    for half in range(2):

        def feed(chunk, carry):
            cols = pl.ds(pl.multiple_of(chunk * step, step), step)
            act_grad = dot(grads["dF"][...], weights["down"][half, cols, :], NT)
            pre_grad = act_grad * keep["D"][half, :, cols].astype(F32)
            up_bias_grad[half, :, cols] = jnp.sum(pre_grad, 0, keepdims=True)
            pre_grad = pre_grad.astype(BF)
            grads["dU"][half, :, cols] = pre_grad
            grad_mid[...] += dot(pre_grad, weights["up"][half, :, cols], NT)
            return carry

        lax.fori_loop(0, per_half, feed, 0)

    def middle(rows):
        scaled, inv_std = standardize(keep["H"][rows, :])
        grad = grad_mid[rows, :]
        sums[1] += fold_rows(grad * scaled)
        sums[3] += fold_rows(grad)
        hidden_grad = grad_in[rows, :] + norm_back(grad, scaled, inv_std, vec[1:2, :])
        grad_in[rows, :] = hidden_grad
        sums[4] += fold_rows(hidden_grad * keep["A"][rows, :].astype(F32))
        grads["dA"][rows, :] = (vec[4:5, :] * hidden_grad).astype(BF)

    row_loop(row_count, middle)
    weights.wait("out")
    mix_grad = work["dO"]
    for half in range(2):
        mix_grad[:, half * local : (half + 1) * local] = dot(
            grads["dA"][...], weights["out"][half], NT
        ).astype(BF)
    masks = head_masks()

    def attend(pair, carry):
        cols = pl.ds(pl.multiple_of(pair * 128, 128), 128)
        query, key, value = keep["Q"][:, cols], keep["K"][:, cols], keep["V"][:, cols]
        out_grad = mix_grad[:, cols]
        key_t = key.T
        value_grad = key_grad = None
        query_grads = []
        for at in range(2):
            prob = keep["P"][2 * pair + at]
            own_grad = out_grad * masks[at]
            part = dot(prob, own_grad)
            value_grad = part if value_grad is None else value_grad + part
            prob_grad = dot(value, own_grad, NT)
            wide = prob.astype(F32)
            product = wide * prob_grad
            score_grad = (product - wide * jnp.sum(product, 0, keepdims=True)).astype(BF)
            part = dot(score_grad, query * masks[at])
            key_grad = part if key_grad is None else key_grad + part
            query_grads.append(dot(key_t[64 * at : 64 * at + 64], score_grad))
        grads["dV"][:, cols] = value_grad.astype(BF)
        grads["dK"][:, cols] = key_grad.astype(BF)
        grads["dQ"][:, cols] = (jnp.concatenate(query_grads, 0).T * 0.125).astype(BF)
        return carry

    lax.fori_loop(0, HEADS // 2, attend, 0)
    weights.wait("qkv")
    grad_all = work["dN"]
    qkv = weights["qkv"]
    for half in range(2):
        cols = slice(half * local, (half + 1) * local)
        part = dot(grads["dK"][:, cols], qkv[half, 1], NT) + dot(
            grads["dV"][:, cols], qkv[half, 2], NT
        )
        if half == 0:
            grad_all[...] = part
        else:
            grad_all[...] += part
        grad_all[ctx:, :] += dot(grads["dQ"][:, cols], qkv[half, 0], NT)

    def leave(rows):
        scaled, inv_std = standardize(rows_all[rows, :])
        grad = grad_all[rows, :]
        sums[0] += fold_rows(grad * scaled)
        sums[2] += fold_rows(grad)
        grad_all[rows, :] = norm_back(grad, scaled, inv_std, vec[0:1, :])

    row_loop(rows_all.shape[0], leave)


def write_sums(sums, target):
    for at in range(8):
        target[at : at + 1, :] = jnp.sum(sums[at], 0, keepdims=True)


def pick_rows(order_column, patches):
    places = lax.broadcasted_iota(jnp.int32, (order_column.shape[0], patches.shape[0]), 1)
    return dot((places == order_column).astype(F32).astype(BF), patches)


KEPT = ("X", "N", "Q", "K", "V", "P", "O", "A", "H", "M", "G", "D", "F")
GRADS = ("dF", "dU", "dA", "dQ", "dK", "dV")
OPERANDS = ("dF", "G", "dU", "M", "dA", "O", "dQ", "dK", "dV", "N")


def kept_shapes(rows, keys, width, hidden):
    return {
        "X": ((rows, width), BF),
        "N": ((keys, width), BF),
        "Q": ((rows, width), BF),
        "K": ((keys, width), BF),
        "V": ((keys, width), BF),
        "P": ((HEADS, keys, rows), BF),
        "O": ((rows, width), BF),
        "A": ((rows, width), BF),
        "H": ((rows, width), F32),
        "M": ((rows, width), BF),
        "G": ((2, rows, hidden), BF),
        "D": ((2, rows, hidden), BF),
        "F": ((rows, width), F32),
    }


def grad_shapes(rows, keys, width, hidden):
    return {
        "dF": ((rows, width), BF),
        "dU": ((2, rows, hidden), BF),
        "dA": ((rows, width), BF),
        "dQ": ((rows, width), BF),
        "dK": ((keys, width), BF),
        "dV": ((keys, width), BF),
    }


def vmem(shape_type):
    return pltpu.VMEM(*shape_type)


ONCE = pl.Buffered(1)


def whole(shape):
    return pl.BlockSpec(tuple(shape), lambda _: (0,) * len(shape), pipeline_mode=ONCE)


def image_of(array, image):
    return pl.BlockSpec(
        (None,) + array.shape[1:],
        lambda _: (image,) + (0,) * (array.ndim - 1),
        pipeline_mode=ONCE,
    )


ANY = pl.BlockSpec(memory_space=pl.ANY)


def shape_of(shape_type):
    return jax.ShapeDtypeStruct(*shape_type)


def nothing(shapes):
    return pl.pallas_call(
        lambda *refs: None,
        out_shape=[shape_of(s) for s in shapes],
        out_specs=[ANY] * len(shapes),
        name="no_values",
    )()


def params_of(**extra):
    return pltpu.CompilerParams(vmem_limit_bytes=VMEM_BYTES, **extra)


def block_cost(rows, keys, width, hidden, passes):
    flops = 2 * rows * width * (2 * width + 4 * hidden) + 4 * keys * width * width
    flops += 4 * rows * keys * width
    return pl.CostEstimate(flops=passes * flops, bytes_accessed=24_000_000, transcendentals=0)


def encoder_forward(image, which, patches, order_column, vec, up_bias, matrices, save):
    _, places, width = patches.shape
    rows = places // 2
    hidden = matrices[4].shape[1]
    local = width // 2
    shapes = kept_shapes(rows, rows, width, hidden)
    names = [n for n in KEPT]

    def kernel(patch_ref, order_ref, vec_ref, bias_ref, *refs):
        sources, refs = refs[:8], refs[8:]
        result, refs = refs[0], refs[1:]
        if save:
            keep = dict(zip(names, refs[: len(names)]))
            refs = refs[len(names) :]
        else:
            own = [n for n in names if n not in ("X", "G", "D")]
            keep = dict(zip(own, refs[: len(own)]))
            refs = refs[len(own) :]
        rows_ref, refs = refs[0], refs[1:]
        weights = Weights(sources, refs[:4], refs[4])
        weights.start(("qkv", "out", "up", "down"))
        rows_ref[...] = pick_rows(order_ref[...], patch_ref[...])
        if save:
            keep["X"][...] = rows_ref[...].astype(BF)

        def result_fn(rows_at, value):
            result[rows_at, :] = value.astype(BF)

        forward(rows_ref, 0, vec_ref, bias_ref, weights, keep, result_fn)

    out_shapes = [((rows, width), BF)] + ([shapes[n] for n in names] if save else [])
    scratch = [] if save else [vmem(shapes[n]) for n in names if n not in ("X", "G", "D")]
    scratch = scratch + [pltpu.VMEM((rows, width), F32)] + weight_scratch(width, local, hidden)
    order_spec = pl.BlockSpec(
        (None, rows, 1), lambda _: (image, which, 0), pipeline_mode=ONCE
    )
    return pl.pallas_call(
        kernel,
        grid=(1,),
        out_shape=[shape_of(s) for s in out_shapes],
        in_specs=[image_of(patches, image), order_spec, whole(vec.shape), whole(up_bias.shape)]
        + [ANY] * 8,
        out_specs=[whole(s[0]) for s in out_shapes],
        scratch_shapes=scratch,
        compiler_params=params_of(),
        cost_estimate=block_cost(rows, rows, width, hidden, 1),
        name="encoder_forward" if save else "encoder_targets",
    )(patches, order_column, vec, up_bias, *matrices)


def encoder_backward(image, latent_grad, cotangent, order_row, kept, vec, matrices):
    rows, width = latent_grad.shape
    hidden = matrices[4].shape[1]
    local = width // 2
    shapes = grad_shapes(rows, rows, width, hidden)
    names = list(GRADS)

    def kernel(back_ref, cot_ref, order_ref, vec_ref, *refs):
        sources, refs = refs[:8], refs[8:]
        keep = dict(zip(KEPT, refs[: len(KEPT)]))
        refs = refs[len(KEPT) :]
        input_grad, vec_grad, bias_grad, refs = refs[0], refs[1], refs[2], refs[3:]
        grads = dict(zip(names, refs[: len(names)]))
        refs = refs[len(names) :]
        rows_ref, d_hidden, d_mid, d_out, d_norm, sums = refs[:6]
        weights = Weights(sources, refs[6:10], refs[10])
        weights.start(("down", "up", "out", "qkv"))
        work = {"dH": d_hidden, "dM": d_mid, "dO": d_out, "dN": d_norm}
        rows_ref[...] = keep["X"][...].astype(F32)

        def out_grad_fn(rows_at):
            return cot_ref[rows_at, :].astype(F32) + back_ref[rows_at, :].astype(F32)

        backward(rows_ref, 0, out_grad_fn, vec_ref, weights, keep, grads, work, sums, bias_grad)
        write_sums(sums, vec_grad)

        def join(rows_at):
            total = d_norm[rows_at, :] + d_hidden[rows_at, :]
            high = total.astype(BF)
            d_out[rows_at, :] = high
            grads_low[rows_at, :] = (total - high.astype(F32)).astype(BF)

        grads_low = refs[11]
        row_loop(rows, join)

        def place(index, carry):
            first = pl.multiple_of(index * 128, 128)
            places = lax.broadcasted_iota(jnp.int32, (128, rows), 0) + first
            hot = (places == order_ref[...]).astype(F32).astype(BF)
            input_grad[pl.ds(first, 128), :] = dot(hot, d_out[...]) + dot(hot, grads_low[...])
            return carry

        lax.fori_loop(0, input_grad.shape[0] // 128, place, 0)

    out_shapes = [((2 * rows, width), F32), ((8, width), F32), ((2, 1, hidden), F32)]
    out_shapes += [shapes[n] for n in names]
    scratch = [
        pltpu.VMEM((rows, width), F32),
        pltpu.VMEM((rows, width), F32),
        pltpu.VMEM((rows, width), F32),
        pltpu.VMEM((rows, width), BF),
        pltpu.VMEM((rows, width), F32),
        pltpu.VMEM((8, 8, width), F32),
    ]
    scratch += weight_scratch(width, local, hidden) + [pltpu.VMEM((rows, width), BF)]
    order_spec = pl.BlockSpec((None, 1, rows), lambda _: (image, 0, 0), pipeline_mode=ONCE)
    outs = pl.pallas_call(
        kernel,
        grid=(1,),
        out_shape=[shape_of(s) for s in out_shapes],
        in_specs=[whole(latent_grad.shape), image_of(cotangent, image), order_spec, whole(vec.shape)]
        + [ANY] * 8
        + [whole(k.shape) for k in kept],
        out_specs=[whole(s[0]) for s in out_shapes],
        scratch_shapes=scratch,
        compiler_params=params_of(),
        cost_estimate=block_cost(rows, rows, width, hidden, 1),
        name="encoder_backward",
    )(latent_grad, cotangent, order_row, vec, *matrices, *kept)
    grads = dict(zip(names, outs[3:]))
    grads.update(dict(zip(KEPT, kept)))
    return outs[0], outs[1], outs[2], [grads[n] for n in OPERANDS]


def operand_shapes(rows, keys, width, hidden):
    shapes = dict(grad_shapes(rows, keys, width, hidden))
    shapes.update(kept_shapes(rows, keys, width, hidden))
    return [shapes[n] for n in OPERANDS]


def regressor_block(image, latent, codes, token, cotangent, vec, up_bias, matrices):
    ctx, width = latent.shape
    rows = codes.shape[1] - ctx
    keys = rows + ctx
    hidden = matrices[4].shape[1]
    local = width // 2
    kept = kept_shapes(rows, keys, width, hidden)
    shapes = grad_shapes(rows, keys, width, hidden)
    own = [n for n in KEPT if n != "X" and n not in OPERANDS]

    def kernel(latent_ref, code_ref, token_ref, cot_ref, vec_ref, bias_ref, *refs):
        sources, refs = refs[:8], refs[8:]
        result, back, input_grad, vec_grad, bias_grad = refs[:5]
        refs = refs[5:]
        named = dict(zip(OPERANDS, refs[: len(OPERANDS)]))
        refs = refs[len(OPERANDS) :]
        keep = dict(named)
        keep.update(zip(own, refs[: len(own)]))
        refs = refs[len(own) :]
        rows_ref, d_hidden, d_mid, d_out, sums = refs[:5]
        weights = Weights(sources, refs[5:9], refs[9])
        weights.start(("qkv", "out", "up", "down"))

        def fill(rows_at):
            rows_ref[rows_at, :] = latent_ref[rows_at, :].astype(F32) + code_ref[rows_at, :]
            lower = pl.ds(rows_at.start + ctx, ROWS_AT_ONCE)
            rows_ref[lower, :] = token_ref[...] + code_ref[lower, :]

        row_loop(ctx, fill)

        def result_fn(rows_at, value):
            result[rows_at, :] = value.astype(BF)

        forward(rows_ref, ctx, vec_ref, bias_ref, weights, keep, result_fn)
        work = {"dH": d_hidden, "dM": d_mid, "dO": d_out, "dN": input_grad}

        def out_grad_fn(rows_at):
            return cot_ref[rows_at, :].astype(F32)

        weights.wait = lambda name: None
        backward(
            rows_ref, ctx, out_grad_fn, vec_ref, weights, keep, named, work, sums, bias_grad
        )

        def leave(rows_at):
            back[rows_at, :] = input_grad[rows_at, :].astype(BF)
            lower = pl.ds(rows_at.start + ctx, ROWS_AT_ONCE)
            total = input_grad[lower, :] + d_hidden[rows_at, :]
            input_grad[lower, :] = total
            sums[7] += fold_rows(total)

        row_loop(rows, leave)
        write_sums(sums, vec_grad)

    out_shapes = [
        ((rows, width), BF),
        ((ctx, width), BF),
        ((keys, width), F32),
        ((8, width), F32),
        ((2, 1, hidden), F32),
    ] + operand_shapes(rows, keys, width, hidden)
    scratch = [vmem(kept[n]) for n in own]
    scratch += [
        pltpu.VMEM((keys, width), F32),
        pltpu.VMEM((rows, width), F32),
        pltpu.VMEM((rows, width), F32),
        pltpu.VMEM((rows, width), BF),
        pltpu.VMEM((8, 8, width), F32),
    ]
    scratch += weight_scratch(width, local, hidden)
    outs = pl.pallas_call(
        kernel,
        grid=(1,),
        out_shape=[shape_of(s) for s in out_shapes],
        in_specs=[
            whole(latent.shape),
            image_of(codes, image),
            whole(token.shape),
            image_of(cotangent, image),
            whole(vec.shape),
            whole(up_bias.shape),
        ]
        + [ANY] * 8,
        out_specs=[whole(s[0]) for s in out_shapes],
        scratch_shapes=scratch,
        compiler_params=params_of(),
        cost_estimate=block_cost(rows, keys, width, hidden, 2),
        name="regressor_block",
    )(latent, codes, token, cotangent, vec, up_bias, *matrices)
    return outs


def weight_grad(name, lefts, rights, first_rows, split_left, step, halves):
    images = len(lefts)
    wide = (lefts if split_left else rights)[0]
    other = (rights if split_left else lefts)[0]
    if wide.ndim == 3:
        blocks = (wide.shape[0], wide.shape[2] // step)
        wide_spec = pl.BlockSpec((None, wide.shape[1], step), lambda h, c: (h, 0, c))
        width = wide.shape[2]
    else:
        blocks = (halves, wide.shape[1] // halves // step)
        wide_spec = pl.BlockSpec(
            (wide.shape[0], step), lambda h, c: (0, h * blocks[1] + c)
        )
        width = wide.shape[1] // halves
    other_spec = pl.BlockSpec(other.shape, lambda h, c: (0, 0))
    if split_left:
        out = ((halves, width, other.shape[1]), BF)
        out_spec = pl.BlockSpec((None, step, other.shape[1]), lambda h, c: (h, c, 0))
    else:
        out = ((halves, other.shape[1], width), BF)
        out_spec = pl.BlockSpec((None, other.shape[1], step), lambda h, c: (h, 0, c))

    def kernel(*refs):
        total = None
        for at in range(images):
            left, right = refs[at][...], refs[images + at][...]
            if first_rows:
                left = left[first_rows:]
            part = dot(left, right, TN)
            total = part if total is None else total + part
        refs[-1][...] = total.astype(BF)

    specs = ([wide_spec] * images + [other_spec] * images) if split_left else (
        [other_spec] * images + [wide_spec] * images
    )
    rows = rights[0].shape[-2]
    return pl.pallas_call(
        kernel,
        grid=blocks,
        out_shape=shape_of(out),
        in_specs=specs,
        out_specs=out_spec,
        compiler_params=params_of(),
        cost_estimate=pl.CostEstimate(
            flops=2 * images * rows * halves * width * other.shape[1],
            bytes_accessed=8_000_000,
            transcendentals=0,
        ),
        name=name,
    )(*lefts, *rights)


def matrix_grads(operands, ctx):
    named = [dict(zip(OPERANDS, one)) for one in operands]

    def column(name):
        return [one[name] for one in named]

    down = weight_grad("down_grad", column("G"), column("dF"), 0, True, 512, 2)
    up = weight_grad("up_grad", column("M"), column("dU"), 0, False, 512, 2)
    out = weight_grad("out_grad", column("O"), column("dA"), 0, True, 384, 2)
    query = weight_grad("query_grad", column("N"), column("dQ"), ctx, False, 384, 2)
    key = weight_grad("key_grad", column("N"), column("dK"), 0, False, 384, 2)
    value = weight_grad("value_grad", column("N"), column("dV"), 0, False, 384, 2)
    return down, up, out, query, key, value


def place_code(positions, model_width):
    half_width = model_width // 2
    frequency = jnp.exp(
        jnp.arange(half_width, dtype=F32) * (-math.log(10000.0) / half_width)
    )
    angles = positions.astype(F32)[..., None] * frequency
    return jnp.concatenate([jnp.sin(angles), jnp.cos(angles)], -1)


def shards(
    patches,
    order,
    cotangent,
    norm_gains,
    norm_biases,
    layer_scales,
    qkv_weight,
    out_weight,
    up_weight,
    up_bias,
    down_weight,
    down_bias,
    mask_token,
):
    images, places, width = patches.shape
    rows = places // 2
    hidden = up_weight.shape[2]
    local = width // 2
    encoder = lax.axis_index("stream") == 0

    def swapped(value):
        return lax.ppermute(value, "head", SWAP)

    own = (qkv_weight[0], out_weight[0], up_weight[0], down_weight[0])
    matrices = []
    for value in own:
        matrices += [value, swapped(value)]
    bias_pair = jnp.stack([up_bias[0], swapped(up_bias[0])]).astype(F32)[:, None, :]
    vec = jnp.concatenate(
        [
            norm_gains[0],
            norm_biases[0],
            layer_scales[0],
            down_bias[0][None],
            jnp.zeros((1, width), F32),
        ]
    )
    token = mask_token[None]
    cotangent = cotangent[0]
    order_column = order[:, :, None]
    order_row = order[:, None, :]

    kept_list = list(kept_shapes(rows, rows, width, hidden).values())
    row_shape = ((rows, width), BF)
    code_shape = ((images, places, width), F32)
    operand_list = [
        operand_shapes(rows, rows, width, hidden),
        operand_shapes(rows, places, width, hidden),
    ]

    kept, latents = [], []
    codes = None
    for image in range(images):

        def run_encoder():
            outs = encoder_forward(
                image, 0, patches, order_column, vec, up_bias=bias_pair, matrices=matrices, save=True
            )
            return tuple(outs) + ((nothing([code_shape])[0],) if image == 0 else ())

        def run_other():
            outs = nothing([row_shape] + kept_list)
            return tuple(outs) + ((place_code(order, width),) if image == 0 else ())

        outs = lax.cond(encoder, run_encoder, run_other)
        if image == 0:
            codes = outs[-1]
            outs = outs[:-1]
        latents.append(outs[0])
        kept.append(outs[1:])
    arrived = [lax.ppermute(one, "stream", [(0, 1)]) for one in latents]

    features, returned, reg_inputs, reg_vecs, reg_biases, reg_operands = [], [], [], [], [], []
    for image in range(images):

        def run_targets():
            (target,) = encoder_forward(
                image, 1, patches, order_column, vec, bias_pair, matrices, save=False
            )
            rest = nothing(
                [row_shape, ((places, width), F32), ((8, width), F32), ((2, 1, hidden), F32)]
                + operand_list[1]
            )
            return (target,) + tuple(rest)

        def run_regressor():
            return tuple(
                regressor_block(
                    image, arrived[image], codes, token, cotangent, vec, bias_pair, matrices
                )
            )

        outs = lax.cond(encoder, run_targets, run_regressor)
        features.append(outs[0])
        returned.append(lax.ppermute(outs[1], "stream", [(1, 0)]))
        reg_inputs.append(outs[2])
        reg_vecs.append(outs[3])
        reg_biases.append(outs[4])
        reg_operands.append(outs[5:])

    input_grads, vec_grads, bias_grads, enc_operands = [], [], [], []
    for image in range(images):

        def run_backward():
            got = encoder_backward(
                image, returned[image], cotangent, order_row[:, :, :rows], kept[image], vec, matrices
            )
            return (got[0], got[1], got[2]) + tuple(got[3])

        def run_pass():
            return (reg_inputs[image], reg_vecs[image], reg_biases[image]) + tuple(
                nothing(operand_list[0])
            )

        outs = lax.cond(encoder, run_backward, run_pass)
        input_grads.append(outs[0])
        vec_grads.append(outs[1])
        bias_grads.append(outs[2])
        enc_operands.append(outs[3:])

    parts = lax.cond(
        encoder,
        lambda: matrix_grads(enc_operands, 0),
        lambda: matrix_grads(reg_operands, rows),
    )
    vec_grad = sum(vec_grads)
    bias_grad = sum(bias_grads)[:, 0]

    def reduced(value, dim):
        mine = value[0].astype(F32) + swapped(value[1]).astype(F32)
        part = lax.psum_scatter(mine.astype(BF), "dp", scatter_dimension=dim, tiled=True)
        return lax.all_gather(part, "dp", axis=dim, tiled=True).astype(F32)

    down, up, out, query, key, value = (reduced(one, 0) for one in parts)
    bias_own = bias_grad[0] + swapped(bias_grad[1])
    bias_total = lax.psum(bias_own, "dp")
    totals = lax.psum(vec_grad, ("dp", "head"))
    token_grad = lax.psum(jnp.where(encoder, 0.0, totals[7]), "stream")

    latent_out = jnp.where(encoder, jnp.stack(latents), jnp.stack(arrived))
    return (
        latent_out,
        jnp.stack(features)[None],
        jnp.stack(input_grads)[None],
        totals[0:2][None],
        totals[2:4][None],
        totals[4:6][None],
        jnp.stack([query, key, value])[None],
        out[None],
        up[None],
        bias_total[None],
        down[None],
        totals[6][None],
        token_grad,
    )


def solution(mesh):
    in_specs = (
        P(("dp", "head"), None, None),
        P(("dp", "head"), None),
        P("stream", ("dp", "head"), None, None),
        P("stream", None, None),
        P("stream", None, None),
        P("stream", None, None),
        P("stream", None, None, "head"),
        P("stream", "head", None),
        P("stream", None, "head"),
        P("stream", "head"),
        P("stream", "head", None),
        P("stream", None),
        P(),
    )
    out_specs = (
        P(("dp", "head"), None, None),
        P("stream", ("dp", "head"), None, None),
        P("stream", ("dp", "head"), None, None),
        P("stream", None, None),
        P("stream", None, None),
        P("stream", None, None),
        P("stream", None, None, "head"),
        P("stream", "head", None),
        P("stream", None, "head"),
        P("stream", "head"),
        P("stream", "head", None),
        P("stream", None),
        P(),
    )
    return jax.shard_map(shards, mesh=mesh, in_specs=in_specs, out_specs=out_specs, check_vma=False)
```

```python
import functools
import math

import jax
import jax.numpy as jnp
from jax import lax
from jax.experimental import pallas as pl
from jax.experimental.pallas import tpu as pltpu
from jax.sharding import PartitionSpec as P

HEADS = 12
EPSILON = 1e-06
BF = jnp.bfloat16
F32 = jnp.float32
ROWS_AT_ONCE = 64
NN = ((1,), (0,))
NT = ((1,), (1,))
TN = ((0,), (0,))
SWAP = ((0, 1), (1, 0))
VMEM_BYTES = 60 * 1024 * 1024


def dot(left, right, dims=NN):
    return lax.dot_general(left, right, (dims, ((), ())), preferred_element_type=F32)


def row_loop(rows, body):
    def step(index, carry):
        body(pl.ds(pl.multiple_of(index * ROWS_AT_ONCE, ROWS_AT_ONCE), ROWS_AT_ONCE))
        return carry

    lax.fori_loop(0, rows // ROWS_AT_ONCE, step, 0)


def standardize(values):
    centred = values - jnp.mean(values, -1, keepdims=True)
    inv_std = lax.rsqrt(jnp.mean(centred * centred, -1, keepdims=True) + EPSILON)
    return centred * inv_std, inv_std


def norm_into(source, target, gain, bias):
    def body(rows):
        scaled, _ = standardize(source[rows, :])
        target[rows, :] = (scaled * gain + bias).astype(BF)

    row_loop(source.shape[0], body)


def fold_rows(values):
    return jnp.sum(values.reshape(-1, 8, values.shape[-1]), 0)


def norm_back(grad, scaled, inv_std, gain):
    scaled_grad = grad * gain
    return inv_std * (
        scaled_grad
        - jnp.mean(scaled_grad, -1, keepdims=True)
        - scaled * jnp.mean(scaled_grad * scaled, -1, keepdims=True)
    )


class Weights:
    NAMES = ("qkv", "out", "up", "down")

    def __init__(self, sources, buffers, sems, names=NAMES):
        self.buffers = dict(zip(self.NAMES, buffers))
        self.copies = {}
        for at, name in enumerate(self.NAMES):
            if name not in names:
                continue
            for half in range(2):
                self.copies[name, half] = pltpu.make_async_copy(
                    sources[2 * at + half], self.buffers[name].at[half], sems.at[at, half]
                )

    def start(self, order):
        for name in order:
            for half in range(2):
                self.copies[name, half].start()

    def wait(self, name):
        for half in range(2):
            self.copies[name, half].wait()

    def __getitem__(self, name):
        return self.buffers[name]


def weight_scratch(width, local, hidden):
    return [
        pltpu.VMEM((2, 3, width, local), BF),
        pltpu.VMEM((2, local, width), BF),
        pltpu.VMEM((2, width, hidden), BF),
        pltpu.VMEM((2, hidden, width), BF),
        pltpu.SemaphoreType.DMA((4, 2)),
    ]


def head_masks():
    lanes = lax.broadcasted_iota(jnp.int32, (1, 128), 1)
    low = (lanes < 64).astype(F32)
    return low.astype(BF), (1.0 - low).astype(BF)


def forward(rows_all, ctx, vec, up_bias, weights, keep, result_fn):
    width = rows_all.shape[1]
    row_count = rows_all.shape[0] - ctx
    normed, queries, keys, values, probs, mixed = (
        keep[name] for name in ("N", "Q", "K", "V", "P", "O")
    )
    norm_into(rows_all, normed, vec[0:1, :], vec[2:3, :])
    weights.wait("qkv")
    local = weights["qkv"].shape[3]
    for half in range(2):
        cols = slice(half * local, (half + 1) * local)
        queries[:, cols] = (dot(normed[ctx:, :], weights["qkv"][half, 0]) * 0.125).astype(BF)
        keys[:, cols] = dot(normed[...], weights["qkv"][half, 1]).astype(BF)
        values[:, cols] = dot(normed[...], weights["qkv"][half, 2]).astype(BF)
    masks = head_masks()

    def attend(pair, carry):
        cols = pl.ds(pl.multiple_of(pair * 128, 128), 128)
        query, key = queries[:, cols], keys[:, cols]
        value_t = values[:, cols].T
        outs = []
        for at in range(2):
            scores = dot(key, query * masks[at], NT)
            weight = jnp.exp(scores - jnp.max(scores, 0, keepdims=True))
            prob = (weight * (1.0 / jnp.sum(weight, 0, keepdims=True))).astype(BF)
            probs[2 * pair + at] = prob
            outs.append(dot(value_t[64 * at : 64 * at + 64], prob))
        mixed[:, cols] = jnp.concatenate(outs, 0).T.astype(BF)
        return carry

    lax.fori_loop(0, HEADS // 2, attend, 0)
    weights.wait("out")
    attended = dot(mixed[:, :local], weights["out"][0]) + dot(mixed[:, local:], weights["out"][1])
    hidden, normed_two = keep["H"], keep["M"]
    keep["A"][...] = attended.astype(keep["A"].dtype)
    hidden[...] = rows_all[ctx:, :] + vec[4:5, :] * attended
    norm_into(hidden, normed_two, vec[1:2, :], vec[3:4, :])
    weights.wait("up")
    weights.wait("down")
    fed = keep["F"]
    fed[...] = jnp.broadcast_to(vec[6:7, :], fed.shape)
    step = 512
    per_half = weights["up"].shape[2] // step
    for half in range(2):

        def feed(chunk, carry):
            cols = pl.ds(pl.multiple_of(chunk * step, step), step)
            pre = dot(normed_two[...], weights["up"][half, :, cols]) + up_bias[half, :, cols]
            phi = 0.5 + 0.5 * lax.erf(pre * math.sqrt(0.5))
            act = (pre * phi).astype(BF)
            if "G" in keep:
                keep["G"][half, :, cols] = act
                density = jnp.exp(pre * pre * -0.5) * (1.0 / math.sqrt(2.0 * math.pi))
                keep["D"][half, :, cols] = (phi + pre * density).astype(BF)
            fed[...] += dot(act, weights["down"][half, cols, :])
            return carry

        lax.fori_loop(0, per_half, feed, 0)

    def finish(rows):
        result_fn(rows, hidden[rows, :] + vec[5:6, :] * fed[rows, :])

    row_loop(row_count, finish)


def backward(rows_all, ctx, out_grad_fn, vec, weights, keep, grads, work, sums, up_bias_grad):
    width = rows_all.shape[1]
    row_count = rows_all.shape[0] - ctx
    local = width // 2
    grad_in = work["dH"]
    for at in range(8):
        sums[at] = jnp.zeros((8, width), F32)

    def enter(rows):
        grad = out_grad_fn(rows)
        grad_in[rows, :] = grad
        branch = vec[5:6, :] * grad
        sums[5] += fold_rows(grad * keep["F"][rows, :].astype(F32))
        sums[6] += fold_rows(branch)
        grads["dF"][rows, :] = branch.astype(BF)

    row_loop(row_count, enter)
    weights.wait("down")
    weights.wait("up")
    grad_mid = work["dM"]
    grad_mid[...] = jnp.zeros_like(grad_mid)
    step = 512
    per_half = weights["up"].shape[2] // step
    for half in range(2):

        def feed(chunk, carry):
            cols = pl.ds(pl.multiple_of(chunk * step, step), step)
            act_grad = dot(grads["dF"][...], weights["down"][half, cols, :], NT)
            pre_grad = act_grad * keep["D"][half, :, cols].astype(F32)
            up_bias_grad[half, :, cols] = jnp.sum(pre_grad, 0, keepdims=True)
            pre_grad = pre_grad.astype(BF)
            grads["dU"][half, :, cols] = pre_grad
            grad_mid[...] += dot(pre_grad, weights["up"][half, :, cols], NT)
            return carry

        lax.fori_loop(0, per_half, feed, 0)

    def middle(rows):
        scaled, inv_std = standardize(keep["H"][rows, :])
        grad = grad_mid[rows, :]
        sums[1] += fold_rows(grad * scaled)
        sums[3] += fold_rows(grad)
        hidden_grad = grad_in[rows, :] + norm_back(grad, scaled, inv_std, vec[1:2, :])
        grad_in[rows, :] = hidden_grad
        sums[4] += fold_rows(hidden_grad * keep["A"][rows, :].astype(F32))
        grads["dA"][rows, :] = (vec[4:5, :] * hidden_grad).astype(BF)

    row_loop(row_count, middle)
    weights.wait("out")
    mix_grad = work["dO"]
    for half in range(2):
        mix_grad[:, half * local : (half + 1) * local] = dot(
            grads["dA"][...], weights["out"][half], NT
        ).astype(BF)
    masks = head_masks()

    def attend(pair, carry):
        cols = pl.ds(pl.multiple_of(pair * 128, 128), 128)
        query, key, value = keep["Q"][:, cols], keep["K"][:, cols], keep["V"][:, cols]
        out_grad = mix_grad[:, cols]
        key_t = key.T
        value_grad = key_grad = None
        query_grads = []
        for at in range(2):
            prob = keep["P"][2 * pair + at]
            own_grad = out_grad * masks[at]
            part = dot(prob, own_grad)
            value_grad = part if value_grad is None else value_grad + part
            prob_grad = dot(value, own_grad, NT)
            wide = prob.astype(F32)
            product = wide * prob_grad
            score_grad = (product - wide * jnp.sum(product, 0, keepdims=True)).astype(BF)
            part = dot(score_grad, query * masks[at])
            key_grad = part if key_grad is None else key_grad + part
            query_grads.append(dot(key_t[64 * at : 64 * at + 64], score_grad))
        grads["dV"][:, cols] = value_grad.astype(BF)
        grads["dK"][:, cols] = key_grad.astype(BF)
        grads["dQ"][:, cols] = (jnp.concatenate(query_grads, 0).T * 0.125).astype(BF)
        return carry

    lax.fori_loop(0, HEADS // 2, attend, 0)
    weights.wait("qkv")
    grad_all = work["dN"]
    qkv = weights["qkv"]
    for half in range(2):
        cols = slice(half * local, (half + 1) * local)
        part = dot(grads["dK"][:, cols], qkv[half, 1], NT) + dot(
            grads["dV"][:, cols], qkv[half, 2], NT
        )
        if half == 0:
            grad_all[...] = part
        else:
            grad_all[...] += part
        grad_all[ctx:, :] += dot(grads["dQ"][:, cols], qkv[half, 0], NT)

    def leave(rows):
        scaled, inv_std = standardize(rows_all[rows, :])
        grad = grad_all[rows, :]
        sums[0] += fold_rows(grad * scaled)
        sums[2] += fold_rows(grad)
        grad_all[rows, :] = norm_back(grad, scaled, inv_std, vec[0:1, :])

    row_loop(rows_all.shape[0], leave)


def write_sums(sums, target):
    for at in range(8):
        target[at : at + 1, :] = jnp.sum(sums[at], 0, keepdims=True)


def pick_rows(order_column, patches):
    places = lax.broadcasted_iota(jnp.int32, (order_column.shape[0], patches.shape[0]), 1)
    return dot((places == order_column).astype(F32).astype(BF), patches)


KEPT = ("X", "N", "Q", "K", "V", "P", "O", "A", "H", "M", "G", "D", "F")
GRADS = ("dF", "dU", "dA", "dQ", "dK", "dV")
OPERANDS = ("dF", "G", "dU", "M", "dA", "O", "dQ", "dK", "dV", "N")


def kept_shapes(rows, keys, width, hidden):
    return {
        "X": ((rows, width), BF),
        "N": ((keys, width), BF),
        "Q": ((rows, width), BF),
        "K": ((keys, width), BF),
        "V": ((keys, width), BF),
        "P": ((HEADS, keys, rows), BF),
        "O": ((rows, width), BF),
        "A": ((rows, width), BF),
        "H": ((rows, width), F32),
        "M": ((rows, width), BF),
        "G": ((2, rows, hidden), BF),
        "D": ((2, rows, hidden), BF),
        "F": ((rows, width), F32),
    }


def grad_shapes(rows, keys, width, hidden):
    return {
        "dF": ((rows, width), BF),
        "dU": ((2, rows, hidden), BF),
        "dA": ((rows, width), BF),
        "dQ": ((rows, width), BF),
        "dK": ((keys, width), BF),
        "dV": ((keys, width), BF),
    }


def vmem(shape_type):
    return pltpu.VMEM(*shape_type)


ONCE = pl.Buffered(1)


def whole(shape):
    return pl.BlockSpec(tuple(shape), lambda _: (0,) * len(shape), pipeline_mode=ONCE)


def image_of(array, image):
    return pl.BlockSpec(
        (None,) + array.shape[1:],
        lambda _: (image,) + (0,) * (array.ndim - 1),
        pipeline_mode=ONCE,
    )


ANY = pl.BlockSpec(memory_space=pl.ANY)


def shape_of(shape_type):
    return jax.ShapeDtypeStruct(*shape_type)


def nothing(shapes):
    return pl.pallas_call(
        lambda *refs: None,
        out_shape=[shape_of(s) for s in shapes],
        out_specs=[ANY] * len(shapes),
        name="no_values",
    )()


def params_of(**extra):
    return pltpu.CompilerParams(vmem_limit_bytes=VMEM_BYTES, **extra)


def block_cost(rows, keys, width, hidden, passes):
    flops = 2 * rows * width * (2 * width + 4 * hidden) + 4 * keys * width * width
    flops += 4 * rows * keys * width
    return pl.CostEstimate(flops=passes * flops, bytes_accessed=24_000_000, transcendentals=0)


def encoder_forward(image, which, patches, order_column, vec, up_bias, matrices, save):
    _, places, width = patches.shape
    rows = places // 2
    hidden = matrices[4].shape[1]
    local = width // 2
    shapes = kept_shapes(rows, rows, width, hidden)
    names = [n for n in KEPT]

    def kernel(patch_ref, order_ref, vec_ref, bias_ref, *refs):
        sources, refs = refs[:8], refs[8:]
        result, refs = refs[0], refs[1:]
        if save:
            keep = dict(zip(names, refs[: len(names)]))
            refs = refs[len(names) :]
        else:
            own = [n for n in names if n not in ("X", "G", "D")]
            keep = dict(zip(own, refs[: len(own)]))
            refs = refs[len(own) :]
        rows_ref, refs = refs[0], refs[1:]
        weights = Weights(sources, refs[:4], refs[4])
        weights.start(("qkv", "out", "up", "down"))
        rows_ref[...] = pick_rows(order_ref[...], patch_ref[...])
        if save:
            keep["X"][...] = rows_ref[...].astype(BF)

        def result_fn(rows_at, value):
            result[rows_at, :] = value.astype(BF)

        forward(rows_ref, 0, vec_ref, bias_ref, weights, keep, result_fn)

    out_shapes = [((rows, width), BF)] + ([shapes[n] for n in names] if save else [])
    scratch = [] if save else [vmem(shapes[n]) for n in names if n not in ("X", "G", "D")]
    scratch = scratch + [pltpu.VMEM((rows, width), F32)] + weight_scratch(width, local, hidden)
    order_spec = pl.BlockSpec(
        (None, rows, 1), lambda _: (image, which, 0), pipeline_mode=ONCE
    )
    return pl.pallas_call(
        kernel,
        grid=(1,),
        out_shape=[shape_of(s) for s in out_shapes],
        in_specs=[image_of(patches, image), order_spec, whole(vec.shape), whole(up_bias.shape)]
        + [ANY] * 8,
        out_specs=[whole(s[0]) for s in out_shapes],
        scratch_shapes=scratch,
        compiler_params=params_of(),
        cost_estimate=block_cost(rows, rows, width, hidden, 1),
        name="encoder_forward" if save else "encoder_targets",
    )(patches, order_column, vec, up_bias, *matrices)


def encoder_backward(image, latent_grad, cotangent, order_row, kept, vec, matrices):
    rows, width = latent_grad.shape
    hidden = matrices[4].shape[1]
    local = width // 2
    shapes = grad_shapes(rows, rows, width, hidden)
    names = list(GRADS)

    def kernel(back_ref, cot_ref, order_ref, vec_ref, *refs):
        sources, refs = refs[:8], refs[8:]
        keep = dict(zip(KEPT, refs[: len(KEPT)]))
        refs = refs[len(KEPT) :]
        input_grad, vec_grad, bias_grad, refs = refs[0], refs[1], refs[2], refs[3:]
        grads = dict(zip(names, refs[: len(names)]))
        refs = refs[len(names) :]
        rows_ref, d_hidden, d_mid, d_out, d_norm, sums = refs[:6]
        weights = Weights(sources, refs[6:10], refs[10])
        weights.start(("down", "up", "out", "qkv"))
        work = {"dH": d_hidden, "dM": d_mid, "dO": d_out, "dN": d_norm}
        rows_ref[...] = keep["X"][...].astype(F32)

        def out_grad_fn(rows_at):
            return cot_ref[rows_at, :].astype(F32) + back_ref[rows_at, :].astype(F32)

        backward(rows_ref, 0, out_grad_fn, vec_ref, weights, keep, grads, work, sums, bias_grad)
        write_sums(sums, vec_grad)

        def join(rows_at):
            total = d_norm[rows_at, :] + d_hidden[rows_at, :]
            high = total.astype(BF)
            d_out[rows_at, :] = high
            grads_low[rows_at, :] = (total - high.astype(F32)).astype(BF)

        grads_low = refs[11]
        row_loop(rows, join)

        def place(index, carry):
            first = pl.multiple_of(index * 128, 128)
            places = lax.broadcasted_iota(jnp.int32, (128, rows), 0) + first
            hot = (places == order_ref[...]).astype(F32).astype(BF)
            input_grad[pl.ds(first, 128), :] = dot(hot, d_out[...]) + dot(hot, grads_low[...])
            return carry

        lax.fori_loop(0, input_grad.shape[0] // 128, place, 0)

    out_shapes = [((2 * rows, width), F32), ((8, width), F32), ((2, 1, hidden), F32)]
    out_shapes += [shapes[n] for n in names]
    scratch = [
        pltpu.VMEM((rows, width), F32),
        pltpu.VMEM((rows, width), F32),
        pltpu.VMEM((rows, width), F32),
        pltpu.VMEM((rows, width), BF),
        pltpu.VMEM((rows, width), F32),
        pltpu.VMEM((8, 8, width), F32),
    ]
    scratch += weight_scratch(width, local, hidden) + [pltpu.VMEM((rows, width), BF)]
    order_spec = pl.BlockSpec((None, 1, rows), lambda _: (image, 0, 0), pipeline_mode=ONCE)
    outs = pl.pallas_call(
        kernel,
        grid=(1,),
        out_shape=[shape_of(s) for s in out_shapes],
        in_specs=[whole(latent_grad.shape), image_of(cotangent, image), order_spec, whole(vec.shape)]
        + [ANY] * 8
        + [whole(k.shape) for k in kept],
        out_specs=[whole(s[0]) for s in out_shapes],
        scratch_shapes=scratch,
        compiler_params=params_of(),
        cost_estimate=block_cost(rows, rows, width, hidden, 1),
        name="encoder_backward",
    )(latent_grad, cotangent, order_row, vec, *matrices, *kept)
    grads = dict(zip(names, outs[3:]))
    grads.update(dict(zip(KEPT, kept)))
    return outs[0], outs[1], outs[2], [grads[n] for n in OPERANDS]


def operand_shapes(rows, keys, width, hidden):
    shapes = dict(grad_shapes(rows, keys, width, hidden))
    shapes.update(kept_shapes(rows, keys, width, hidden))
    return [shapes[n] for n in OPERANDS]


def regressor_block(image, latent, codes, token, cotangent, vec, up_bias, matrices):
    ctx, width = latent.shape
    rows = codes.shape[1] - ctx
    keys = rows + ctx
    hidden = matrices[4].shape[1]
    local = width // 2
    kept = kept_shapes(rows, keys, width, hidden)
    shapes = grad_shapes(rows, keys, width, hidden)
    own = [n for n in KEPT if n != "X" and n not in OPERANDS]

    def kernel(latent_ref, code_ref, token_ref, cot_ref, vec_ref, bias_ref, *refs):
        sources, refs = refs[:8], refs[8:]
        result, back, input_grad, vec_grad, bias_grad = refs[:5]
        refs = refs[5:]
        named = dict(zip(OPERANDS, refs[: len(OPERANDS)]))
        refs = refs[len(OPERANDS) :]
        keep = dict(named)
        keep.update(zip(own, refs[: len(own)]))
        refs = refs[len(own) :]
        rows_ref, d_hidden, d_mid, d_out, sums = refs[:5]
        weights = Weights(sources, refs[5:9], refs[9])
        weights.start(("qkv", "out", "up", "down"))

        def fill(rows_at):
            rows_ref[rows_at, :] = latent_ref[rows_at, :].astype(F32) + code_ref[rows_at, :]
            lower = pl.ds(rows_at.start + ctx, ROWS_AT_ONCE)
            rows_ref[lower, :] = token_ref[...] + code_ref[lower, :]

        row_loop(ctx, fill)

        def result_fn(rows_at, value):
            result[rows_at, :] = value.astype(BF)

        forward(rows_ref, ctx, vec_ref, bias_ref, weights, keep, result_fn)
        work = {"dH": d_hidden, "dM": d_mid, "dO": d_out, "dN": input_grad}

        def out_grad_fn(rows_at):
            return cot_ref[rows_at, :].astype(F32)

        weights.wait = lambda name: None
        backward(
            rows_ref, ctx, out_grad_fn, vec_ref, weights, keep, named, work, sums, bias_grad
        )

        def leave(rows_at):
            back[rows_at, :] = input_grad[rows_at, :].astype(BF)
            lower = pl.ds(rows_at.start + ctx, ROWS_AT_ONCE)
            total = input_grad[lower, :] + d_hidden[rows_at, :]
            input_grad[lower, :] = total
            sums[7] += fold_rows(total)

        row_loop(rows, leave)
        write_sums(sums, vec_grad)

    out_shapes = [
        ((rows, width), BF),
        ((ctx, width), BF),
        ((keys, width), F32),
        ((8, width), F32),
        ((2, 1, hidden), F32),
    ] + operand_shapes(rows, keys, width, hidden)
    scratch = [vmem(kept[n]) for n in own]
    scratch += [
        pltpu.VMEM((keys, width), F32),
        pltpu.VMEM((rows, width), F32),
        pltpu.VMEM((rows, width), F32),
        pltpu.VMEM((rows, width), BF),
        pltpu.VMEM((8, 8, width), F32),
    ]
    scratch += weight_scratch(width, local, hidden)
    outs = pl.pallas_call(
        kernel,
        grid=(1,),
        out_shape=[shape_of(s) for s in out_shapes],
        in_specs=[
            whole(latent.shape),
            image_of(codes, image),
            whole(token.shape),
            image_of(cotangent, image),
            whole(vec.shape),
            whole(up_bias.shape),
        ]
        + [ANY] * 8,
        out_specs=[whole(s[0]) for s in out_shapes],
        scratch_shapes=scratch,
        compiler_params=params_of(),
        cost_estimate=block_cost(rows, keys, width, hidden, 2),
        name="regressor_block",
    )(latent, codes, token, cotangent, vec, up_bias, *matrices)
    return outs


def weight_grad(name, lefts, rights, first_rows, split_left, step, halves):
    images = len(lefts)
    wide = (lefts if split_left else rights)[0]
    other = (rights if split_left else lefts)[0]
    if wide.ndim == 3:
        blocks = (wide.shape[0], wide.shape[2] // step)
        wide_spec = pl.BlockSpec((None, wide.shape[1], step), lambda h, c: (h, 0, c))
        width = wide.shape[2]
    else:
        blocks = (halves, wide.shape[1] // halves // step)
        wide_spec = pl.BlockSpec(
            (wide.shape[0], step), lambda h, c: (0, h * blocks[1] + c)
        )
        width = wide.shape[1] // halves
    other_spec = pl.BlockSpec(other.shape, lambda h, c: (0, 0))
    if split_left:
        out = ((halves, width, other.shape[1]), BF)
        out_spec = pl.BlockSpec((None, step, other.shape[1]), lambda h, c: (h, c, 0))
    else:
        out = ((halves, other.shape[1], width), BF)
        out_spec = pl.BlockSpec((None, other.shape[1], step), lambda h, c: (h, 0, c))

    def kernel(*refs):
        total = None
        for at in range(images):
            left, right = refs[at][...], refs[images + at][...]
            if first_rows:
                left = left[first_rows:]
            part = dot(left, right, TN)
            total = part if total is None else total + part
        refs[-1][...] = total.astype(BF)

    specs = ([wide_spec] * images + [other_spec] * images) if split_left else (
        [other_spec] * images + [wide_spec] * images
    )
    rows = rights[0].shape[-2]
    return pl.pallas_call(
        kernel,
        grid=blocks,
        out_shape=shape_of(out),
        in_specs=specs,
        out_specs=out_spec,
        compiler_params=params_of(),
        cost_estimate=pl.CostEstimate(
            flops=2 * images * rows * halves * width * other.shape[1],
            bytes_accessed=8_000_000,
            transcendentals=0,
        ),
        name=name,
    )(*lefts, *rights)


def matrix_grads(operands, ctx):
    named = [dict(zip(OPERANDS, one)) for one in operands]

    def column(name):
        return [one[name] for one in named]

    down = weight_grad("down_grad", column("G"), column("dF"), 0, True, 512, 2)
    up = weight_grad("up_grad", column("M"), column("dU"), 0, False, 512, 2)
    out = weight_grad("out_grad", column("O"), column("dA"), 0, True, 384, 2)
    query = weight_grad("query_grad", column("N"), column("dQ"), ctx, False, 384, 2)
    key = weight_grad("key_grad", column("N"), column("dK"), 0, False, 384, 2)
    value = weight_grad("value_grad", column("N"), column("dV"), 0, False, 384, 2)
    return down, up, out, query, key, value


UNIT = 128
LAG = 2


class Exchange:
    LINE = 4
    WIDE = 10
    DEEP = 8
    UNITS = 2 * WIDE + 2 * DEEP


def unit_pieces(width, local, hidden):
    pieces = []
    for at in range(hidden // UNIT):
        pieces.append([("down", at * UNIT, 0, width, 0)])
    for block in range(hidden // width):
        for at in range(width // UNIT):
            pieces.append([("up", at * UNIT, block * width, width, 0)])
    for at in range(local // UNIT):
        pieces.append([("out", at * UNIT, 0, width, 0)])
    for at in range(width // UNIT):
        pieces.append([("key", at * UNIT, 0, local, 0), ("value", at * UNIT, 0, local, local)])
    for at in range(local // UNIT):
        pieces.append(
            [("query", at * UNIT, 0, local, 0), ("query", local + at * UNIT, 0, local, local)]
        )
    return pieces


MATRICES = ("down", "up", "out", "query", "key", "value")


def exchange_kernel(pieces, *refs):
    parts = dict(zip(MATRICES, refs[:6]))
    small_ref, result, totals_ref, other_ref = refs[6:10]
    total, own_half, from_column, from_line, from_deep, from_side, done = refs[10:17]
    small_own, small_half, small_side, small_line = refs[17:21]
    (own_sem, half_send, half_recv, x1_send, x1_recv, x2_send, x2_recv, z1_send, z1_recv) = refs[21:30]
    (z2_send, z2_recv, ax_send, ax_recv, a2_send, a2_recv, a1_send, a1_recv) = refs[30:38]
    (a4_send, a4_recv, out_sem, s_send, s_recv) = refs[38:43]
    line, wide, deep = Exchange.LINE, Exchange.WIDE, Exchange.DEEP
    dp = lax.axis_index("dp")
    place, column = dp // 2, dp % 2
    side = {"dp": place * 2 + 1 - column}
    partner = {"head": 1 - lax.axis_index("head")}
    mirror = {"stream": 1 - lax.axis_index("stream")}

    def along(direction, ahead):
        return {"dp": dp + 2 * (2 * direction - 1) * ahead}

    ranks = (line - 1 - place, place)

    def unit(buffer, at):
        return buffer.at[pl.ds(pl.multiple_of(at * UNIT, UNIT), UNIT), :]

    def remote(source, target, send, recv, device):
        return pltpu.make_async_remote_copy(
            src_ref=source,
            dst_ref=target,
            send_sem=send,
            recv_sem=recv,
            device_id=device,
            device_id_type=pl.DeviceIdType.MESH,
        )

    barrier = pltpu.get_barrier_semaphore()

    def greet(device):
        pl.semaphore_signal(barrier, inc=1, device_id=device, device_id_type=pl.DeviceIdType.MESH)

    for device in (partner, side, mirror):
        greet(device)
    for ahead in range(1, line):
        greet({"dp": ((place + ahead) % line) * 2 + column})
    pl.semaphore_wait(barrier, 2 + line)

    small_copy = pltpu.make_async_copy(small_ref, small_own, s_send.at[0])
    small_copy.start()
    small_out = remote(small_ref, small_half, s_send.at[1], s_recv.at[0], partner)
    small_out.start()

    def piece_copies(at):
        local_copies, remote_copies = [], []
        for name, row, first, cols, to in pieces[at]:
            here = (pl.ds(at * UNIT, UNIT), pl.ds(to, cols))
            there = (pl.ds(row, UNIT), pl.ds(first, cols))
            local_copies.append(
                pltpu.make_async_copy(
                    parts[name].at[(0,) + there], total.at[here], own_sem.at[at]
                )
            )
            remote_copies.append(
                remote(
                    parts[name].at[(1,) + there],
                    own_half.at[here],
                    half_send.at[at],
                    half_recv.at[at],
                    partner,
                )
            )
        return local_copies, remote_copies

    order = []
    for at in range(max(wide, deep)):
        if at < wide:
            order += [2 * at, 2 * at + 1]
        if at < deep:
            order += [2 * wide + 2 * at, 2 * wide + 2 * at + 1]
    for at in order:
        local_copies, remote_copies = piece_copies(at)
        for copy in local_copies + remote_copies:
            copy.start()

    def add(target, at, first, first_at, second, second_at):
        def body(index, carry):
            offset = index * 32
            left = first[pl.ds(pl.multiple_of(first_at * UNIT + offset, 32), 32), :]
            right = second[pl.ds(pl.multiple_of(second_at * UNIT + offset, 32), 32), :]
            target[pl.ds(pl.multiple_of(at * UNIT + offset, 32), 32), :] = (
                left.astype(F32) + right.astype(F32)
            ).astype(BF)
            return carry

        lax.fori_loop(0, UNIT // 32, body, 0)

    def prepare(at):
        pltpu.make_async_copy(unit(total, at), unit(total, at), own_sem.at[at]).wait()
        remote(
            unit(own_half, at), unit(own_half, at), half_send.at[at], half_recv.at[at], partner
        ).wait_recv()
        add(total, at, total, at, own_half, at)

    def x1(at):
        return remote(
            unit(total, 2 * at + 1 - column), unit(from_column, at), x1_send.at[at], x1_recv.at[at], side
        )

    def x2(direction, at, ahead=1):
        slot = direction * (wide // 2) + at
        return remote(
            unit(total, 4 * at + 2 * direction + column),
            unit(from_line, slot),
            x2_send.at[slot],
            x2_recv.at[slot],
            along(direction, ahead),
        )

    def z1(direction, at):
        slot = direction * deep + at
        return remote(
            unit(total, 2 * wide + 2 * at + direction),
            unit(from_deep, slot),
            z1_send.at[slot],
            z1_recv.at[slot],
            along(direction, 1),
        )

    def z2(direction, at):
        return remote(
            unit(total, 2 * wide + 2 * at + direction),
            unit(from_side, at // 2),
            z2_send.at[at // 2],
            z2_recv.at[at // 2],
            side,
        )

    def finished(at, send, recv, slot, device):
        return remote(unit(done, at), unit(done, at), send.at[slot], recv.at[slot], device)

    def ax(at, sent):
        parity = column if sent else 1 - column
        return finished(2 * at + parity, ax_send, ax_recv, at, side)

    def a2(direction, at):
        slot = direction * (wide // 2) + at
        return finished(
            4 * at + 2 * direction + column, a2_send, a2_recv, slot, along(direction, -1)
        )

    def a1(direction, at):
        slot = direction * deep + at
        return finished(
            2 * wide + 2 * at + direction, a1_send, a1_recv, slot, along(direction, -1)
        )

    def a4(direction, at):
        return finished(2 * wide + 2 * at + direction, a4_send, a4_recv, at // 2, side)

    def put(at):
        pltpu.make_async_copy(unit(done, at), unit(result, at), out_sem.at[at]).start()

    def small_phase(step):
        @pl.when(step == 2)
        def _():
            small_copy.wait()
            small_out.wait_recv()
            small_own[0:8, :] = small_own[0:8, :] + small_half[0:8, :]
            small_own[8:16, :] = small_own[8:16, :] + small_half[16:24, :]
            small_side_copy().start()

        @pl.when(step == 4)
        def _():
            small_side_copy().wait_recv()
            small_line[place] = small_own[0:16, :] + small_side[...]
            for ahead in range(1, line):
                small_line_copy(ahead).start()

        @pl.when(step == 8)
        def _():
            for ahead in range(1, line):
                small_line_copy(ahead).wait_recv()
            summed = small_line[0]
            for at in range(1, line):
                summed = summed + small_line[at]
            totals_ref[...] = summed
            small_mirror_copy().start()

    def small_side_copy():
        return remote(small_own.at[0:16, :], small_side, s_send.at[2], s_recv.at[1], side)

    def small_line_copy(ahead):
        there = (place + ahead) % line
        return remote(
            small_line.at[place],
            small_line.at[place],
            s_send.at[2 + ahead],
            s_recv.at[1 + ahead],
            {"dp": there * 2 + column},
        )

    def small_mirror_copy():
        return remote(
            totals_ref, other_ref, s_send.at[2 + line], s_recv.at[1 + line], mirror
        )

    def step_body(step, carry):
        @pl.when(step < wide)
        def _():
            prepare(2 * step + 1 - column)
            x1(step).start()

        @pl.when(step < deep)
        def _():
            for direction in range(2):
                prepare(2 * wide + 2 * step + direction)

                @pl.when(ranks[direction] == 0)
                def _():
                    z1(direction, step).start()

        @pl.when(step < wide)
        def _():
            prepare(2 * step + column)

        at = step - LAG

        @pl.when((at >= 0) & (at < wide))
        def _():
            x1(at).wait_recv()
            add(total, 2 * at + column, total, 2 * at + column, from_column, at)
            for direction in range(2):

                @pl.when((at % 2 == direction) & (ranks[direction] == 0))
                def _():
                    x2(direction, at // 2).start()

        for direction in range(2):
            rank = ranks[direction]
            at = step - LAG * rank

            @pl.when((rank >= 1) & (at >= 0) & (at < deep))
            def _():
                where = 2 * wide + 2 * at + direction
                z1(direction, at).wait_recv()
                add(total, where, total, where, from_deep, direction * deep + at)

                @pl.when(rank < line - 1)
                def _():
                    z1(direction, at).start()

                @pl.when((rank == line - 1) & (at % 2 != column))
                def _():
                    z2(direction, at).start()

            twice = step - LAG - LAG * rank - direction

            @pl.when((rank >= 1) & (twice >= 0) & (twice < wide) & (twice % 2 == 0))
            def _():
                at = twice // 2
                where = 4 * at + 2 * direction + column
                x2(direction, at).wait_recv()
                slot = direction * (wide // 2) + at

                @pl.when(rank < line - 1)
                def _():
                    add(total, where, total, where, from_line, slot)
                    x2(direction, at).start()

                @pl.when(rank == line - 1)
                def _():
                    add(done, where, total, where, from_line, slot)
                    a2(direction, at).start()
                    ax(2 * at + direction, True).start()
                    put(where)

            at = step - LAG * line

            @pl.when((rank == line - 1) & (at >= 0) & (at < deep) & (at % 2 == column))
            def _():
                where = 2 * wide + 2 * at + direction
                z2(direction, at).wait_recv()
                add(done, where, total, where, from_side, at // 2)
                a1(direction, at).start()
                a4(direction, at).start()
                put(where)

            later = step - LAG * line - LAG

            @pl.when((rank == line - 1) & (later >= 0) & (later < deep) & (later % 2 != column))
            def _():
                a4(direction, later).wait_recv()
                a1(direction, later).start()
                put(2 * wide + 2 * later + direction)

            back = LAG * (line - 1 - rank)
            twice = step - LAG * line - back - direction

            @pl.when((rank < line - 1) & (twice >= 0) & (twice < wide) & (twice % 2 == 0))
            def _():
                at = twice // 2
                a2(direction, at).wait_recv()

                @pl.when(rank > 0)
                def _():
                    a2(direction, at).start()

                ax(2 * at + direction, True).start()
                put(4 * at + 2 * direction + column)

            for other in range(2):
                at = step - LAG * line - back - LAG * other

                @pl.when(
                    (rank < line - 1)
                    & (at >= 0)
                    & (at < deep)
                    & ((at + column) % 2 == other)
                )
                def _():
                    a1(direction, at).wait_recv()

                    @pl.when(rank > 0)
                    def _():
                        a1(direction, at).start()

                    put(2 * wide + 2 * at + direction)

            twice = step - LAG * line - back - direction - LAG

            @pl.when((twice >= 0) & (twice < wide) & (twice % 2 == 0))
            def _():
                at = twice + direction
                ax(at, False).wait_recv()
                put(2 * at + 1 - column)

        small_phase(step)
        return carry

    steps = wide - 1 + LAG * line + LAG * (line - 1) + LAG + 1
    lax.fori_loop(0, steps, step_body, 0)

    small_mirror_copy().wait()
    small_out.wait_send()
    small_side_copy().wait_send()
    for ahead in range(1, line):
        small_line_copy(ahead).wait_send()

    def drain(at, carry):
        remote(
            unit(own_half, at), unit(own_half, at), half_send.at[at], half_recv.at[at], partner
        ).wait_send()
        pltpu.make_async_copy(unit(done, at), unit(result, at), out_sem.at[at]).wait()
        return carry

    lax.fori_loop(0, Exchange.UNITS, drain, 0)

    def drain_wide(at, carry):
        x1(at).wait_send()
        ax(at, True).wait_send()
        return carry

    lax.fori_loop(0, wide, drain_wide, 0)
    for direction in range(2):
        rank = ranks[direction]

        def drain_line(at, carry):
            @pl.when(rank < line - 1)
            def _():
                x2(direction, at).wait_send()

            @pl.when(rank > 0)
            def _():
                a2(direction, at).wait_send()

            return carry

        lax.fori_loop(0, wide // 2, drain_line, 0)

        def drain_deep(at, carry):
            @pl.when(rank < line - 1)
            def _():
                z1(direction, at).wait_send()

            @pl.when(rank > 0)
            def _():
                a1(direction, at).wait_send()

            @pl.when((rank == line - 1) & (at % 2 != column))
            def _():
                z2(direction, at).wait_send()

            @pl.when((rank == line - 1) & (at % 2 == column))
            def _():
                a4(direction, at).wait_send()

            return carry

        lax.fori_loop(0, deep, drain_deep, 0)


def exchange(parts, small, width, local, hidden):
    pieces = unit_pieces(width, local, hidden)
    units, wide, deep = Exchange.UNITS, Exchange.WIDE, Exchange.DEEP
    assert len(pieces) == units

    def buffer(count):
        return pltpu.VMEM((count * UNIT, width), BF)

    def sems(*counts):
        return [pltpu.SemaphoreType.DMA((count,)) for count in counts]

    line = Exchange.LINE
    vspec = pl.BlockSpec(memory_space=pltpu.VMEM)
    return pl.pallas_call(
        functools.partial(exchange_kernel, pieces),
        out_shape=[
            jax.ShapeDtypeStruct((units * UNIT, width), BF),
            jax.ShapeDtypeStruct((16, width), F32),
            jax.ShapeDtypeStruct((16, width), F32),
        ],
        in_specs=[ANY] * 7,
        out_specs=[ANY, vspec, vspec],
        scratch_shapes=[
            buffer(units),
            buffer(units),
            buffer(wide),
            buffer(wide),
            buffer(2 * deep),
            buffer(deep // 2),
            buffer(units),
            pltpu.VMEM((24, width), F32),
            pltpu.VMEM((24, width), F32),
            pltpu.VMEM((16, width), F32),
            pltpu.VMEM((line, 16, width), F32),
        ]
        + sems(units, units, units, wide, wide, wide, wide, 2 * deep, 2 * deep)
        + sems(deep // 2, deep // 2, wide, wide, wide, wide, 2 * deep, 2 * deep)
        + sems(deep // 2, deep // 2, units, 3 + line, 2 + line),
        compiler_params=params_of(collective_id=0, has_side_effects=True),
        cost_estimate=pl.CostEstimate(flops=0, bytes_accessed=200_000_000, transcendentals=0),
        name="gradient_exchange",
    )(*[parts[name] for name in MATRICES], small)


def place_code(positions, model_width):
    half_width = model_width // 2
    frequency = jnp.exp(
        jnp.arange(half_width, dtype=F32) * (-math.log(10000.0) / half_width)
    )
    angles = positions.astype(F32)[..., None] * frequency
    return jnp.concatenate([jnp.sin(angles), jnp.cos(angles)], -1)


def shards(
    patches,
    order,
    cotangent,
    norm_gains,
    norm_biases,
    layer_scales,
    qkv_weight,
    out_weight,
    up_weight,
    up_bias,
    down_weight,
    down_bias,
    mask_token,
):
    images, places, width = patches.shape
    rows = places // 2
    hidden = up_weight.shape[2]
    local = width // 2
    encoder = lax.axis_index("stream") == 0

    def swapped(value):
        return lax.ppermute(value, "head", SWAP)

    own = (qkv_weight[0], out_weight[0], up_weight[0], down_weight[0])
    matrices = []
    for value in own:
        matrices += [value, swapped(value)]
    bias_pair = jnp.stack([up_bias[0], swapped(up_bias[0])]).astype(F32)[:, None, :]
    vec = jnp.concatenate(
        [
            norm_gains[0],
            norm_biases[0],
            layer_scales[0],
            down_bias[0][None],
            jnp.zeros((1, width), F32),
        ]
    )
    token = mask_token[None]
    cotangent = cotangent[0]
    order_column = order[:, :, None]
    order_row = order[:, None, :]

    kept_list = list(kept_shapes(rows, rows, width, hidden).values())
    row_shape = ((rows, width), BF)
    code_shape = ((images, places, width), F32)
    operand_list = [
        operand_shapes(rows, rows, width, hidden),
        operand_shapes(rows, places, width, hidden),
    ]

    kept, latents = [], []
    codes = None
    for image in range(images):

        def run_encoder():
            outs = encoder_forward(
                image, 0, patches, order_column, vec, up_bias=bias_pair, matrices=matrices, save=True
            )
            return tuple(outs) + ((nothing([code_shape])[0],) if image == 0 else ())

        def run_other():
            outs = nothing([row_shape] + kept_list)
            return tuple(outs) + ((place_code(order, width),) if image == 0 else ())

        outs = lax.cond(encoder, run_encoder, run_other)
        if image == 0:
            codes = outs[-1]
            outs = outs[:-1]
        latents.append(outs[0])
        kept.append(outs[1:])
    arrived = [lax.ppermute(one, "stream", [(0, 1)]) for one in latents]

    features, returned, reg_inputs, reg_vecs, reg_biases, reg_operands = [], [], [], [], [], []
    for image in range(images):

        def run_targets():
            (target,) = encoder_forward(
                image, 1, patches, order_column, vec, bias_pair, matrices, save=False
            )
            rest = nothing(
                [row_shape, ((places, width), F32), ((8, width), F32), ((2, 1, hidden), F32)]
                + operand_list[1]
            )
            return (target,) + tuple(rest)

        def run_regressor():
            return tuple(
                regressor_block(
                    image, arrived[image], codes, token, cotangent, vec, bias_pair, matrices
                )
            )

        outs = lax.cond(encoder, run_targets, run_regressor)
        features.append(outs[0])
        returned.append(lax.ppermute(outs[1], "stream", [(1, 0)]))
        reg_inputs.append(outs[2])
        reg_vecs.append(outs[3])
        reg_biases.append(outs[4])
        reg_operands.append(outs[5:])

    input_grads, vec_grads, bias_grads, enc_operands = [], [], [], []
    for image in range(images):

        def run_backward():
            got = encoder_backward(
                image, returned[image], cotangent, order_row[:, :, :rows], kept[image], vec, matrices
            )
            return (got[0], got[1], got[2]) + tuple(got[3])

        def run_pass():
            return (reg_inputs[image], reg_vecs[image], reg_biases[image]) + tuple(
                nothing(operand_list[0])
            )

        outs = lax.cond(encoder, run_backward, run_pass)
        input_grads.append(outs[0])
        vec_grads.append(outs[1])
        bias_grads.append(outs[2])
        enc_operands.append(outs[3:])

    parts = lax.cond(
        encoder,
        lambda: matrix_grads(enc_operands, 0),
        lambda: matrix_grads(reg_operands, rows),
    )
    vec_grad = sum(vec_grads)
    bias_grad = sum(bias_grads)[:, 0]

    if lax.axis_size("dp") == 2 * Exchange.LINE and width == 768 and hidden == 1536:
        small = jnp.concatenate(
            [
                vec_grad,
                jnp.pad(bias_grad[0].reshape(-1, width), ((0, 6), (0, 0))),
                jnp.pad(bias_grad[1].reshape(-1, width), ((0, 6), (0, 0))),
            ]
        )
        named = dict(zip(MATRICES, parts))
        summed, totals, other = exchange(named, small, width, local, hidden)
        bounds = [0, hidden, 2 * hidden, 2 * hidden + local, 2 * hidden + local + width]
        summed = summed.astype(F32)
        down = summed[: bounds[1]]
        up = jnp.concatenate(
            [summed[bounds[1] + at * width : bounds[1] + (at + 1) * width] for at in range(hidden // width)], 1
        )
        out = summed[bounds[2] : bounds[3]]
        key, value = summed[bounds[3] : bounds[4], :local], summed[bounds[3] : bounds[4], local:]
        query = jnp.concatenate([summed[bounds[4] :, :local], summed[bounds[4] :, local:]])
        bias_total = totals[8 : 8 + hidden // width].reshape(hidden)
        token_grad = jnp.where(encoder, other[7], totals[7])
    else:

        def reduced(value):
            mine = value[0].astype(F32) + swapped(value[1]).astype(F32)
            part = lax.psum_scatter(mine.astype(BF), "dp", scatter_dimension=0, tiled=True)
            return lax.all_gather(part, "dp", axis=0, tiled=True).astype(F32)

        down, up, out, query, key, value = (reduced(one) for one in parts)
        bias_total = lax.psum(bias_grad[0] + swapped(bias_grad[1]), "dp")
        totals = lax.psum(vec_grad, ("dp", "head"))
        token_grad = lax.psum(jnp.where(encoder, 0.0, totals[7]), "stream")

    latent_out = jnp.where(encoder, jnp.stack(latents), jnp.stack(arrived))
    return (
        latent_out,
        jnp.stack(features)[None],
        jnp.stack(input_grads)[None],
        totals[0:2][None],
        totals[2:4][None],
        totals[4:6][None],
        jnp.stack([query, key, value])[None],
        out[None],
        up[None],
        bias_total[None],
        down[None],
        totals[6][None],
        token_grad,
    )


def solution(mesh):
    in_specs = (
        P(("dp", "head"), None, None),
        P(("dp", "head"), None),
        P("stream", ("dp", "head"), None, None),
        P("stream", None, None),
        P("stream", None, None),
        P("stream", None, None),
        P("stream", None, None, "head"),
        P("stream", "head", None),
        P("stream", None, "head"),
        P("stream", "head"),
        P("stream", "head", None),
        P("stream", None),
        P(),
    )
    out_specs = (
        P(("dp", "head"), None, None),
        P("stream", ("dp", "head"), None, None),
        P("stream", ("dp", "head"), None, None),
        P("stream", None, None),
        P("stream", None, None),
        P("stream", None, None),
        P("stream", None, None, "head"),
        P("stream", "head", None),
        P("stream", None, "head"),
        P("stream", "head"),
        P("stream", "head", None),
        P("stream", None),
        P(),
    )
    return jax.shard_map(shards, mesh=mesh, in_specs=in_specs, out_specs=out_specs, check_vma=False)
```

```python
import functools
import math

import jax
import jax.numpy as jnp
from jax import lax
from jax.experimental import pallas as pl
from jax.experimental.pallas import tpu as pltpu
from jax.sharding import PartitionSpec as P

HEADS = 12
EPSILON = 1e-06
BF = jnp.bfloat16
F32 = jnp.float32
ROWS_AT_ONCE = 64
NN = ((1,), (0,))
NT = ((1,), (1,))
TN = ((0,), (0,))
SWAP = ((0, 1), (1, 0))
VMEM_BYTES = 60 * 1024 * 1024


def dot(left, right, dims=NN):
    return lax.dot_general(left, right, (dims, ((), ())), preferred_element_type=F32)


def row_loop(rows, body):
    def step(index, carry):
        body(pl.ds(pl.multiple_of(index * ROWS_AT_ONCE, ROWS_AT_ONCE), ROWS_AT_ONCE))
        return carry

    lax.fori_loop(0, rows // ROWS_AT_ONCE, step, 0)


def halves_loop(size, body):
    def step(half, carry):
        body(half, pl.ds(pl.multiple_of(half * size, size), size))
        return carry

    lax.fori_loop(0, 2, step, 0)


def standardize(values):
    centred = values - jnp.mean(values, -1, keepdims=True)
    inv_std = lax.rsqrt(jnp.mean(centred * centred, -1, keepdims=True) + EPSILON)
    return centred * inv_std, inv_std


def norm_into(source, target, gain, bias):
    def body(rows):
        scaled, _ = standardize(source[rows, :])
        target[rows, :] = (scaled * gain + bias).astype(BF)

    row_loop(source.shape[0], body)


def fold_rows(values):
    return jnp.sum(values.reshape(-1, 8, values.shape[-1]), 0)


def norm_back(grad, scaled, inv_std, gain):
    scaled_grad = grad * gain
    return inv_std * (
        scaled_grad
        - jnp.mean(scaled_grad, -1, keepdims=True)
        - scaled * jnp.mean(scaled_grad * scaled, -1, keepdims=True)
    )


class Weights:
    NAMES = ("qkv", "out", "up", "down")

    def __init__(self, sources, buffers, sems, names=NAMES, first_only=False):
        self.first_only = first_only
        self.buffers = dict(zip(self.NAMES, buffers))
        self.copies = {}
        for at, name in enumerate(self.NAMES):
            if name not in names:
                continue
            for half in range(2):
                self.copies[name, half] = pltpu.make_async_copy(
                    sources[2 * at + half], self.buffers[name].at[half], sems.at[at, half]
                )

    def each(self, names, method):
        def run():
            for name in names:
                for half in range(2):
                    getattr(self.copies[name, half], method)()

        if self.first_only:
            pl.when(pl.program_id(0) == 0)(run)
        else:
            run()

    def start(self, order):
        self.each(order, "start")

    def wait(self, name):
        self.each((name,), "wait")

    def __getitem__(self, name):
        return self.buffers[name]


def weight_scratch(width, local, hidden):
    return [
        pltpu.VMEM((2, 3, width, local), BF),
        pltpu.VMEM((2, local, width), BF),
        pltpu.VMEM((2, width, hidden), BF),
        pltpu.VMEM((2, hidden, width), BF),
        pltpu.SemaphoreType.DMA((4, 2)),
    ]


def head_masks():
    lanes = lax.broadcasted_iota(jnp.int32, (1, 128), 1)
    low = (lanes < 64).astype(F32)
    return low.astype(BF), (1.0 - low).astype(BF)


def forward(rows_all, ctx, vec, up_bias, weights, keep, result_fn):
    width = rows_all.shape[1]
    row_count = rows_all.shape[0] - ctx
    normed, queries, keys, values, probs, mixed = (
        keep[name] for name in ("N", "Q", "K", "V", "P", "O")
    )
    norm_into(rows_all, normed, vec[0:1, :], vec[2:3, :])
    weights.wait("qkv")
    local = weights["qkv"].shape[3]

    def project(half, cols):
        queries[:, cols] = (dot(normed[ctx:, :], weights["qkv"][half, 0]) * 0.125).astype(BF)
        keys[:, cols] = dot(normed[...], weights["qkv"][half, 1]).astype(BF)
        values[:, cols] = dot(normed[...], weights["qkv"][half, 2]).astype(BF)

    halves_loop(local, project)
    masks = head_masks()

    def attend(pair, carry):
        cols = pl.ds(pl.multiple_of(pair * 128, 128), 128)
        query, key = queries[:, cols], keys[:, cols]
        value_t = values[:, cols].T
        outs = []
        for at in range(2):
            scores = dot(key, query * masks[at], NT)
            weight = jnp.exp(scores - jnp.max(scores, 0, keepdims=True))
            prob = (weight * (1.0 / jnp.sum(weight, 0, keepdims=True))).astype(BF)
            probs[2 * pair + at] = prob
            outs.append(dot(value_t[64 * at : 64 * at + 64], prob))
        mixed[:, cols] = jnp.concatenate(outs, 0).T.astype(BF)
        return carry

    lax.fori_loop(0, HEADS // 2, attend, 0)
    weights.wait("out")
    attended = dot(mixed[:, :local], weights["out"][0]) + dot(mixed[:, local:], weights["out"][1])
    hidden, normed_two = keep["H"], keep["M"]
    keep["A"][...] = attended.astype(keep["A"].dtype)
    hidden[...] = rows_all[ctx:, :] + vec[4:5, :] * attended
    norm_into(hidden, normed_two, vec[1:2, :], vec[3:4, :])
    weights.wait("up")
    weights.wait("down")
    fed = keep["F"]
    fed[...] = jnp.broadcast_to(vec[6:7, :], fed.shape)
    step = 512
    per_half = weights["up"].shape[2] // step

    def feed(index, carry):
        half, chunk = index // per_half, index % per_half
        cols = pl.ds(pl.multiple_of(chunk * step, step), step)
        pre = dot(normed_two[...], weights["up"][half, :, cols]) + up_bias[half, :, cols]
        phi = 0.5 + 0.5 * lax.erf(pre * math.sqrt(0.5))
        act = (pre * phi).astype(BF)
        if "G" in keep:
            keep["G"][half, :, cols] = act
            density = jnp.exp(pre * pre * -0.5) * (1.0 / math.sqrt(2.0 * math.pi))
            keep["D"][half, :, cols] = (phi + pre * density).astype(BF)
        fed[...] += dot(act, weights["down"][half, cols, :])
        return carry

    lax.fori_loop(0, 2 * per_half, feed, 0)

    def finish(rows):
        result_fn(rows, hidden[rows, :] + vec[5:6, :] * fed[rows, :])

    row_loop(row_count, finish)


def backward(rows_all, ctx, out_grad_fn, vec, weights, keep, grads, work, sums, up_bias_grad):
    width = rows_all.shape[1]
    row_count = rows_all.shape[0] - ctx
    local = width // 2
    grad_in = work["dH"]
    for at in range(8):
        sums[at] = jnp.zeros((8, width), F32)

    def enter(rows):
        grad = out_grad_fn(rows)
        grad_in[rows, :] = grad
        branch = vec[5:6, :] * grad
        sums[5] += fold_rows(grad * keep["F"][rows, :].astype(F32))
        sums[6] += fold_rows(branch)
        grads["dF"][rows, :] = branch.astype(BF)

    row_loop(row_count, enter)
    weights.wait("down")
    weights.wait("up")
    grad_mid = work["dM"]
    grad_mid[...] = jnp.zeros_like(grad_mid)
    step = 512
    per_half = weights["up"].shape[2] // step

    def feed(index, carry):
        half, chunk = index // per_half, index % per_half
        cols = pl.ds(pl.multiple_of(chunk * step, step), step)
        act_grad = dot(grads["dF"][...], weights["down"][half, cols, :], NT)
        pre_grad = act_grad * keep["D"][half, :, cols].astype(F32)
        up_bias_grad[half, :, cols] = jnp.sum(pre_grad, 0, keepdims=True)
        pre_grad = pre_grad.astype(BF)
        grads["dU"][half, :, cols] = pre_grad
        grad_mid[...] += dot(pre_grad, weights["up"][half, :, cols], NT)
        return carry

    lax.fori_loop(0, 2 * per_half, feed, 0)

    def middle(rows):
        scaled, inv_std = standardize(keep["H"][rows, :])
        grad = grad_mid[rows, :]
        sums[1] += fold_rows(grad * scaled)
        sums[3] += fold_rows(grad)
        hidden_grad = grad_in[rows, :] + norm_back(grad, scaled, inv_std, vec[1:2, :])
        grad_in[rows, :] = hidden_grad
        sums[4] += fold_rows(hidden_grad * keep["A"][rows, :].astype(F32))
        grads["dA"][rows, :] = (vec[4:5, :] * hidden_grad).astype(BF)

    row_loop(row_count, middle)
    weights.wait("out")
    mix_grad = work["dO"]

    def unmix(half, cols):
        mix_grad[:, cols] = dot(grads["dA"][...], weights["out"][half], NT).astype(BF)

    halves_loop(local, unmix)
    masks = head_masks()

    def attend(pair, carry):
        cols = pl.ds(pl.multiple_of(pair * 128, 128), 128)
        query, key, value = keep["Q"][:, cols], keep["K"][:, cols], keep["V"][:, cols]
        out_grad = mix_grad[:, cols]
        key_t = key.T
        value_grad = key_grad = None
        query_grads = []
        for at in range(2):
            prob = keep["P"][2 * pair + at]
            own_grad = out_grad * masks[at]
            part = dot(prob, own_grad)
            value_grad = part if value_grad is None else value_grad + part
            prob_grad = dot(value, own_grad, NT)
            wide = prob.astype(F32)
            product = wide * prob_grad
            score_grad = (product - wide * jnp.sum(product, 0, keepdims=True)).astype(BF)
            part = dot(score_grad, query * masks[at])
            key_grad = part if key_grad is None else key_grad + part
            query_grads.append(dot(key_t[64 * at : 64 * at + 64], score_grad))
        grads["dV"][:, cols] = value_grad.astype(BF)
        grads["dK"][:, cols] = key_grad.astype(BF)
        grads["dQ"][:, cols] = (jnp.concatenate(query_grads, 0).T * 0.125).astype(BF)
        return carry

    lax.fori_loop(0, HEADS // 2, attend, 0)
    weights.wait("qkv")
    grad_all = work["dN"]
    qkv = weights["qkv"]
    grad_all[...] = jnp.zeros_like(grad_all)

    def unproject(half, cols):
        grad_all[...] += dot(grads["dK"][:, cols], qkv[half, 1], NT) + dot(
            grads["dV"][:, cols], qkv[half, 2], NT
        )
        grad_all[ctx:, :] += dot(grads["dQ"][:, cols], qkv[half, 0], NT)

    halves_loop(local, unproject)

    def leave(rows):
        scaled, inv_std = standardize(rows_all[rows, :])
        grad = grad_all[rows, :]
        sums[0] += fold_rows(grad * scaled)
        sums[2] += fold_rows(grad)
        grad_all[rows, :] = norm_back(grad, scaled, inv_std, vec[0:1, :])

    row_loop(rows_all.shape[0], leave)


def write_sums(sums, target):
    for at in range(8):
        target[at : at + 1, :] = jnp.sum(sums[at], 0, keepdims=True)


def pick_rows(order_column, patches):
    places = lax.broadcasted_iota(jnp.int32, (order_column.shape[0], patches.shape[0]), 1)
    return dot((places == order_column).astype(F32).astype(BF), patches)


KEPT = ("X", "N", "Q", "K", "V", "P", "O", "A", "H", "M", "G", "D", "F")
GRADS = ("dF", "dU", "dA", "dQ", "dK", "dV")
OPERANDS = ("dF", "G", "dU", "M", "dA", "O", "dQ", "dK", "dV", "N")


def kept_shapes(rows, keys, width, hidden):
    return {
        "X": ((rows, width), BF),
        "N": ((keys, width), BF),
        "Q": ((rows, width), BF),
        "K": ((keys, width), BF),
        "V": ((keys, width), BF),
        "P": ((HEADS, keys, rows), BF),
        "O": ((rows, width), BF),
        "A": ((rows, width), BF),
        "H": ((rows, width), F32),
        "M": ((rows, width), BF),
        "G": ((2, rows, hidden), BF),
        "D": ((2, rows, hidden), BF),
        "F": ((rows, width), F32),
    }


def grad_shapes(rows, keys, width, hidden):
    return {
        "dF": ((rows, width), BF),
        "dU": ((2, rows, hidden), BF),
        "dA": ((rows, width), BF),
        "dQ": ((rows, width), BF),
        "dK": ((keys, width), BF),
        "dV": ((keys, width), BF),
    }


def vmem(shape_type):
    return pltpu.VMEM(*shape_type)


ONCE = pl.Buffered(1)


def whole(shape):
    return pl.BlockSpec(tuple(shape), lambda _: (0,) * len(shape), pipeline_mode=ONCE)


def image_of(array, image):
    return pl.BlockSpec(
        (None,) + array.shape[1:],
        lambda _: (image,) + (0,) * (array.ndim - 1),
        pipeline_mode=ONCE,
    )


ANY = pl.BlockSpec(memory_space=pl.ANY)


def shape_of(shape_type):
    return jax.ShapeDtypeStruct(*shape_type)


def nothing(shapes):
    return pl.pallas_call(
        lambda *refs: None,
        out_shape=[shape_of(s) for s in shapes],
        out_specs=[ANY] * len(shapes),
        name="no_values",
    )()


def params_of(**extra):
    return pltpu.CompilerParams(vmem_limit_bytes=VMEM_BYTES, **extra)


def block_cost(rows, keys, width, hidden, passes):
    flops = 2 * rows * width * (2 * width + 4 * hidden) + 4 * keys * width * width
    flops += 4 * rows * keys * width
    return pl.CostEstimate(flops=passes * flops, bytes_accessed=24_000_000, transcendentals=0)


def encoder_forward(image, which, patches, order_column, vec, up_bias, matrices, save):
    images, places, width = patches.shape
    rows = places // 2
    hidden = matrices[4].shape[1]
    local = width // 2
    shapes = kept_shapes(rows, rows, width, hidden)
    names = [n for n in KEPT]

    def kernel(patch_ref, order_ref, vec_ref, bias_ref, *refs):
        sources, refs = refs[:8], refs[8:]
        result, refs = refs[0], refs[1:]
        if save:
            keep = dict(zip(names, refs[: len(names)]))
            refs = refs[len(names) :]
        else:
            own = [n for n in names if n not in ("X", "G", "D")]
            keep = dict(zip(own, refs[: len(own)]))
            refs = refs[len(own) :]
        rows_ref, refs = refs[0], refs[1:]
        weights = Weights(sources, refs[:4], refs[4], first_only=not save)
        weights.start(("qkv", "out", "up", "down"))
        rows_ref[...] = pick_rows(order_ref[...], patch_ref[...])
        if save:
            keep["X"][...] = rows_ref[...].astype(BF)

        def result_fn(rows_at, value):
            result[rows_at, :] = value.astype(BF)

        forward(rows_ref, 0, vec_ref, bias_ref, weights, keep, result_fn)

    out_shapes = [((rows, width), BF)] + ([shapes[n] for n in names] if save else [])
    out_specs = [whole(s[0]) for s in out_shapes]
    patch_spec = image_of(patches, image)
    scratch = [] if save else [vmem(shapes[n]) for n in names if n not in ("X", "G", "D")]
    scratch = scratch + [pltpu.VMEM((rows, width), F32)] + weight_scratch(width, local, hidden)
    order_spec = pl.BlockSpec(
        (None, rows, 1), lambda _: (image, which, 0), pipeline_mode=ONCE
    )
    if not save:
        out_shapes = [((images, rows, width), BF)]
        out_specs = [pl.BlockSpec((None, rows, width), lambda i: (i, 0, 0))]
        patch_spec = pl.BlockSpec((None, places, width), lambda i: (i, 0, 0))
        order_spec = pl.BlockSpec((None, rows, 1), lambda i: (i, which, 0))
    return pl.pallas_call(
        kernel,
        grid=(1 if save else images,),
        out_shape=[shape_of(s) for s in out_shapes],
        in_specs=[patch_spec, order_spec, whole(vec.shape), whole(up_bias.shape)] + [ANY] * 8,
        out_specs=out_specs,
        scratch_shapes=scratch,
        compiler_params=params_of(),
        cost_estimate=block_cost(rows, rows, width, hidden, 1),
        name="encoder_forward" if save else "encoder_targets",
    )(patches, order_column, vec, up_bias, *matrices)


def encoder_backward(image, latent_grad, cotangent, order_row, kept, vec, matrices):
    rows, width = latent_grad.shape
    hidden = matrices[4].shape[1]
    local = width // 2
    shapes = grad_shapes(rows, rows, width, hidden)
    names = list(GRADS)

    def kernel(back_ref, cot_ref, order_ref, vec_ref, *refs):
        sources, refs = refs[:8], refs[8:]
        keep = dict(zip(KEPT, refs[: len(KEPT)]))
        refs = refs[len(KEPT) :]
        input_grad, vec_grad, bias_grad, refs = refs[0], refs[1], refs[2], refs[3:]
        grads = dict(zip(names, refs[: len(names)]))
        refs = refs[len(names) :]
        rows_ref, d_hidden, d_mid, d_out, d_norm, sums = refs[:6]
        weights = Weights(sources, refs[6:10], refs[10])
        weights.start(("down", "up", "out", "qkv"))
        work = {"dH": d_hidden, "dM": d_mid, "dO": d_out, "dN": d_norm}
        rows_ref[...] = keep["X"][...].astype(F32)

        def out_grad_fn(rows_at):
            return cot_ref[rows_at, :].astype(F32) + back_ref[rows_at, :].astype(F32)

        backward(rows_ref, 0, out_grad_fn, vec_ref, weights, keep, grads, work, sums, bias_grad)
        write_sums(sums, vec_grad)

        def join(rows_at):
            total = d_norm[rows_at, :] + d_hidden[rows_at, :]
            high = total.astype(BF)
            d_out[rows_at, :] = high
            grads_low[rows_at, :] = (total - high.astype(F32)).astype(BF)

        grads_low = refs[11]
        row_loop(rows, join)

        def place(index, carry):
            first = pl.multiple_of(index * 128, 128)
            places = lax.broadcasted_iota(jnp.int32, (128, rows), 0) + first
            hot = (places == order_ref[...]).astype(F32).astype(BF)
            input_grad[pl.ds(first, 128), :] = dot(hot, d_out[...]) + dot(hot, grads_low[...])
            return carry

        lax.fori_loop(0, input_grad.shape[0] // 128, place, 0)

    out_shapes = [((2 * rows, width), F32), ((8, width), F32), ((2, 1, hidden), F32)]
    out_shapes += [shapes[n] for n in names]
    scratch = [
        pltpu.VMEM((rows, width), F32),
        pltpu.VMEM((rows, width), F32),
        pltpu.VMEM((rows, width), F32),
        pltpu.VMEM((rows, width), BF),
        pltpu.VMEM((rows, width), F32),
        pltpu.VMEM((8, 8, width), F32),
    ]
    scratch += weight_scratch(width, local, hidden) + [pltpu.VMEM((rows, width), BF)]
    order_spec = pl.BlockSpec((None, 1, rows), lambda _: (image, 0, 0), pipeline_mode=ONCE)
    outs = pl.pallas_call(
        kernel,
        grid=(1,),
        out_shape=[shape_of(s) for s in out_shapes],
        in_specs=[whole(latent_grad.shape), image_of(cotangent, image), order_spec, whole(vec.shape)]
        + [ANY] * 8
        + [whole(k.shape) for k in kept],
        out_specs=[whole(s[0]) for s in out_shapes],
        scratch_shapes=scratch,
        compiler_params=params_of(),
        cost_estimate=block_cost(rows, rows, width, hidden, 1),
        name="encoder_backward",
    )(latent_grad, cotangent, order_row, vec, *matrices, *kept)
    return tuple(outs)


def operand_shapes(rows, keys, width, hidden):
    shapes = dict(grad_shapes(rows, keys, width, hidden))
    shapes.update(kept_shapes(rows, keys, width, hidden))
    return [shapes[n] for n in OPERANDS]


def regressor_block(image, latent, codes, token, cotangent, vec, up_bias, matrices):
    ctx, width = latent.shape
    rows = codes.shape[1] - ctx
    keys = rows + ctx
    hidden = matrices[4].shape[1]
    local = width // 2
    kept = kept_shapes(rows, keys, width, hidden)
    shapes = grad_shapes(rows, keys, width, hidden)
    own = [n for n in KEPT if n != "X" and n not in OPERANDS]

    def kernel(latent_ref, code_ref, token_ref, cot_ref, vec_ref, bias_ref, *refs):
        sources, refs = refs[:8], refs[8:]
        result, back, input_grad, vec_grad, bias_grad = refs[:5]
        refs = refs[5:]
        named = dict(zip(OPERANDS, refs[: len(OPERANDS)]))
        refs = refs[len(OPERANDS) :]
        keep = dict(named)
        keep.update(zip(own, refs[: len(own)]))
        refs = refs[len(own) :]
        rows_ref, d_hidden, d_mid, d_out, sums = refs[:5]
        weights = Weights(sources, refs[5:9], refs[9])
        weights.start(("qkv", "out", "up", "down"))

        def fill(rows_at):
            rows_ref[rows_at, :] = latent_ref[rows_at, :].astype(F32) + code_ref[rows_at, :]
            lower = pl.ds(rows_at.start + ctx, ROWS_AT_ONCE)
            rows_ref[lower, :] = token_ref[...] + code_ref[lower, :]

        row_loop(ctx, fill)

        def result_fn(rows_at, value):
            result[rows_at, :] = value.astype(BF)

        forward(rows_ref, ctx, vec_ref, bias_ref, weights, keep, result_fn)
        work = {"dH": d_hidden, "dM": d_mid, "dO": d_out, "dN": input_grad}

        def out_grad_fn(rows_at):
            return cot_ref[rows_at, :].astype(F32)

        weights.wait = lambda name: None
        backward(
            rows_ref, ctx, out_grad_fn, vec_ref, weights, keep, named, work, sums, bias_grad
        )

        def leave(rows_at):
            back[rows_at, :] = input_grad[rows_at, :].astype(BF)
            lower = pl.ds(rows_at.start + ctx, ROWS_AT_ONCE)
            total = input_grad[lower, :] + d_hidden[rows_at, :]
            input_grad[lower, :] = total
            sums[7] += fold_rows(total)

        row_loop(rows, leave)
        write_sums(sums, vec_grad)

    out_shapes = [
        ((rows, width), BF),
        ((ctx, width), BF),
        ((keys, width), F32),
        ((8, width), F32),
        ((2, 1, hidden), F32),
    ] + operand_shapes(rows, keys, width, hidden)
    scratch = [vmem(kept[n]) for n in own]
    scratch += [
        pltpu.VMEM((keys, width), F32),
        pltpu.VMEM((rows, width), F32),
        pltpu.VMEM((rows, width), F32),
        pltpu.VMEM((rows, width), BF),
        pltpu.VMEM((8, 8, width), F32),
    ]
    scratch += weight_scratch(width, local, hidden)
    outs = pl.pallas_call(
        kernel,
        grid=(1,),
        out_shape=[shape_of(s) for s in out_shapes],
        in_specs=[
            whole(latent.shape),
            image_of(codes, image),
            whole(token.shape),
            image_of(cotangent, image),
            whole(vec.shape),
            whole(up_bias.shape),
        ]
        + [ANY] * 8,
        out_specs=[whole(s[0]) for s in out_shapes],
        scratch_shapes=scratch,
        compiler_params=params_of(),
        cost_estimate=block_cost(rows, keys, width, hidden, 2),
        name="regressor_block",
    )(latent, codes, token, cotangent, vec, up_bias, *matrices)
    return outs


def weight_grad(name, lefts, rights, first_rows, split_left, step, halves):
    images = len(lefts)
    wide = (lefts if split_left else rights)[0]
    other = (rights if split_left else lefts)[0]
    if wide.ndim == 3:
        blocks = (wide.shape[0], wide.shape[2] // step)
        wide_spec = pl.BlockSpec((None, wide.shape[1], step), lambda h, c: (h, 0, c))
        width = wide.shape[2]
    else:
        blocks = (halves, wide.shape[1] // halves // step)
        wide_spec = pl.BlockSpec(
            (wide.shape[0], step), lambda h, c: (0, h * blocks[1] + c)
        )
        width = wide.shape[1] // halves
    other_spec = pl.BlockSpec(other.shape, lambda h, c: (0, 0))
    if split_left:
        out = ((halves, width, other.shape[1]), BF)
        out_spec = pl.BlockSpec((None, step, other.shape[1]), lambda h, c: (h, c, 0))
    else:
        out = ((halves, other.shape[1], width), BF)
        out_spec = pl.BlockSpec((None, other.shape[1], step), lambda h, c: (h, 0, c))

    def kernel(*refs):
        total = None
        for at in range(images):
            left, right = refs[at][...], refs[images + at][...]
            if first_rows:
                left = left[first_rows:]
            part = dot(left, right, TN)
            total = part if total is None else total + part
        refs[-1][...] = total.astype(BF)

    specs = ([wide_spec] * images + [other_spec] * images) if split_left else (
        [other_spec] * images + [wide_spec] * images
    )
    rows = rights[0].shape[-2]
    return pl.pallas_call(
        kernel,
        grid=blocks,
        out_shape=shape_of(out),
        in_specs=specs,
        out_specs=out_spec,
        compiler_params=params_of(),
        cost_estimate=pl.CostEstimate(
            flops=2 * images * rows * halves * width * other.shape[1],
            bytes_accessed=8_000_000,
            transcendentals=0,
        ),
        name=name,
    )(*lefts, *rights)


def matrix_grads(operands, ctx):
    named = [dict(zip(OPERANDS, one)) for one in operands]

    def column(name):
        return [one[name] for one in named]

    down = weight_grad("down_grad", column("G"), column("dF"), 0, True, 512, 2)
    up = weight_grad("up_grad", column("M"), column("dU"), 0, False, 512, 2)
    out = weight_grad("out_grad", column("O"), column("dA"), 0, True, 384, 2)
    query = weight_grad("query_grad", column("N"), column("dQ"), ctx, False, 384, 2)
    key = weight_grad("key_grad", column("N"), column("dK"), 0, False, 384, 2)
    value = weight_grad("value_grad", column("N"), column("dV"), 0, False, 384, 2)
    return down, up, out, query, key, value


UNIT = 128
LAG = 2
GIVE = 8


class Exchange:
    LINE = 4
    WIDE = 10
    DEEP = 8
    UNITS = 2 * WIDE + 2 * DEEP


def exchange_kernel(images, *refs):
    count = len(OPERANDS)
    sources = []
    for _ in range(2):
        sources.append([dict(zip(OPERANDS, refs[at * count :])) for at in range(images)])
        refs = refs[images * count :]
    vec_refs, bias_refs, refs = refs[:images], refs[images : 2 * images], refs[2 * images :]
    down_ref, up_ref, out_ref, qkv_ref = (ref.at[0] for ref in refs[:4])
    totals_ref, other_ref = refs[4:6]
    refs = refs[6:]
    held = dict(zip(OPERANDS, refs[:count]))
    acc, gives, wide_out = refs[count : count + 3]
    refs = refs[count + 3 :]
    total, own_half, from_column, from_line, from_deep, from_side, done = refs[:7]
    small_ref, small_own, small_half, small_side, small_line = refs[7:12]
    (load_sem, half_send, half_recv, x1_send, x1_recv, x2_send, x2_recv, z1_send, z1_recv) = refs[12:21]
    (z2_send, z2_recv, ax_send, ax_recv, a2_send, a2_recv, a1_send, a1_recv) = refs[21:29]
    (a4_send, a4_recv, out_sem, s_send, s_recv) = refs[29:34]
    line, wide, deep = Exchange.LINE, Exchange.WIDE, Exchange.DEEP
    dp = lax.axis_index("dp")
    place, column = dp // 2, dp % 2
    side = {"dp": place * 2 + 1 - column}
    partner = {"head": 1 - lax.axis_index("head")}
    mirror = {"stream": 1 - lax.axis_index("stream")}

    def along(direction, ahead):
        return {"dp": dp + 2 * (2 * direction - 1) * ahead}

    ranks = (line - 1 - place, place)

    stream = lax.axis_index("stream")
    rows, width = held["M"].shape[1:]
    hidden = held["G"].shape[3]
    local = width // 2

    def load(names, method):
        for which in range(2):

            @pl.when(stream == which)
            def _():
                for image, source in enumerate(sources[which]):
                    for name in names:
                        at = OPERANDS.index(name)
                        target = held[name].at[image]
                        if source[name].shape != target.shape:
                            target = target.at[pl.ds(0, source[name].shape[0]), :]
                        copy = pltpu.make_async_copy(source[name], target, load_sem.at[at, image])
                        getattr(copy, method)()

    soon = ("G", "dF", "M", "dU")
    rest = tuple(name for name in OPERANDS if name not in soon)
    load(soon, "start")
    load(rest, "start")

    def unit(buffer, at):
        return buffer.at[pl.ds(pl.multiple_of(at * UNIT, UNIT), UNIT), :]

    def remote(source, target, send, recv, device):
        return pltpu.make_async_remote_copy(
            src_ref=source,
            dst_ref=target,
            send_sem=send,
            recv_sem=recv,
            device_id=device,
            device_id_type=pl.DeviceIdType.MESH,
        )

    barrier = pltpu.get_barrier_semaphore()

    def greet(device):
        pl.semaphore_signal(barrier, inc=1, device_id=device, device_id_type=pl.DeviceIdType.MESH)

    for device in (partner, side, mirror):
        greet(device)
    for ahead in range(1, line):
        greet({"dp": ((place + ahead) % line) * 2 + column})
    pl.semaphore_wait(barrier, 2 + line)

    small_ref[...] = jnp.zeros_like(small_ref)
    small_ref[0:8, :] = sum(ref[...] for ref in vec_refs)
    for half in range(2):
        for at in range(hidden // width):
            row = 8 * (half + 1) + at
            cols = slice(at * width, (at + 1) * width)
            small_ref[row : row + 1, :] = sum(ref[half, :, cols] for ref in bias_refs)
    small_out = remote(small_ref, small_half, s_send.at[1], s_recv.at[0], partner)
    small_out.start()

    first_up = hidden // UNIT
    first_out = 2 * first_up
    first_pair = first_out + local // UNIT
    first_query = first_pair + width // UNIT
    bounds = (0, first_up, first_out, first_pair, first_query, Exchange.UNITS)

    def by_kind(at, bodies):
        for kind, one in enumerate(bodies):

            @pl.when((at >= bounds[kind]) & (at < bounds[kind + 1]))
            def _():
                one(at - bounds[kind])

    def block(at, size=UNIT):
        return pl.ds(pl.multiple_of(at * size, size), size)

    def summed(one):
        parts = [one(image) for image in range(images)]
        return functools.reduce(jnp.add, parts)

    def product(at, half):
        cols = slice(half * local, (half + 1) * local)
        query_rows = pl.ds(pl.multiple_of(stream * rows, rows), rows)

        def down(index):
            acc[...] = summed(
                lambda i: dot(held["G"][i, half, :, block(index)], held["dF"][i], TN)
            )

        def up(index):
            per = width // UNIT
            acc[...] = summed(
                lambda i: dot(
                    held["M"][i, :, block(index % per)],
                    held["dU"][i, half, :, block(index // per, width)],
                    TN,
                )
            )

        def out(index):
            acc[...] = summed(
                lambda i: dot(
                    held["O"][i, :, block(half * (local // UNIT) + index)], held["dA"][i], TN
                )
            )

        def pair(index):
            def part(name, keys):
                return summed(
                    lambda i: dot(held["N"][i, keys, block(index)], held[name][i, keys, cols], TN)
                )

            acc[:, :local] = part("dK", slice(0, rows))
            acc[:, local:] = part("dV", slice(0, rows))

            @pl.when(stream == 1)
            def _():
                acc[:, :local] += part("dK", slice(rows, None))
                acc[:, local:] += part("dV", slice(rows, None))

        def query(index):
            for at in range(2):
                acc[:, at * local : (at + 1) * local] = summed(
                    lambda i: dot(
                        held["N"][i, query_rows, block(at * (local // UNIT) + index)],
                        held["dQ"][i, :, cols],
                        TN,
                    )
                )

        by_kind(at, (down, up, out, pair, query))

    def chunks(body):
        def step(index, carry):
            body(pl.multiple_of(index * 32, 32))
            return carry

        lax.fori_loop(0, UNIT // 32, step, 0)

    def half_copy(slot, at):
        return remote(
            unit(gives, slot), unit(own_half, at), half_send.at[slot], half_recv.at[at], partner
        )

    def unit_of(step, index):
        second = index * (3 - index) // 2
        own = index // 2
        wide_unit = 2 * step + 1 - column + own * (2 * column - 1)
        return wide_unit + second * (2 * wide + 2 * step + own - wide_unit), second

    def make_give(step):
        def body(index, carry):
            at, second = unit_of(step, index)

            @pl.when((step < wide) & (second * step < deep))
            def _():
                slot = (4 * step + index) % GIVE

                @pl.when(4 * step >= GIVE)
                def _():
                    half_copy(slot, at).wait_send()

                product(at, 1)

                def convert(offset):
                    gives[pl.ds(pl.multiple_of(slot * UNIT + offset, 32), 32), :] = acc[
                        pl.ds(offset, 32), :
                    ].astype(BF)

                chunks(convert)
                half_copy(slot, at).start()

            return carry

        lax.fori_loop(0, 4, body, 0)

    def make_own(step):
        def body(index, carry):
            at, second = unit_of(step, index)

            @pl.when((step >= 0) & (step < wide) & (second * step < deep))
            def _():
                product(at, 0)
                half_copy(0, at).wait_recv()

                def join(offset):
                    where = pl.ds(pl.multiple_of(at * UNIT + offset, 32), 32)
                    total[where, :] = (
                        acc[pl.ds(offset, 32), :] + own_half[where, :].astype(F32)
                    ).astype(BF)

                chunks(join)

                @pl.when(index == 0)
                def _():
                    x1(step).start()

                for direction in range(2):

                    @pl.when((index == 1 + direction) & (ranks[direction] == 0))
                    def _():
                        z1(direction, step).start()

            return carry

        lax.fori_loop(0, 4, body, 0)

    def add(target, at, first, first_at, second, second_at):
        def body(index, carry):
            offset = index * 32
            left = first[pl.ds(pl.multiple_of(first_at * UNIT + offset, 32), 32), :]
            right = second[pl.ds(pl.multiple_of(second_at * UNIT + offset, 32), 32), :]
            target[pl.ds(pl.multiple_of(at * UNIT + offset, 32), 32), :] = (
                left.astype(F32) + right.astype(F32)
            ).astype(BF)
            return carry

        lax.fori_loop(0, UNIT // 32, body, 0)

    def x1(at):
        return remote(
            unit(total, 2 * at + 1 - column), unit(from_column, at), x1_send.at[at], x1_recv.at[at], side
        )

    def x2(direction, at, ahead=1):
        slot = direction * (wide // 2) + at
        return remote(
            unit(total, 4 * at + 2 * direction + column),
            unit(from_line, slot),
            x2_send.at[slot],
            x2_recv.at[slot],
            along(direction, ahead),
        )

    def z1(direction, at):
        slot = direction * deep + at
        return remote(
            unit(total, 2 * wide + 2 * at + direction),
            unit(from_deep, slot),
            z1_send.at[slot],
            z1_recv.at[slot],
            along(direction, 1),
        )

    def z2(direction, at):
        return remote(
            unit(total, 2 * wide + 2 * at + direction),
            unit(from_side, at // 2),
            z2_send.at[at // 2],
            z2_recv.at[at // 2],
            side,
        )

    def finished(at, send, recv, slot, device):
        return remote(unit(done, at), unit(done, at), send.at[slot], recv.at[slot], device)

    def ax(at, sent):
        parity = column if sent else 1 - column
        return finished(2 * at + parity, ax_send, ax_recv, at, side)

    def a2(direction, at):
        slot = direction * (wide // 2) + at
        return finished(
            4 * at + 2 * direction + column, a2_send, a2_recv, slot, along(direction, -1)
        )

    def a1(direction, at):
        slot = direction * deep + at
        return finished(
            2 * wide + 2 * at + direction, a1_send, a1_recv, slot, along(direction, -1)
        )

    def a4(direction, at):
        return finished(2 * wide + 2 * at + direction, a4_send, a4_recv, at // 2, side)

    def put(at):
        def widen(offset):
            where = pl.ds(pl.multiple_of(at * UNIT + offset, 32), 32)
            wide_out[where, :] = done[where, :].astype(F32)

        chunks(widen)

        def send(target, cols=slice(None)):
            pltpu.make_async_copy(unit(wide_out, at).at[:, cols], target, out_sem.at[at]).start()

        left, right = pl.ds(0, local), pl.ds(local, local)

        def up(index):
            per = width // UNIT
            send(up_ref.at[block(index % per), block(index // per, width)])

        def pair(index):
            send(qkv_ref.at[1, block(index), :], left)
            send(qkv_ref.at[2, block(index), :], right)

        def query(index):
            send(qkv_ref.at[0, block(index), :], left)
            send(qkv_ref.at[0, block(local // UNIT + index), :], right)

        by_kind(
            at,
            (
                lambda index: send(down_ref.at[block(index), :]),
                up,
                lambda index: send(out_ref.at[block(index), :]),
                pair,
                query,
            ),
        )

    def small_phase(step):
        @pl.when(step == 2)
        def _():
            small_out.wait_recv()
            small_own[0:8, :] = small_ref[0:8, :] + small_half[0:8, :]
            small_own[8:16, :] = small_ref[8:16, :] + small_half[16:24, :]
            small_side_copy().start()

        @pl.when(step == 4)
        def _():
            small_side_copy().wait_recv()
            small_line[place] = small_own[...] + small_side[...]
            for ahead in range(1, line):
                small_line_copy(ahead).start()

        @pl.when(step == 8)
        def _():
            for ahead in range(1, line):
                small_line_copy(ahead).wait_recv()
            summed = small_line[0]
            for at in range(1, line):
                summed = summed + small_line[at]
            totals_ref[...] = summed
            small_mirror_copy().start()

    def small_side_copy():
        return remote(small_own, small_side, s_send.at[2], s_recv.at[1], side)

    def small_line_copy(ahead):
        there = (place + ahead) % line
        return remote(
            small_line.at[place],
            small_line.at[place],
            s_send.at[2 + ahead],
            s_recv.at[1 + ahead],
            {"dp": there * 2 + column},
        )

    def small_mirror_copy():
        return remote(
            totals_ref, other_ref, s_send.at[2 + line], s_recv.at[1 + line], mirror
        )

    def step_body(step, carry):
        @pl.when(step == 1)
        def _():
            load(rest, "wait")

        make_give(step + 1)
        make_own(step)

        at = step - LAG

        @pl.when((at >= 0) & (at < wide))
        def _():
            x1(at).wait_recv()
            add(total, 2 * at + column, total, 2 * at + column, from_column, at)
            for direction in range(2):

                @pl.when((at % 2 == direction) & (ranks[direction] == 0))
                def _():
                    x2(direction, at // 2).start()

        for direction in range(2):
            rank = ranks[direction]
            at = step - LAG * rank

            @pl.when((rank >= 1) & (at >= 0) & (at < deep))
            def _():
                where = 2 * wide + 2 * at + direction
                z1(direction, at).wait_recv()
                add(total, where, total, where, from_deep, direction * deep + at)

                @pl.when(rank < line - 1)
                def _():
                    z1(direction, at).start()

                @pl.when((rank == line - 1) & (at % 2 != column))
                def _():
                    z2(direction, at).start()

            twice = step - LAG - LAG * rank - direction

            @pl.when((rank >= 1) & (twice >= 0) & (twice < wide) & (twice % 2 == 0))
            def _():
                at = twice // 2
                where = 4 * at + 2 * direction + column
                x2(direction, at).wait_recv()
                slot = direction * (wide // 2) + at

                @pl.when(rank < line - 1)
                def _():
                    add(total, where, total, where, from_line, slot)
                    x2(direction, at).start()

                @pl.when(rank == line - 1)
                def _():
                    add(done, where, total, where, from_line, slot)
                    a2(direction, at).start()
                    ax(2 * at + direction, True).start()
                    put(where)

            at = step - LAG * line

            @pl.when((rank == line - 1) & (at >= 0) & (at < deep) & (at % 2 == column))
            def _():
                where = 2 * wide + 2 * at + direction
                z2(direction, at).wait_recv()
                add(done, where, total, where, from_side, at // 2)
                a1(direction, at).start()
                a4(direction, at).start()
                put(where)

            later = step - LAG * line - LAG

            @pl.when((rank == line - 1) & (later >= 0) & (later < deep) & (later % 2 != column))
            def _():
                a4(direction, later).wait_recv()
                a1(direction, later).start()
                put(2 * wide + 2 * later + direction)

            back = LAG * (line - 1 - rank)
            twice = step - LAG * line - back - direction

            @pl.when((rank < line - 1) & (twice >= 0) & (twice < wide) & (twice % 2 == 0))
            def _():
                at = twice // 2
                a2(direction, at).wait_recv()

                @pl.when(rank > 0)
                def _():
                    a2(direction, at).start()

                ax(2 * at + direction, True).start()
                put(4 * at + 2 * direction + column)

            for other in range(2):
                at = step - LAG * line - back - LAG * other

                @pl.when(
                    (rank < line - 1)
                    & (at >= 0)
                    & (at < deep)
                    & ((at + column) % 2 == other)
                )
                def _():
                    a1(direction, at).wait_recv()

                    @pl.when(rank > 0)
                    def _():
                        a1(direction, at).start()

                    put(2 * wide + 2 * at + direction)

            twice = step - LAG * line - back - direction - LAG

            @pl.when((twice >= 0) & (twice < wide) & (twice % 2 == 0))
            def _():
                at = twice + direction
                ax(at, False).wait_recv()
                put(2 * at + 1 - column)

        small_phase(step)
        return carry

    steps = wide - 1 + LAG * line + LAG * (line - 1) + LAG + 1
    load(soon, "wait")
    lax.fori_loop(-1, steps, step_body, 0)

    small_mirror_copy().wait()
    small_out.wait_send()
    small_side_copy().wait_send()
    for ahead in range(1, line):
        small_line_copy(ahead).wait_send()

    def drain(at, carry):
        pltpu.make_async_copy(unit(wide_out, at), unit(wide_out, at), out_sem.at[at]).wait()
        return carry

    lax.fori_loop(0, Exchange.UNITS, drain, 0)

    def drain_give(slot, carry):
        half_copy(slot, 0).wait_send()
        return carry

    lax.fori_loop(0, GIVE, drain_give, 0)

    def drain_wide(at, carry):
        x1(at).wait_send()
        ax(at, True).wait_send()
        return carry

    lax.fori_loop(0, wide, drain_wide, 0)
    for direction in range(2):
        rank = ranks[direction]

        def drain_line(at, carry):
            @pl.when(rank < line - 1)
            def _():
                x2(direction, at).wait_send()

            @pl.when(rank > 0)
            def _():
                a2(direction, at).wait_send()

            return carry

        lax.fori_loop(0, wide // 2, drain_line, 0)

        def drain_deep(at, carry):
            @pl.when(rank < line - 1)
            def _():
                z1(direction, at).wait_send()

            @pl.when(rank > 0)
            def _():
                a1(direction, at).wait_send()

            @pl.when((rank == line - 1) & (at % 2 != column))
            def _():
                z2(direction, at).wait_send()

            @pl.when((rank == line - 1) & (at % 2 == column))
            def _():
                a4(direction, at).wait_send()

            return carry

        lax.fori_loop(0, deep, drain_deep, 0)


def exchange(enc_operands, reg_operands, vec_grads, bias_grads, width, local, hidden):
    units, wide, deep = Exchange.UNITS, Exchange.WIDE, Exchange.DEEP
    images = len(enc_operands)

    def buffer(count, dtype=BF):
        return pltpu.VMEM((count * UNIT, width), dtype)

    def sems(*counts):
        return [pltpu.SemaphoreType.DMA((count,)) for count in counts]

    line = Exchange.LINE
    vspec = pl.BlockSpec(memory_space=pltpu.VMEM)
    return pl.pallas_call(
        functools.partial(exchange_kernel, images),
        out_shape=[
            jax.ShapeDtypeStruct((1, hidden, width), F32),
            jax.ShapeDtypeStruct((1, width, hidden), F32),
            jax.ShapeDtypeStruct((1, local, width), F32),
            jax.ShapeDtypeStruct((1, 3, width, local), F32),
            jax.ShapeDtypeStruct((16, width), F32),
            jax.ShapeDtypeStruct((16, width), F32),
        ],
        in_specs=[ANY] * (2 * images * len(OPERANDS)) + [vspec] * (2 * images),
        out_specs=[ANY] * 4 + [vspec, vspec],
        scratch_shapes=[pltpu.VMEM((images,) + one.shape, BF) for one in reg_operands[0]]
        + [
            buffer(1, F32),
            buffer(GIVE),
            buffer(units, F32),
            buffer(units),
            buffer(units),
            buffer(wide),
            buffer(wide),
            buffer(2 * deep),
            buffer(deep // 2),
            buffer(units),
            pltpu.VMEM((24, width), F32),
            pltpu.VMEM((16, width), F32),
            pltpu.VMEM((24, width), F32),
            pltpu.VMEM((16, width), F32),
            pltpu.VMEM((line, 16, width), F32),
            pltpu.SemaphoreType.DMA((len(OPERANDS), images)),
        ]
        + sems(GIVE, units, wide, wide, wide, wide, 2 * deep, 2 * deep)
        + sems(deep // 2, deep // 2, wide, wide, wide, wide, 2 * deep, 2 * deep)
        + sems(deep // 2, deep // 2, units, 3 + line, 2 + line),
        compiler_params=params_of(collective_id=0, has_side_effects=True),
        cost_estimate=pl.CostEstimate(flops=0, bytes_accessed=200_000_000, transcendentals=0),
        name="gradient_exchange",
    )(*sum(enc_operands, []), *sum(reg_operands, []), *vec_grads, *bias_grads)


def place_code(positions, model_width):
    half_width = model_width // 2
    frequency = jnp.exp(
        jnp.arange(half_width, dtype=F32) * (-math.log(10000.0) / half_width)
    )
    angles = positions.astype(F32)[..., None] * frequency
    return jnp.sin(jnp.concatenate([angles, angles + 0.5 * math.pi], -1))


def shards(
    patches,
    order,
    cotangent,
    norm_gains,
    norm_biases,
    layer_scales,
    qkv_weight,
    out_weight,
    up_weight,
    up_bias,
    down_weight,
    down_bias,
    mask_token,
):
    images, places, width = patches.shape
    rows = places // 2
    hidden = up_weight.shape[2]
    local = width // 2
    encoder = lax.axis_index("stream") == 0

    def swapped(value):
        return lax.ppermute(value, "head", SWAP)

    own = (qkv_weight[0], out_weight[0], up_weight[0], down_weight[0])
    matrices = []
    for value in own:
        matrices += [value, swapped(value)]
    bias_pair = jnp.stack([up_bias[0], swapped(up_bias[0])]).astype(F32)[:, None, :]
    vec = jnp.concatenate(
        [
            norm_gains[0],
            norm_biases[0],
            layer_scales[0],
            down_bias[0][None],
            jnp.zeros((1, width), F32),
        ]
    )
    token = mask_token[None]
    cotangent = cotangent[0]
    order_column = order[:, :, None]
    order_row = order[:, None, :]

    kept_list = list(kept_shapes(rows, rows, width, hidden).values())
    row_shape = ((rows, width), BF)
    code_shape = ((images, places, width), F32)
    grad_list = list(grad_shapes(rows, rows, width, hidden).values())
    operand_list = operand_shapes(rows, places, width, hidden)

    kept, latents = [], []
    codes = None
    for image in range(images):

        def run_encoder():
            outs = encoder_forward(
                image, 0, patches, order_column, vec, up_bias=bias_pair, matrices=matrices, save=True
            )
            return tuple(outs) + ((nothing([code_shape])[0],) if image == 0 else ())

        def run_other():
            outs = nothing([row_shape] + kept_list)
            return tuple(outs) + ((place_code(order, width),) if image == 0 else ())

        outs = lax.cond(encoder, run_encoder, run_other)
        if image == 0:
            codes = outs[-1]
            outs = outs[:-1]
        latents.append(outs[0])
        kept.append(outs[1:])
    arrived = [lax.ppermute(one, "stream", [(0, 1)]) for one in latents]

    features, returned, reg_inputs, reg_vecs, reg_biases, reg_operands = [], [], [], [], [], []
    for image in range(images):

        def run_targets():
            rest = tuple(
                nothing(
                    [row_shape, row_shape, ((places, width), F32)]
                    + [((8, width), F32), ((2, 1, hidden), F32)]
                    + operand_list
                )
            )
            if image == 0:
                rest += tuple(
                    encoder_forward(
                        None, 1, patches, order_column, vec, bias_pair, matrices, save=False
                    )
                )
            return rest

        def run_regressor():
            outs = regressor_block(
                image, arrived[image], codes, token, cotangent, vec, bias_pair, matrices
            )
            if image == 0:
                outs = tuple(outs) + tuple(nothing([((images, rows, width), BF)]))
            return tuple(outs)

        outs = lax.cond(encoder, run_targets, run_regressor)
        if image == 0:
            targets = outs[-1]
            outs = outs[:-1]
        features.append(outs[0])
        returned.append(lax.ppermute(outs[1], "stream", [(1, 0)]))
        reg_inputs.append(outs[2])
        reg_vecs.append(outs[3])
        reg_biases.append(outs[4])
        reg_operands.append(list(outs[5:]))

    input_grads, vec_grads, bias_grads, enc_operands = [], [], [], []
    for image in range(images):

        def run_backward():
            return encoder_backward(
                image, returned[image], cotangent, order_row[:, :, :rows], kept[image], vec, matrices
            )

        def run_pass():
            return (reg_inputs[image], reg_vecs[image], reg_biases[image]) + tuple(
                nothing(grad_list)
            )

        outs = lax.cond(encoder, run_backward, run_pass)
        input_grads.append(outs[0])
        vec_grads.append(outs[1])
        bias_grads.append(outs[2])
        named = dict(zip(KEPT, kept[image]))
        named.update(zip(GRADS, outs[3:]))
        enc_operands.append([named[name] for name in OPERANDS])

    if lax.axis_size("dp") == 2 * Exchange.LINE and width == 768 and hidden == 1536:
        down, up, out, qkv, totals, other = exchange(
            enc_operands, reg_operands, vec_grads, bias_grads, width, local, hidden
        )
        bias_total = totals[8 : 8 + hidden // width].reshape(hidden)
        token_grad = jnp.where(encoder, other[7], totals[7])
    else:
        parts = lax.cond(
            encoder,
            lambda: matrix_grads(enc_operands, 0),
            lambda: matrix_grads(reg_operands, rows),
        )
        vec_grad = sum(vec_grads)
        bias_grad = sum(bias_grads)[:, 0]

        def reduced(value):
            mine = value[0].astype(F32) + swapped(value[1]).astype(F32)
            part = lax.psum_scatter(mine.astype(BF), "dp", scatter_dimension=0, tiled=True)
            return lax.all_gather(part, "dp", axis=0, tiled=True).astype(F32)

        down, up, out, query, key, value = (reduced(one) for one in parts)
        qkv = jnp.stack([query, key, value])
        qkv, out, up, down = (one[None] for one in (qkv, out, up, down))
        bias_total = lax.psum(bias_grad[0] + swapped(bias_grad[1]), "dp")
        totals = lax.psum(vec_grad, ("dp", "head"))
        token_grad = lax.psum(jnp.where(encoder, 0.0, totals[7]), "stream")

    latent_out = jnp.where(encoder, jnp.stack(latents), jnp.stack(arrived))
    return (
        latent_out,
        jnp.where(encoder, targets, jnp.stack(features))[None],
        jnp.stack(input_grads)[None],
        totals[0:2][None],
        totals[2:4][None],
        totals[4:6][None],
        qkv,
        out,
        up,
        bias_total[None],
        down,
        totals[6][None],
        token_grad,
    )


def solution(mesh):
    in_specs = (
        P(("dp", "head"), None, None),
        P(("dp", "head"), None),
        P("stream", ("dp", "head"), None, None),
        P("stream", None, None),
        P("stream", None, None),
        P("stream", None, None),
        P("stream", None, None, "head"),
        P("stream", "head", None),
        P("stream", None, "head"),
        P("stream", "head"),
        P("stream", "head", None),
        P("stream", None),
        P(),
    )
    out_specs = (
        P(("dp", "head"), None, None),
        P("stream", ("dp", "head"), None, None),
        P("stream", ("dp", "head"), None, None),
        P("stream", None, None),
        P("stream", None, None),
        P("stream", None, None),
        P("stream", None, None, "head"),
        P("stream", "head", None),
        P("stream", None, "head"),
        P("stream", "head"),
        P("stream", "head", None),
        P("stream", None),
        P(),
    )
    return jax.shard_map(shards, mesh=mesh, in_specs=in_specs, out_specs=out_specs, check_vma=False)
```

```python
import functools
import math

import jax
import jax.numpy as jnp
from jax import lax
from jax.experimental import pallas as pl
from jax.experimental.pallas import tpu as pltpu
from jax.sharding import PartitionSpec as P

HEADS = 12
EPSILON = 1e-06
BF = jnp.bfloat16
F32 = jnp.float32
ROWS_AT_ONCE = 64
NN = ((1,), (0,))
NT = ((1,), (1,))
TN = ((0,), (0,))
SWAP = ((0, 1), (1, 0))
VMEM_BYTES = 60 * 1024 * 1024


def dot(left, right, dims=NN):
    return lax.dot_general(left, right, (dims, ((), ())), preferred_element_type=F32)


def row_loop(rows, body):
    def step(index, carry):
        body(pl.ds(pl.multiple_of(index * ROWS_AT_ONCE, ROWS_AT_ONCE), ROWS_AT_ONCE))
        return carry

    lax.fori_loop(0, rows // ROWS_AT_ONCE, step, 0)


def halves_loop(size, body):
    def step(half, carry):
        body(half, pl.ds(pl.multiple_of(half * size, size), size))
        return carry

    lax.fori_loop(0, 2, step, 0)


def standardize(values):
    centred = values - jnp.mean(values, -1, keepdims=True)
    inv_std = lax.rsqrt(jnp.mean(centred * centred, -1, keepdims=True) + EPSILON)
    return centred * inv_std, inv_std


def norm_into(source, target, gain, bias):
    def body(rows):
        scaled, _ = standardize(source[rows, :])
        target[rows, :] = (scaled * gain + bias).astype(BF)

    row_loop(source.shape[0], body)


def fold_rows(values):
    return jnp.sum(values.reshape(-1, 8, values.shape[-1]), 0)


def norm_back(grad, scaled, inv_std, gain):
    scaled_grad = grad * gain
    return inv_std * (
        scaled_grad
        - jnp.mean(scaled_grad, -1, keepdims=True)
        - scaled * jnp.mean(scaled_grad * scaled, -1, keepdims=True)
    )


class Weights:
    NAMES = ("qkv", "out", "up", "down")

    def __init__(self, sources, buffers, sems, names=NAMES, first_only=False):
        self.first_only = first_only
        self.buffers = dict(zip(self.NAMES, buffers))
        self.copies = {}
        for at, name in enumerate(self.NAMES):
            if name not in names:
                continue
            for half in range(2):
                self.copies[name, half] = pltpu.make_async_copy(
                    sources[2 * at + half], self.buffers[name].at[half], sems.at[at, half]
                )

    def each(self, names, method):
        def run():
            for name in names:
                for half in range(2):
                    getattr(self.copies[name, half], method)()

        if self.first_only:
            pl.when(pl.program_id(0) == 0)(run)
        else:
            run()

    def start(self, order):
        self.each(order, "start")

    def wait(self, name):
        self.each((name,), "wait")

    def __getitem__(self, name):
        return self.buffers[name]


class Held(dict):
    def __init__(self, buffers):
        super().__init__(buffers)
        self.coming, self.going = {}, {}

    def copy_in(self, names, sources, sems):
        for at, (name, source) in enumerate(zip(names, sources)):
            self.coming[name] = pltpu.make_async_copy(source, self[name], sems.at[at])
            self.coming[name].start()

    def copy_out(self, names, targets, sems):
        for at, (name, target) in enumerate(zip(names, targets)):
            self.going[name] = pltpu.make_async_copy(self[name], target, sems.at[at])

    def need(self, *names):
        for name in names:
            if name in self.coming:
                self.coming[name].wait()

    def ready(self, *names):
        for name in names:
            if name in self.going:
                self.going[name].start()

    def finish(self):
        for copy in self.going.values():
            copy.wait()


def weight_scratch(width, local, hidden):
    return [
        pltpu.VMEM((2, 3, width, local), BF),
        pltpu.VMEM((2, local, width), BF),
        pltpu.VMEM((2, width, hidden), BF),
        pltpu.VMEM((2, hidden, width), BF),
        pltpu.SemaphoreType.DMA((4, 2)),
    ]


def head_masks():
    lanes = lax.broadcasted_iota(jnp.int32, (1, 128), 1)
    low = (lanes < 64).astype(F32)
    return low.astype(BF), (1.0 - low).astype(BF)


def forward(rows_all, ctx, vec, up_bias, weights, keep, result_fn):
    width = rows_all.shape[1]
    row_count = rows_all.shape[0] - ctx
    normed, queries, keys, values, probs, mixed = (
        keep[name] for name in ("N", "Q", "K", "V", "P", "O")
    )
    norm_into(rows_all, normed, vec[0:1, :], vec[2:3, :])
    keep.ready("N")
    weights.wait("qkv")
    local = weights["qkv"].shape[3]

    def project(half, cols):
        queries[:, cols] = (dot(normed[ctx:, :], weights["qkv"][half, 0]) * 0.125).astype(BF)
        keys[:, cols] = dot(normed[...], weights["qkv"][half, 1]).astype(BF)
        values[:, cols] = dot(normed[...], weights["qkv"][half, 2]).astype(BF)

    halves_loop(local, project)
    keep.ready("Q", "K", "V")
    masks = head_masks()

    def attend(pair, carry):
        cols = pl.ds(pl.multiple_of(pair * 128, 128), 128)
        query, key = queries[:, cols], keys[:, cols]
        value_t = values[:, cols].T
        outs = []
        for at in range(2):
            scores = dot(key, query * masks[at], NT)
            weight = jnp.exp(scores - jnp.max(scores, 0, keepdims=True))
            prob = (weight * (1.0 / jnp.sum(weight, 0, keepdims=True))).astype(BF)
            probs[2 * pair + at] = prob
            outs.append(dot(value_t[64 * at : 64 * at + 64], prob))
        mixed[:, cols] = jnp.concatenate(outs, 0).T.astype(BF)
        return carry

    lax.fori_loop(0, HEADS // 2, attend, 0)
    keep.ready("P", "O")
    weights.wait("out")
    attended = dot(mixed[:, :local], weights["out"][0]) + dot(mixed[:, local:], weights["out"][1])
    hidden, normed_two = keep["H"], keep["M"]
    keep["A"][...] = attended.astype(keep["A"].dtype)
    hidden[...] = rows_all[ctx:, :] + vec[4:5, :] * attended
    norm_into(hidden, normed_two, vec[1:2, :], vec[3:4, :])
    keep.ready("A", "H", "M")
    weights.wait("up")
    weights.wait("down")
    fed = keep["F"]
    fed[...] = jnp.broadcast_to(vec[6:7, :], fed.shape)
    step = 512
    per_half = weights["up"].shape[2] // step

    def feed(index, carry):
        half, chunk = index // per_half, index % per_half
        cols = pl.ds(pl.multiple_of(chunk * step, step), step)
        pre = dot(normed_two[...], weights["up"][half, :, cols]) + up_bias[half, :, cols]
        phi = 0.5 + 0.5 * lax.erf(pre * math.sqrt(0.5))
        act = (pre * phi).astype(BF)
        if "G" in keep:
            keep["G"][half, :, cols] = act
            density = jnp.exp(pre * pre * -0.5) * (1.0 / math.sqrt(2.0 * math.pi))
            keep["D"][half, :, cols] = (phi + pre * density).astype(BF)
        fed[...] += dot(act, weights["down"][half, cols, :])
        return carry

    lax.fori_loop(0, 2 * per_half, feed, 0)

    keep.ready("G", "D", "F")

    def finish(rows):
        result_fn(rows, hidden[rows, :] + vec[5:6, :] * fed[rows, :])

    row_loop(row_count, finish)


def backward(rows_all, ctx, out_grad_fn, vec, weights, keep, grads, work, sums, up_bias_grad):
    width = rows_all.shape[1]
    row_count = rows_all.shape[0] - ctx
    local = width // 2
    grad_in = work["dH"]
    for at in range(8):
        sums[at] = jnp.zeros((8, width), F32)

    def enter(rows):
        grad = out_grad_fn(rows)
        grad_in[rows, :] = grad
        branch = vec[5:6, :] * grad
        sums[5] += fold_rows(grad * keep["F"][rows, :].astype(F32))
        sums[6] += fold_rows(branch)
        grads["dF"][rows, :] = branch.astype(BF)

    keep.need("F")
    row_loop(row_count, enter)
    grads.ready("dF")
    keep.need("D")
    weights.wait("down")
    weights.wait("up")
    grad_mid = work["dM"]
    grad_mid[...] = jnp.zeros_like(grad_mid)
    step = 512
    per_half = weights["up"].shape[2] // step

    def feed(index, carry):
        half, chunk = index // per_half, index % per_half
        cols = pl.ds(pl.multiple_of(chunk * step, step), step)
        act_grad = dot(grads["dF"][...], weights["down"][half, cols, :], NT)
        pre_grad = act_grad * keep["D"][half, :, cols].astype(F32)
        up_bias_grad[half, :, cols] = jnp.sum(pre_grad, 0, keepdims=True)
        pre_grad = pre_grad.astype(BF)
        grads["dU"][half, :, cols] = pre_grad
        grad_mid[...] += dot(pre_grad, weights["up"][half, :, cols], NT)
        return carry

    lax.fori_loop(0, 2 * per_half, feed, 0)

    def middle(rows):
        scaled, inv_std = standardize(keep["H"][rows, :])
        grad = grad_mid[rows, :]
        sums[1] += fold_rows(grad * scaled)
        sums[3] += fold_rows(grad)
        hidden_grad = grad_in[rows, :] + norm_back(grad, scaled, inv_std, vec[1:2, :])
        grad_in[rows, :] = hidden_grad
        sums[4] += fold_rows(hidden_grad * keep["A"][rows, :].astype(F32))
        grads["dA"][rows, :] = (vec[4:5, :] * hidden_grad).astype(BF)

    grads.ready("dU")
    keep.need("H", "A")
    row_loop(row_count, middle)
    grads.ready("dA")
    weights.wait("out")
    mix_grad = work["dO"]

    def unmix(half, cols):
        mix_grad[:, cols] = dot(grads["dA"][...], weights["out"][half], NT).astype(BF)

    halves_loop(local, unmix)
    masks = head_masks()

    def attend(pair, carry):
        cols = pl.ds(pl.multiple_of(pair * 128, 128), 128)
        query, key, value = keep["Q"][:, cols], keep["K"][:, cols], keep["V"][:, cols]
        out_grad = mix_grad[:, cols]
        key_t = key.T
        value_grad = key_grad = None
        query_grads = []
        for at in range(2):
            prob = keep["P"][2 * pair + at]
            own_grad = out_grad * masks[at]
            part = dot(prob, own_grad)
            value_grad = part if value_grad is None else value_grad + part
            prob_grad = dot(value, own_grad, NT)
            wide = prob.astype(F32)
            product = wide * prob_grad
            score_grad = (product - wide * jnp.sum(product, 0, keepdims=True)).astype(BF)
            part = dot(score_grad, query * masks[at])
            key_grad = part if key_grad is None else key_grad + part
            query_grads.append(dot(key_t[64 * at : 64 * at + 64], score_grad))
        grads["dV"][:, cols] = value_grad.astype(BF)
        grads["dK"][:, cols] = key_grad.astype(BF)
        grads["dQ"][:, cols] = (jnp.concatenate(query_grads, 0).T * 0.125).astype(BF)
        return carry

    keep.need("P", "Q", "K", "V")
    lax.fori_loop(0, HEADS // 2, attend, 0)
    grads.ready("dQ", "dK", "dV")
    weights.wait("qkv")
    grad_all = work["dN"]
    qkv = weights["qkv"]
    grad_all[...] = jnp.zeros_like(grad_all)

    def unproject(half, cols):
        grad_all[...] += dot(grads["dK"][:, cols], qkv[half, 1], NT) + dot(
            grads["dV"][:, cols], qkv[half, 2], NT
        )
        grad_all[ctx:, :] += dot(grads["dQ"][:, cols], qkv[half, 0], NT)

    halves_loop(local, unproject)

    def leave(rows):
        scaled, inv_std = standardize(rows_all[rows, :].astype(F32))
        grad = grad_all[rows, :]
        sums[0] += fold_rows(grad * scaled)
        sums[2] += fold_rows(grad)
        grad_all[rows, :] = norm_back(grad, scaled, inv_std, vec[0:1, :])

    keep.need("X")
    row_loop(rows_all.shape[0], leave)


def write_sums(sums, target):
    for at in range(8):
        target[at : at + 1, :] = jnp.sum(sums[at], 0, keepdims=True)


def pick_rows(order_column, patches):
    places = lax.broadcasted_iota(jnp.int32, (order_column.shape[0], patches.shape[0]), 1)
    return dot((places == order_column).astype(F32).astype(BF), patches)


READ_BACK = ("F", "D", "H", "A", "P", "Q", "K", "V", "X")
KEPT = ("X", "N", "Q", "K", "V", "P", "O", "A", "H", "M", "G", "D", "F")
GRADS = ("dF", "dU", "dA", "dQ", "dK", "dV")
OPERANDS = ("dF", "G", "dU", "M", "dA", "O", "dQ", "dK", "dV", "N")


def kept_shapes(rows, keys, width, hidden):
    return {
        "X": ((rows, width), BF),
        "N": ((keys, width), BF),
        "Q": ((rows, width), BF),
        "K": ((keys, width), BF),
        "V": ((keys, width), BF),
        "P": ((HEADS, keys, rows), BF),
        "O": ((rows, width), BF),
        "A": ((rows, width), BF),
        "H": ((rows, width), F32),
        "M": ((rows, width), BF),
        "G": ((2, rows, hidden), BF),
        "D": ((2, rows, hidden), BF),
        "F": ((rows, width), F32),
    }


def grad_shapes(rows, keys, width, hidden):
    return {
        "dF": ((rows, width), BF),
        "dU": ((2, rows, hidden), BF),
        "dA": ((rows, width), BF),
        "dQ": ((rows, width), BF),
        "dK": ((keys, width), BF),
        "dV": ((keys, width), BF),
    }


def vmem(shape_type):
    return pltpu.VMEM(*shape_type)


ONCE = pl.Buffered(1)


def whole(shape):
    return pl.BlockSpec(tuple(shape), lambda _: (0,) * len(shape), pipeline_mode=ONCE)


def image_of(array, image):
    return pl.BlockSpec(
        (None,) + array.shape[1:],
        lambda _: (image,) + (0,) * (array.ndim - 1),
        pipeline_mode=ONCE,
    )


ANY = pl.BlockSpec(memory_space=pl.ANY)


def shape_of(shape_type):
    return jax.ShapeDtypeStruct(*shape_type)


def nothing(shapes):
    return pl.pallas_call(
        lambda *refs: None,
        out_shape=[shape_of(s) for s in shapes],
        out_specs=[ANY] * len(shapes),
        name="no_values",
    )()


def params_of(**extra):
    return pltpu.CompilerParams(vmem_limit_bytes=VMEM_BYTES, **extra)


def block_cost(rows, keys, width, hidden, passes):
    flops = 2 * rows * width * (2 * width + 4 * hidden) + 4 * keys * width * width
    flops += 4 * rows * keys * width
    return pl.CostEstimate(flops=passes * flops, bytes_accessed=24_000_000, transcendentals=0)


def encoder_forward(image, which, patches, order_column, vec, up_bias, matrices, save):
    images, places, width = patches.shape
    rows = places // 2
    hidden = matrices[4].shape[1]
    local = width // 2
    shapes = kept_shapes(rows, rows, width, hidden)
    names = [n for n in KEPT]
    own = names if save else [n for n in names if n not in ("X", "G", "D")]

    def kernel(patch_ref, order_ref, vec_ref, bias_ref, *refs):
        sources, refs = refs[:8], refs[8:]
        result, refs = refs[0], refs[1:]
        if save:
            targets, refs = refs[: len(names)], refs[len(names) :]
        keep = Held(zip(own, refs))
        refs = refs[len(own) :]
        rows_ref, refs = refs[0], refs[1:]
        weights = Weights(sources, refs[:4], refs[4], first_only=not save)
        weights.start(("qkv", "out", "up", "down"))
        rows_ref[...] = pick_rows(order_ref[...], patch_ref[...])
        if save:
            keep.copy_out(names, targets, refs[5])
            keep["X"][...] = rows_ref[...].astype(BF)
            keep.ready("X")

        def result_fn(rows_at, value):
            result[rows_at, :] = value.astype(BF)

        forward(rows_ref, 0, vec_ref, bias_ref, weights, keep, result_fn)
        keep.finish()

    out_shapes = [((rows, width), BF)] + ([shapes[n] for n in names] if save else [])
    out_specs = [whole(out_shapes[0][0])] + [ANY] * (len(out_shapes) - 1)
    patch_spec = image_of(patches, image)
    scratch = [vmem(shapes[n]) for n in own] + [pltpu.VMEM((rows, width), F32)]
    scratch += weight_scratch(width, local, hidden) + [pltpu.SemaphoreType.DMA((len(names),))]
    order_spec = pl.BlockSpec(
        (None, rows, 1), lambda _: (image, which, 0), pipeline_mode=ONCE
    )
    if not save:
        out_shapes = [((images, rows, width), BF)]
        out_specs = [pl.BlockSpec((None, rows, width), lambda i: (i, 0, 0))]
        patch_spec = pl.BlockSpec((None, places, width), lambda i: (i, 0, 0))
        order_spec = pl.BlockSpec((None, rows, 1), lambda i: (i, which, 0))
    return pl.pallas_call(
        kernel,
        grid=(1 if save else images,),
        out_shape=[shape_of(s) for s in out_shapes],
        in_specs=[patch_spec, order_spec, whole(vec.shape), whole(up_bias.shape)] + [ANY] * 8,
        out_specs=out_specs,
        scratch_shapes=scratch,
        compiler_params=params_of(),
        cost_estimate=block_cost(rows, rows, width, hidden, 1),
        name="encoder_forward" if save else "encoder_targets",
    )(patches, order_column, vec, up_bias, *matrices)


def encoder_backward(image, latent_grad, cotangent, order_row, kept, vec, matrices):
    rows, width = latent_grad.shape
    hidden = matrices[4].shape[1]
    local = width // 2
    shapes = grad_shapes(rows, rows, width, hidden)
    names = list(GRADS)
    kept = [dict(zip(KEPT, kept))[name] for name in READ_BACK]

    def kernel(back_ref, cot_ref, order_ref, vec_ref, *refs):
        sources, refs = refs[:8], refs[8:]
        saved, refs = refs[: len(READ_BACK)], refs[len(READ_BACK) :]
        input_grad, vec_grad, bias_grad, refs = refs[0], refs[1], refs[2], refs[3:]
        targets, refs = refs[: len(names)], refs[len(names) :]
        keep = Held(zip(READ_BACK, refs))
        grads = Held(zip(names, refs[len(READ_BACK) :]))
        refs = refs[len(READ_BACK) + len(names) :]
        d_hidden, d_mid, d_out, d_norm, sums = refs[:5]
        weights = Weights(sources, refs[5:9], refs[9])
        keep.copy_in(READ_BACK[:2], saved, refs[11])
        weights.start(("down", "up"))
        keep.copy_in(READ_BACK[2:], saved[2:], refs[12])
        weights.start(("out", "qkv"))
        grads.copy_out(names, targets, refs[13])
        work = {"dH": d_hidden, "dM": d_mid, "dO": d_out, "dN": d_norm}

        def out_grad_fn(rows_at):
            return cot_ref[rows_at, :].astype(F32) + back_ref[rows_at, :].astype(F32)

        backward(
            keep["X"], 0, out_grad_fn, vec_ref, weights, keep, grads, work, sums, bias_grad
        )
        write_sums(sums, vec_grad)

        def join(rows_at):
            total = d_norm[rows_at, :] + d_hidden[rows_at, :]
            high = total.astype(BF)
            d_out[rows_at, :] = high
            grads_low[rows_at, :] = (total - high.astype(F32)).astype(BF)

        grads_low = refs[10]
        row_loop(rows, join)

        def place(index, carry):
            first = pl.multiple_of(index * 128, 128)
            places = lax.broadcasted_iota(jnp.int32, (128, rows), 0) + first
            hot = (places == order_ref[...]).astype(F32).astype(BF)
            input_grad[pl.ds(first, 128), :] = dot(hot, d_out[...]) + dot(hot, grads_low[...])
            return carry

        lax.fori_loop(0, input_grad.shape[0] // 128, place, 0)
        grads.finish()

    out_shapes = [((2 * rows, width), F32), ((8, width), F32), ((2, 1, hidden), F32)]
    out_shapes += [shapes[n] for n in names]
    forms = kept_shapes(rows, rows, width, hidden)
    scratch = [vmem(forms[n]) for n in READ_BACK] + [vmem(shapes[n]) for n in names]
    scratch += [
        pltpu.VMEM((rows, width), F32),
        pltpu.VMEM((rows, width), F32),
        pltpu.VMEM((rows, width), BF),
        pltpu.VMEM((rows, width), F32),
        pltpu.VMEM((8, 8, width), F32),
    ]
    scratch += weight_scratch(width, local, hidden) + [pltpu.VMEM((rows, width), BF)]
    scratch += [
        pltpu.SemaphoreType.DMA((2,)),
        pltpu.SemaphoreType.DMA((len(READ_BACK) - 2,)),
        pltpu.SemaphoreType.DMA((len(names),)),
    ]
    order_spec = pl.BlockSpec((None, 1, rows), lambda _: (image, 0, 0), pipeline_mode=ONCE)
    outs = pl.pallas_call(
        kernel,
        grid=(1,),
        out_shape=[shape_of(s) for s in out_shapes],
        in_specs=[whole(latent_grad.shape), image_of(cotangent, image), order_spec, whole(vec.shape)]
        + [ANY] * (8 + len(kept)),
        out_specs=[whole(s[0]) for s in out_shapes[:3]] + [ANY] * len(names),
        scratch_shapes=scratch,
        compiler_params=params_of(),
        cost_estimate=block_cost(rows, rows, width, hidden, 1),
        name="encoder_backward",
    )(latent_grad, cotangent, order_row, vec, *matrices, *kept)
    return tuple(outs)


def operand_shapes(rows, keys, width, hidden):
    shapes = dict(grad_shapes(rows, keys, width, hidden))
    shapes.update(kept_shapes(rows, keys, width, hidden))
    return [shapes[n] for n in OPERANDS]


def regressor_block(image, latent, codes, token, cotangent, vec, up_bias, matrices):
    ctx, width = latent.shape
    rows = codes.shape[1] - ctx
    keys = rows + ctx
    hidden = matrices[4].shape[1]
    local = width // 2
    kept = kept_shapes(rows, keys, width, hidden)
    shapes = grad_shapes(rows, keys, width, hidden)
    own = [n for n in KEPT if n != "X" and n not in OPERANDS]

    def kernel(latent_ref, code_ref, token_ref, cot_ref, vec_ref, bias_ref, *refs):
        sources, refs = refs[:8], refs[8:]
        result, back, input_grad, vec_grad, bias_grad = refs[:5]
        refs = refs[5:]
        targets, refs = refs[: len(OPERANDS)], refs[len(OPERANDS) :]
        held = OPERANDS + tuple(own)
        keep = Held(zip(held, refs))
        refs = refs[len(held) :]
        keep.copy_out(OPERANDS, targets, refs[10])
        rows_ref, d_hidden, d_mid, d_out, sums = refs[:5]
        weights = Weights(sources, refs[5:9], refs[9])
        weights.start(("qkv", "out", "up", "down"))

        def fill(rows_at):
            rows_ref[rows_at, :] = latent_ref[rows_at, :].astype(F32) + code_ref[rows_at, :]
            lower = pl.ds(rows_at.start + ctx, ROWS_AT_ONCE)
            rows_ref[lower, :] = token_ref[...] + code_ref[lower, :]

        row_loop(ctx, fill)

        def result_fn(rows_at, value):
            result[rows_at, :] = value.astype(BF)

        forward(rows_ref, ctx, vec_ref, bias_ref, weights, keep, result_fn)
        work = {"dH": d_hidden, "dM": d_mid, "dO": d_out, "dN": input_grad}

        def out_grad_fn(rows_at):
            return cot_ref[rows_at, :].astype(F32)

        weights.wait = lambda name: None
        backward(
            rows_ref, ctx, out_grad_fn, vec_ref, weights, keep, keep, work, sums, bias_grad
        )

        def leave(rows_at):
            back[rows_at, :] = input_grad[rows_at, :].astype(BF)
            lower = pl.ds(rows_at.start + ctx, ROWS_AT_ONCE)
            total = input_grad[lower, :] + d_hidden[rows_at, :]
            input_grad[lower, :] = total
            sums[7] += fold_rows(total)

        row_loop(rows, leave)
        write_sums(sums, vec_grad)
        keep.finish()

    out_shapes = [
        ((rows, width), BF),
        ((ctx, width), BF),
        ((keys, width), F32),
        ((8, width), F32),
        ((2, 1, hidden), F32),
    ] + operand_shapes(rows, keys, width, hidden)
    scratch = [vmem(one) for one in operand_shapes(rows, keys, width, hidden)]
    scratch += [vmem(kept[n]) for n in own]
    scratch += [
        pltpu.VMEM((keys, width), F32),
        pltpu.VMEM((rows, width), F32),
        pltpu.VMEM((rows, width), F32),
        pltpu.VMEM((rows, width), BF),
        pltpu.VMEM((8, 8, width), F32),
    ]
    scratch += weight_scratch(width, local, hidden)
    scratch += [pltpu.SemaphoreType.DMA((len(OPERANDS),))]
    outs = pl.pallas_call(
        kernel,
        grid=(1,),
        out_shape=[shape_of(s) for s in out_shapes],
        in_specs=[
            whole(latent.shape),
            image_of(codes, image),
            whole(token.shape),
            image_of(cotangent, image),
            whole(vec.shape),
            whole(up_bias.shape),
        ]
        + [ANY] * 8,
        out_specs=[whole(s[0]) for s in out_shapes[:5]] + [ANY] * len(OPERANDS),
        scratch_shapes=scratch,
        compiler_params=params_of(),
        cost_estimate=block_cost(rows, keys, width, hidden, 2),
        name="regressor_block",
    )(latent, codes, token, cotangent, vec, up_bias, *matrices)
    return outs


def weight_grad(name, lefts, rights, first_rows, split_left, step, halves):
    images = len(lefts)
    wide = (lefts if split_left else rights)[0]
    other = (rights if split_left else lefts)[0]
    if wide.ndim == 3:
        blocks = (wide.shape[0], wide.shape[2] // step)
        wide_spec = pl.BlockSpec((None, wide.shape[1], step), lambda h, c: (h, 0, c))
        width = wide.shape[2]
    else:
        blocks = (halves, wide.shape[1] // halves // step)
        wide_spec = pl.BlockSpec(
            (wide.shape[0], step), lambda h, c: (0, h * blocks[1] + c)
        )
        width = wide.shape[1] // halves
    other_spec = pl.BlockSpec(other.shape, lambda h, c: (0, 0))
    if split_left:
        out = ((halves, width, other.shape[1]), BF)
        out_spec = pl.BlockSpec((None, step, other.shape[1]), lambda h, c: (h, c, 0))
    else:
        out = ((halves, other.shape[1], width), BF)
        out_spec = pl.BlockSpec((None, other.shape[1], step), lambda h, c: (h, 0, c))

    def kernel(*refs):
        total = None
        for at in range(images):
            left, right = refs[at][...], refs[images + at][...]
            if first_rows:
                left = left[first_rows:]
            part = dot(left, right, TN)
            total = part if total is None else total + part
        refs[-1][...] = total.astype(BF)

    specs = ([wide_spec] * images + [other_spec] * images) if split_left else (
        [other_spec] * images + [wide_spec] * images
    )
    rows = rights[0].shape[-2]
    return pl.pallas_call(
        kernel,
        grid=blocks,
        out_shape=shape_of(out),
        in_specs=specs,
        out_specs=out_spec,
        compiler_params=params_of(),
        cost_estimate=pl.CostEstimate(
            flops=2 * images * rows * halves * width * other.shape[1],
            bytes_accessed=8_000_000,
            transcendentals=0,
        ),
        name=name,
    )(*lefts, *rights)


def matrix_grads(operands, ctx):
    named = [dict(zip(OPERANDS, one)) for one in operands]

    def column(name):
        return [one[name] for one in named]

    down = weight_grad("down_grad", column("G"), column("dF"), 0, True, 512, 2)
    up = weight_grad("up_grad", column("M"), column("dU"), 0, False, 512, 2)
    out = weight_grad("out_grad", column("O"), column("dA"), 0, True, 384, 2)
    query = weight_grad("query_grad", column("N"), column("dQ"), ctx, False, 384, 2)
    key = weight_grad("key_grad", column("N"), column("dK"), 0, False, 384, 2)
    value = weight_grad("value_grad", column("N"), column("dV"), 0, False, 384, 2)
    return down, up, out, query, key, value


UNIT = 128
LAG = 2
GIVE = 16


class Exchange:
    LINE = 4
    WIDE = 20
    DEEP = 16
    UNITS = 2 * WIDE + 2 * DEEP


def exchange_kernel(images, *refs):
    count = len(OPERANDS)
    sources = []
    for _ in range(2):
        sources.append([dict(zip(OPERANDS, refs[at * count :])) for at in range(images)])
        refs = refs[images * count :]
    vec_refs, bias_refs, refs = refs[:images], refs[images : 2 * images], refs[2 * images :]
    down_ref, up_ref, out_ref, qkv_ref = (ref.at[0] for ref in refs[:4])
    totals_ref, other_ref = refs[4:6]
    refs = refs[6:]
    held = dict(zip(OPERANDS, refs[:count]))
    acc, gives = refs[count : count + 2]
    refs = refs[count + 2 :]
    total, own_half, from_column, from_line, from_deep, from_side, done = refs[:7]
    small_ref, small_own, small_half, small_side, small_line = refs[7:12]
    (load_sem, half_send, half_recv, x1_send, x1_recv, x2_send, x2_recv, z1_send, z1_recv) = refs[12:21]
    (z2_send, z2_recv, ax_send, ax_recv, a2_send, a2_recv, a1_send, a1_recv) = refs[21:29]
    (a4_send, a4_recv, out_sem, s_send, s_recv) = refs[29:34]
    line, wide, deep = Exchange.LINE, Exchange.WIDE, Exchange.DEEP
    dp = lax.axis_index("dp")
    place, column = dp // 2, dp % 2
    side = {"dp": place * 2 + 1 - column}
    partner = {"head": 1 - lax.axis_index("head")}
    mirror = {"stream": 1 - lax.axis_index("stream")}

    def along(direction, ahead):
        return {"dp": dp + 2 * (2 * direction - 1) * ahead}

    ranks = (line - 1 - place, place)

    stream = lax.axis_index("stream")
    rows, width = held["M"].shape[1:]
    hidden = held["G"].shape[3]
    local = width // 2

    def load(names, method):
        for which in range(2):

            @pl.when(stream == which)
            def _():
                for image, source in enumerate(sources[which]):
                    for name in names:
                        at = OPERANDS.index(name)
                        target = held[name].at[image]
                        if source[name].shape != target.shape:
                            target = target.at[pl.ds(0, source[name].shape[0]), :]
                        copy = pltpu.make_async_copy(source[name], target, load_sem.at[at, image])
                        getattr(copy, method)()

    soon = ("G", "dF", "M", "dU")
    rest = tuple(name for name in OPERANDS if name not in soon)
    load(soon, "start")
    load(rest, "start")

    def unit(buffer, at):
        return buffer.at[pl.ds(pl.multiple_of(at * UNIT, UNIT), UNIT), :]

    def remote(source, target, send, recv, device):
        return pltpu.make_async_remote_copy(
            src_ref=source,
            dst_ref=target,
            send_sem=send,
            recv_sem=recv,
            device_id=device,
            device_id_type=pl.DeviceIdType.MESH,
        )

    barrier = pltpu.get_barrier_semaphore()

    def greet(device):
        pl.semaphore_signal(barrier, inc=1, device_id=device, device_id_type=pl.DeviceIdType.MESH)

    for device in (partner, side, mirror):
        greet(device)
    for ahead in range(1, line):
        greet({"dp": ((place + ahead) % line) * 2 + column})
    pl.semaphore_wait(barrier, 2 + line)

    small_ref[...] = jnp.zeros_like(small_ref)
    small_ref[0:8, :] = sum(ref[...] for ref in vec_refs)
    for half in range(2):
        for at in range(hidden // width):
            row = 8 * (half + 1) + at
            cols = slice(at * width, (at + 1) * width)
            small_ref[row : row + 1, :] = sum(ref[half, :, cols] for ref in bias_refs)
    small_out = remote(small_ref, small_half, s_send.at[1], s_recv.at[0], partner)
    small_out.start()

    counts = (
        2 * hidden // UNIT,
        2 * hidden // UNIT,
        2 * local // UNIT,
        width // UNIT,
        width // UNIT,
        width // UNIT,
    )
    bounds = [sum(counts[:at]) for at in range(len(counts) + 1)]

    def by_kind(at, bodies):
        for kind, one in enumerate(bodies):

            @pl.when((at >= bounds[kind]) & (at < bounds[kind + 1]))
            def _():
                one(at - bounds[kind])

    def block(at, size=UNIT):
        return pl.ds(pl.multiple_of(at * size, size), size)

    def summed(one):
        parts = [one(image) for image in range(images)]
        return functools.reduce(jnp.add, parts)

    def product(at, half):
        cols = pl.ds(pl.multiple_of(half * local, local), local)
        query_rows = pl.ds(pl.multiple_of(stream * rows, rows), rows)

        def down(index):
            acc[...] = summed(
                lambda i: dot(
                    held["G"][i, half, :, block(index // 2)],
                    held["dF"][i, :, block(index % 2, local)],
                    TN,
                )
            )

        def up(index):
            per = width // UNIT
            acc[...] = summed(
                lambda i: dot(
                    held["M"][i, :, block(index % per)],
                    held["dU"][i, half, :, block(index // per, local)],
                    TN,
                )
            )

        def out(index):
            acc[...] = summed(
                lambda i: dot(
                    held["O"][i, :, block(half * (local // UNIT) + index // 2)],
                    held["dA"][i, :, block(index % 2, local)],
                    TN,
                )
            )

        def over_keys(name):
            def part(index, keys):
                return summed(
                    lambda i: dot(held["N"][i, keys, block(index)], held[name][i, keys, cols], TN)
                )

            def run(index):
                acc[...] = part(index, slice(0, rows))

                @pl.when(stream == 1)
                def _():
                    acc[...] += part(index, slice(rows, None))

            return run

        def query(index):
            acc[...] = summed(
                lambda i: dot(held["N"][i, query_rows, block(index)], held["dQ"][i, :, cols], TN)
            )

        by_kind(at, (down, up, out, over_keys("dK"), over_keys("dV"), query))

    def chunks(body):
        def step(index, carry):
            body(pl.multiple_of(index * 32, 32))
            return carry

        lax.fori_loop(0, UNIT // 32, step, 0)

    def half_copy(slot, at):
        return remote(
            unit(gives, slot), unit(own_half, at), half_send.at[slot], half_recv.at[at], partner
        )

    def unit_of(step, index):
        second = index * (3 - index) // 2
        own = index // 2
        wide_unit = 2 * step + 1 - column + own * (2 * column - 1)
        return wide_unit + second * (2 * wide + 2 * step + own - wide_unit), second

    def make(now):
        def body(turn, carry):
            index, mine = turn % 4, turn // 4
            step = now + 1 - mine
            at, second = unit_of(step, index)

            @pl.when((step >= 0) & (step < wide) & (second * step < deep))
            def _():
                product(at, 1 - mine)

                @pl.when(mine == 0)
                def _():
                    slot = (4 * step + index) % GIVE

                    @pl.when(4 * step >= GIVE)
                    def _():
                        half_copy(slot, at).wait_send()

                    def convert(offset):
                        gives[pl.ds(pl.multiple_of(slot * UNIT + offset, 32), 32), :] = acc[
                            pl.ds(offset, 32), :
                        ].astype(BF)

                    chunks(convert)
                    half_copy(slot, at).start()

                @pl.when(mine == 1)
                def _():
                    half_copy(0, at).wait_recv()

                    def join(offset):
                        where = pl.ds(pl.multiple_of(at * UNIT + offset, 32), 32)
                        total[where, :] = (
                            acc[pl.ds(offset, 32), :] + own_half[where, :].astype(F32)
                        ).astype(BF)

                    chunks(join)

                    @pl.when(index == 0)
                    def _():
                        x1(step).start()

                    for direction in range(2):

                        @pl.when((index == 1 + direction) & (ranks[direction] == 0))
                        def _():
                            z1(direction, step).start()

            return carry

        lax.fori_loop(0, 8, body, 0)

    def add(target, at, first, first_at, second, second_at):
        def body(index, carry):
            offset = index * 32
            left = first[pl.ds(pl.multiple_of(first_at * UNIT + offset, 32), 32), :]
            right = second[pl.ds(pl.multiple_of(second_at * UNIT + offset, 32), 32), :]
            target[pl.ds(pl.multiple_of(at * UNIT + offset, 32), 32), :] = (
                left.astype(F32) + right.astype(F32)
            ).astype(BF)
            return carry

        lax.fori_loop(0, UNIT // 32, body, 0)

    def x1(at):
        return remote(
            unit(total, 2 * at + 1 - column), unit(from_column, at), x1_send.at[at], x1_recv.at[at], side
        )

    def x2(direction, at, ahead=1):
        slot = direction * (wide // 2) + at
        return remote(
            unit(total, 4 * at + 2 * direction + column),
            unit(from_line, slot),
            x2_send.at[slot],
            x2_recv.at[slot],
            along(direction, ahead),
        )

    def z1(direction, at):
        slot = direction * deep + at
        return remote(
            unit(total, 2 * wide + 2 * at + direction),
            unit(from_deep, slot),
            z1_send.at[slot],
            z1_recv.at[slot],
            along(direction, 1),
        )

    def z2(direction, at):
        return remote(
            unit(total, 2 * wide + 2 * at + direction),
            unit(from_side, at // 2),
            z2_send.at[at // 2],
            z2_recv.at[at // 2],
            side,
        )

    def finished(at, send, recv, slot, device):
        return remote(unit(done, at), unit(done, at), send.at[slot], recv.at[slot], device)

    def ax(at, sent):
        parity = column if sent else 1 - column
        return finished(2 * at + parity, ax_send, ax_recv, at, side)

    def a2(direction, at):
        slot = direction * (wide // 2) + at
        return finished(
            4 * at + 2 * direction + column, a2_send, a2_recv, slot, along(direction, -1)
        )

    def a1(direction, at):
        slot = direction * deep + at
        return finished(
            2 * wide + 2 * at + direction, a1_send, a1_recv, slot, along(direction, -1)
        )

    def a4(direction, at):
        return finished(2 * wide + 2 * at + direction, a4_send, a4_recv, at // 2, side)

    def put(at):
        def send(target):
            pltpu.make_async_copy(unit(done, at), target, out_sem.at[at]).start()

        def by_rows(ref):
            return lambda index: send(ref.at[block(index // 2), block(index % 2, local)])

        def up(index):
            per = width // UNIT
            send(up_ref.at[block(index % per), block(index // per, local)])

        def part(which):
            return lambda index: send(qkv_ref.at[which, block(index), :])

        by_kind(at, (by_rows(down_ref), up, by_rows(out_ref), part(1), part(2), part(0)))

    def small_phase(step):
        @pl.when(step == 2)
        def _():
            small_out.wait_recv()
            small_own[0:8, :] = small_ref[0:8, :] + small_half[0:8, :]
            small_own[8:16, :] = small_ref[8:16, :] + small_half[16:24, :]
            small_side_copy().start()

        @pl.when(step == 4)
        def _():
            small_side_copy().wait_recv()
            small_line[place] = small_own[...] + small_side[...]
            for ahead in range(1, line):
                small_line_copy(ahead).start()

        @pl.when(step == 8)
        def _():
            for ahead in range(1, line):
                small_line_copy(ahead).wait_recv()
            summed = small_line[0]
            for at in range(1, line):
                summed = summed + small_line[at]
            totals_ref[...] = summed
            small_mirror_copy().start()

    def small_side_copy():
        return remote(small_own, small_side, s_send.at[2], s_recv.at[1], side)

    def small_line_copy(ahead):
        there = (place + ahead) % line
        return remote(
            small_line.at[place],
            small_line.at[place],
            s_send.at[2 + ahead],
            s_recv.at[1 + ahead],
            {"dp": there * 2 + column},
        )

    def small_mirror_copy():
        return remote(
            totals_ref, other_ref, s_send.at[2 + line], s_recv.at[1 + line], mirror
        )

    def step_body(step, carry):
        @pl.when(step == 3)
        def _():
            load(rest, "wait")

        make(step)

        at = step - LAG

        @pl.when((at >= 0) & (at < wide))
        def _():
            x1(at).wait_recv()
            add(total, 2 * at + column, total, 2 * at + column, from_column, at)
            for direction in range(2):

                @pl.when((at % 2 == direction) & (ranks[direction] == 0))
                def _():
                    x2(direction, at // 2).start()

        for direction in range(2):
            rank = ranks[direction]
            at = step - LAG * rank

            @pl.when((rank >= 1) & (at >= 0) & (at < deep))
            def _():
                where = 2 * wide + 2 * at + direction
                z1(direction, at).wait_recv()
                add(total, where, total, where, from_deep, direction * deep + at)

                @pl.when(rank < line - 1)
                def _():
                    z1(direction, at).start()

                @pl.when((rank == line - 1) & (at % 2 != column))
                def _():
                    z2(direction, at).start()

            twice = step - LAG - LAG * rank - direction

            @pl.when((rank >= 1) & (twice >= 0) & (twice < wide) & (twice % 2 == 0))
            def _():
                at = twice // 2
                where = 4 * at + 2 * direction + column
                x2(direction, at).wait_recv()
                slot = direction * (wide // 2) + at

                @pl.when(rank < line - 1)
                def _():
                    add(total, where, total, where, from_line, slot)
                    x2(direction, at).start()

                @pl.when(rank == line - 1)
                def _():
                    add(done, where, total, where, from_line, slot)
                    a2(direction, at).start()
                    ax(2 * at + direction, True).start()
                    put(where)

            at = step - LAG * line

            @pl.when((rank == line - 1) & (at >= 0) & (at < deep) & (at % 2 == column))
            def _():
                where = 2 * wide + 2 * at + direction
                z2(direction, at).wait_recv()
                add(done, where, total, where, from_side, at // 2)
                a1(direction, at).start()
                a4(direction, at).start()
                put(where)

            later = step - LAG * line - LAG

            @pl.when((rank == line - 1) & (later >= 0) & (later < deep) & (later % 2 != column))
            def _():
                a4(direction, later).wait_recv()
                a1(direction, later).start()
                put(2 * wide + 2 * later + direction)

            back = LAG * (line - 1 - rank)
            twice = step - LAG * line - back - direction

            @pl.when((rank < line - 1) & (twice >= 0) & (twice < wide) & (twice % 2 == 0))
            def _():
                at = twice // 2
                a2(direction, at).wait_recv()

                @pl.when(rank > 0)
                def _():
                    a2(direction, at).start()

                ax(2 * at + direction, True).start()
                put(4 * at + 2 * direction + column)

            for other in range(2):
                at = step - LAG * line - back - LAG * other

                @pl.when(
                    (rank < line - 1)
                    & (at >= 0)
                    & (at < deep)
                    & ((at + column) % 2 == other)
                )
                def _():
                    a1(direction, at).wait_recv()

                    @pl.when(rank > 0)
                    def _():
                        a1(direction, at).start()

                    put(2 * wide + 2 * at + direction)

            twice = step - LAG * line - back - direction - LAG

            @pl.when((twice >= 0) & (twice < wide) & (twice % 2 == 0))
            def _():
                at = twice + direction
                ax(at, False).wait_recv()
                put(2 * at + 1 - column)

        small_phase(step)
        return carry

    steps = wide - 1 + LAG * line + LAG * (line - 1) + LAG + 1
    load(soon, "wait")
    lax.fori_loop(-1, steps, step_body, 0)

    small_mirror_copy().wait()
    small_out.wait_send()
    small_side_copy().wait_send()
    for ahead in range(1, line):
        small_line_copy(ahead).wait_send()

    def drain(at, carry):
        pltpu.make_async_copy(unit(done, at), unit(done, at), out_sem.at[at]).wait()
        return carry

    lax.fori_loop(0, Exchange.UNITS, drain, 0)

    def drain_give(slot, carry):
        half_copy(slot, 0).wait_send()
        return carry

    lax.fori_loop(0, GIVE, drain_give, 0)

    def drain_wide(at, carry):
        x1(at).wait_send()
        ax(at, True).wait_send()
        return carry

    lax.fori_loop(0, wide, drain_wide, 0)
    for direction in range(2):
        rank = ranks[direction]

        def drain_line(at, carry):
            @pl.when(rank < line - 1)
            def _():
                x2(direction, at).wait_send()

            @pl.when(rank > 0)
            def _():
                a2(direction, at).wait_send()

            return carry

        lax.fori_loop(0, wide // 2, drain_line, 0)

        def drain_deep(at, carry):
            @pl.when(rank < line - 1)
            def _():
                z1(direction, at).wait_send()

            @pl.when(rank > 0)
            def _():
                a1(direction, at).wait_send()

            @pl.when((rank == line - 1) & (at % 2 != column))
            def _():
                z2(direction, at).wait_send()

            @pl.when((rank == line - 1) & (at % 2 == column))
            def _():
                a4(direction, at).wait_send()

            return carry

        lax.fori_loop(0, deep, drain_deep, 0)


def exchange(enc_operands, reg_operands, vec_grads, bias_grads, width, local, hidden):
    units, wide, deep = Exchange.UNITS, Exchange.WIDE, Exchange.DEEP
    images = len(enc_operands)

    def buffer(count, dtype=BF):
        return pltpu.VMEM((count * UNIT, local), dtype)

    def sems(*counts):
        return [pltpu.SemaphoreType.DMA((count,)) for count in counts]

    line = Exchange.LINE
    vspec = pl.BlockSpec(memory_space=pltpu.VMEM)
    return pl.pallas_call(
        functools.partial(exchange_kernel, images),
        out_shape=[
            jax.ShapeDtypeStruct((1, hidden, width), BF),
            jax.ShapeDtypeStruct((1, width, hidden), BF),
            jax.ShapeDtypeStruct((1, local, width), BF),
            jax.ShapeDtypeStruct((1, 3, width, local), BF),
            jax.ShapeDtypeStruct((16, width), F32),
            jax.ShapeDtypeStruct((16, width), F32),
        ],
        in_specs=[ANY] * (2 * images * len(OPERANDS)) + [vspec] * (2 * images),
        out_specs=[ANY] * 4 + [vspec, vspec],
        scratch_shapes=[pltpu.VMEM((images,) + one.shape, BF) for one in reg_operands[0]]
        + [
            buffer(1, F32),
            buffer(GIVE),
            buffer(units),
            buffer(units),
            buffer(wide),
            buffer(wide),
            buffer(2 * deep),
            buffer(deep // 2),
            buffer(units),
            pltpu.VMEM((24, width), F32),
            pltpu.VMEM((16, width), F32),
            pltpu.VMEM((24, width), F32),
            pltpu.VMEM((16, width), F32),
            pltpu.VMEM((line, 16, width), F32),
            pltpu.SemaphoreType.DMA((len(OPERANDS), images)),
        ]
        + sems(GIVE, units, wide, wide, wide, wide, 2 * deep, 2 * deep)
        + sems(deep // 2, deep // 2, wide, wide, wide, wide, 2 * deep, 2 * deep)
        + sems(deep // 2, deep // 2, units, 3 + line, 2 + line),
        compiler_params=params_of(collective_id=0, has_side_effects=True),
        cost_estimate=pl.CostEstimate(flops=0, bytes_accessed=200_000_000, transcendentals=0),
        name="gradient_exchange",
    )(*sum(enc_operands, []), *sum(reg_operands, []), *vec_grads, *bias_grads)


def place_code(positions, model_width):
    half_width = model_width // 2
    frequency = jnp.exp(
        jnp.arange(half_width, dtype=F32) * (-math.log(10000.0) / half_width)
    )
    angles = positions.astype(F32)[..., None] * frequency
    return jnp.sin(jnp.concatenate([angles, angles + 0.5 * math.pi], -1))


def shards(
    patches,
    order,
    cotangent,
    norm_gains,
    norm_biases,
    layer_scales,
    qkv_weight,
    out_weight,
    up_weight,
    up_bias,
    down_weight,
    down_bias,
    mask_token,
):
    images, places, width = patches.shape
    rows = places // 2
    hidden = up_weight.shape[2]
    local = width // 2
    encoder = lax.axis_index("stream") == 0

    def swapped(value):
        return lax.ppermute(value, "head", SWAP)

    own = (qkv_weight[0], out_weight[0], up_weight[0], down_weight[0])
    matrices = []
    for value in own:
        matrices += [value, swapped(value)]
    bias_pair = jnp.stack([up_bias[0], swapped(up_bias[0])]).astype(F32)[:, None, :]
    vec = jnp.concatenate(
        [
            norm_gains[0],
            norm_biases[0],
            layer_scales[0],
            down_bias[0][None],
            jnp.zeros((1, width), F32),
        ]
    )
    token = mask_token[None]
    cotangent = cotangent[0]
    order_column = order[:, :, None]
    order_row = order[:, None, :]

    kept_list = list(kept_shapes(rows, rows, width, hidden).values())
    row_shape = ((rows, width), BF)
    code_shape = ((images, places, width), F32)
    grad_list = list(grad_shapes(rows, rows, width, hidden).values())
    operand_list = operand_shapes(rows, places, width, hidden)

    kept, latents = [], []
    codes = None
    for image in range(images):

        def run_encoder():
            outs = encoder_forward(
                image, 0, patches, order_column, vec, up_bias=bias_pair, matrices=matrices, save=True
            )
            return tuple(outs) + ((nothing([code_shape])[0],) if image == 0 else ())

        def run_other():
            outs = nothing([row_shape] + kept_list)
            return tuple(outs) + ((place_code(order, width),) if image == 0 else ())

        outs = lax.cond(encoder, run_encoder, run_other)
        if image == 0:
            codes = outs[-1]
            outs = outs[:-1]
        latents.append(outs[0])
        kept.append(outs[1:])
    arrived = [lax.ppermute(one, "stream", [(0, 1)]) for one in latents]

    features, returned, reg_inputs, reg_vecs, reg_biases, reg_operands = [], [], [], [], [], []
    for image in range(images):

        def run_targets():
            rest = tuple(
                nothing(
                    [row_shape, row_shape, ((places, width), F32)]
                    + [((8, width), F32), ((2, 1, hidden), F32)]
                    + operand_list
                )
            )
            if image == 0:
                rest += tuple(
                    encoder_forward(
                        None, 1, patches, order_column, vec, bias_pair, matrices, save=False
                    )
                )
            return rest

        def run_regressor():
            outs = regressor_block(
                image, arrived[image], codes, token, cotangent, vec, bias_pair, matrices
            )
            if image == 0:
                outs = tuple(outs) + tuple(nothing([((images, rows, width), BF)]))
            return tuple(outs)

        outs = lax.cond(encoder, run_targets, run_regressor)
        if image == 0:
            targets = outs[-1]
            outs = outs[:-1]
        features.append(outs[0])
        returned.append(lax.ppermute(outs[1], "stream", [(1, 0)]))
        reg_inputs.append(outs[2])
        reg_vecs.append(outs[3])
        reg_biases.append(outs[4])
        reg_operands.append(list(outs[5:]))

    input_grads, vec_grads, bias_grads, enc_operands = [], [], [], []
    for image in range(images):

        def run_backward():
            return encoder_backward(
                image, returned[image], cotangent, order_row[:, :, :rows], kept[image], vec, matrices
            )

        def run_pass():
            return (reg_inputs[image], reg_vecs[image], reg_biases[image]) + tuple(
                nothing(grad_list)
            )

        outs = lax.cond(encoder, run_backward, run_pass)
        input_grads.append(outs[0])
        vec_grads.append(outs[1])
        bias_grads.append(outs[2])
        named = dict(zip(KEPT, kept[image]))
        named.update(zip(GRADS, outs[3:]))
        enc_operands.append([named[name] for name in OPERANDS])

    if lax.axis_size("dp") == 2 * Exchange.LINE and width == 768 and hidden == 1536:
        down, up, out, qkv, totals, other = exchange(
            enc_operands, reg_operands, vec_grads, bias_grads, width, local, hidden
        )
        down, up, out, qkv = (one.astype(F32) for one in (down, up, out, qkv))
        bias_total = totals[8 : 8 + hidden // width].reshape(hidden)
        token_grad = jnp.where(encoder, other[7], totals[7])
    else:
        parts = lax.cond(
            encoder,
            lambda: matrix_grads(enc_operands, 0),
            lambda: matrix_grads(reg_operands, rows),
        )
        vec_grad = sum(vec_grads)
        bias_grad = sum(bias_grads)[:, 0]

        def reduced(value):
            mine = value[0].astype(F32) + swapped(value[1]).astype(F32)
            part = lax.psum_scatter(mine.astype(BF), "dp", scatter_dimension=0, tiled=True)
            return lax.all_gather(part, "dp", axis=0, tiled=True).astype(F32)

        down, up, out, query, key, value = (reduced(one) for one in parts)
        qkv = jnp.stack([query, key, value])
        qkv, out, up, down = (one[None] for one in (qkv, out, up, down))
        bias_total = lax.psum(bias_grad[0] + swapped(bias_grad[1]), "dp")
        totals = lax.psum(vec_grad, ("dp", "head"))
        token_grad = lax.psum(jnp.where(encoder, 0.0, totals[7]), "stream")

    latent_out = jnp.where(encoder, jnp.stack(latents), jnp.stack(arrived))
    return (
        latent_out,
        jnp.where(encoder, targets, jnp.stack(features))[None],
        jnp.stack(input_grads)[None],
        totals[0:2][None],
        totals[2:4][None],
        totals[4:6][None],
        qkv,
        out,
        up,
        bias_total[None],
        down,
        totals[6][None],
        token_grad,
    )


def solution(mesh):
    in_specs = (
        P(("dp", "head"), None, None),
        P(("dp", "head"), None),
        P("stream", ("dp", "head"), None, None),
        P("stream", None, None),
        P("stream", None, None),
        P("stream", None, None),
        P("stream", None, None, "head"),
        P("stream", "head", None),
        P("stream", None, "head"),
        P("stream", "head"),
        P("stream", "head", None),
        P("stream", None),
        P(),
    )
    out_specs = (
        P(("dp", "head"), None, None),
        P("stream", ("dp", "head"), None, None),
        P("stream", ("dp", "head"), None, None),
        P("stream", None, None),
        P("stream", None, None),
        P("stream", None, None),
        P("stream", None, None, "head"),
        P("stream", "head", None),
        P("stream", None, "head"),
        P("stream", "head"),
        P("stream", "head", None),
        P("stream", None),
        P(),
    )
    return jax.shard_map(shards, mesh=mesh, in_specs=in_specs, out_specs=out_specs, check_vma=False)
```

```python
import functools
import math

import jax
import jax.numpy as jnp
from jax import lax
from jax.experimental import pallas as pl
from jax.experimental.pallas import tpu as pltpu
from jax.sharding import PartitionSpec as P

HEADS = 12
EPSILON = 1e-06
BF = jnp.bfloat16
F32 = jnp.float32
ROWS_AT_ONCE = 64
NN = ((1,), (0,))
NT = ((1,), (1,))
TN = ((0,), (0,))
SWAP = ((0, 1), (1, 0))
VMEM_BYTES = 60 * 1024 * 1024


def dot(left, right, dims=NN):
    return lax.dot_general(left, right, (dims, ((), ())), preferred_element_type=F32)


def row_loop(rows, body):
    def step(index, carry):
        body(pl.ds(pl.multiple_of(index * ROWS_AT_ONCE, ROWS_AT_ONCE), ROWS_AT_ONCE))
        return carry

    lax.fori_loop(0, rows // ROWS_AT_ONCE, step, 0)


def halves_loop(size, body):
    def step(half, carry):
        body(half, pl.ds(pl.multiple_of(half * size, size), size))
        return carry

    lax.fori_loop(0, 2, step, 0)


def standardize(values):
    centred = values - jnp.mean(values, -1, keepdims=True)
    inv_std = lax.rsqrt(jnp.mean(centred * centred, -1, keepdims=True) + EPSILON)
    return centred * inv_std, inv_std


def norm_into(source, target, gain, bias):
    def body(rows):
        scaled, _ = standardize(source[rows, :])
        target[rows, :] = (scaled * gain + bias).astype(BF)

    row_loop(source.shape[0], body)


def fold_rows(values):
    return jnp.sum(values.reshape(-1, 8, values.shape[-1]), 0)


def norm_back(grad, scaled, inv_std, gain):
    scaled_grad = grad * gain
    return inv_std * (
        scaled_grad
        - jnp.mean(scaled_grad, -1, keepdims=True)
        - scaled * jnp.mean(scaled_grad * scaled, -1, keepdims=True)
    )


class Weights:
    NAMES = ("qkv", "out", "up", "down")

    def __init__(self, sources, buffers, sems, names=NAMES, first_only=False):
        self.first_only = first_only
        self.buffers = dict(zip(self.NAMES, buffers))
        self.copies = {}
        for at, name in enumerate(self.NAMES):
            if name not in names:
                continue
            for half in range(2):
                self.copies[name, half] = pltpu.make_async_copy(
                    sources[2 * at + half], self.buffers[name].at[half], sems.at[at, half]
                )

    def each(self, names, method):
        def run():
            for name in names:
                for half in range(2):
                    getattr(self.copies[name, half], method)()

        if self.first_only:
            pl.when(pl.program_id(0) == 0)(run)
        else:
            run()

    def start(self, order):
        self.each(order, "start")

    def wait(self, name):
        self.each((name,), "wait")

    def __getitem__(self, name):
        return self.buffers[name]


class Held(dict):
    def __init__(self, buffers):
        super().__init__(buffers)
        self.coming, self.going = {}, {}

    def copy_in(self, names, sources, sems):
        for at, (name, source) in enumerate(zip(names, sources)):
            self.coming[name] = pltpu.make_async_copy(source, self[name], sems.at[at])
            self.coming[name].start()

    def copy_out(self, names, targets, sems):
        for at, (name, target) in enumerate(zip(names, targets)):
            self.going[name] = pltpu.make_async_copy(self[name], target, sems.at[at])

    def need(self, *names):
        for name in names:
            if name in self.coming:
                self.coming[name].wait()

    def ready(self, *names):
        for name in names:
            if name in self.going:
                self.going[name].start()

    def finish(self):
        for copy in self.going.values():
            copy.wait()


def weight_scratch(width, local, hidden):
    return [
        pltpu.VMEM((2, 3, width, local), BF),
        pltpu.VMEM((2, local, width), BF),
        pltpu.VMEM((2, width, hidden), BF),
        pltpu.VMEM((2, hidden, width), BF),
        pltpu.SemaphoreType.DMA((4, 2)),
    ]


def head_masks():
    lanes = lax.broadcasted_iota(jnp.int32, (1, 128), 1)
    low = (lanes < 64).astype(F32)
    return low.astype(BF), (1.0 - low).astype(BF)


def forward(rows_all, ctx, vec, up_bias, weights, keep, result_fn):
    width = rows_all.shape[1]
    row_count = rows_all.shape[0] - ctx
    normed, queries, keys, values, probs, mixed = (
        keep[name] for name in ("N", "Q", "K", "V", "P", "O")
    )
    norm_into(rows_all, normed, vec[0:1, :], vec[2:3, :])
    keep.ready("N")
    weights.wait("qkv")
    local = weights["qkv"].shape[3]

    def project(half, cols):
        queries[:, cols] = (dot(normed[ctx:, :], weights["qkv"][half, 0]) * 0.125).astype(BF)
        keys[:, cols] = dot(normed[...], weights["qkv"][half, 1]).astype(BF)
        values[:, cols] = dot(normed[...], weights["qkv"][half, 2]).astype(BF)

    halves_loop(local, project)
    keep.ready("Q", "K", "V")
    masks = head_masks()

    def attend(pair, carry):
        cols = pl.ds(pl.multiple_of(pair * 128, 128), 128)
        query, key = queries[:, cols], keys[:, cols]
        value_t = values[:, cols].T
        outs = []
        for at in range(2):
            scores = dot(key, query * masks[at], NT)
            weight = jnp.exp(scores - jnp.max(scores, 0, keepdims=True))
            prob = (weight * (1.0 / jnp.sum(weight, 0, keepdims=True))).astype(BF)
            probs[2 * pair + at] = prob
            outs.append(dot(value_t[64 * at : 64 * at + 64], prob))
        mixed[:, cols] = jnp.concatenate(outs, 0).T.astype(BF)
        return carry

    lax.fori_loop(0, HEADS // 2, attend, 0)
    keep.ready("P", "O")
    weights.wait("out")
    attended = dot(mixed[:, :local], weights["out"][0]) + dot(mixed[:, local:], weights["out"][1])
    hidden, normed_two = keep["H"], keep["M"]
    keep["A"][...] = attended.astype(keep["A"].dtype)
    hidden[...] = rows_all[ctx:, :] + vec[4:5, :] * attended
    norm_into(hidden, normed_two, vec[1:2, :], vec[3:4, :])
    keep.ready("A", "H", "M")
    weights.wait("up")
    weights.wait("down")
    fed = keep["F"]
    fed[...] = jnp.broadcast_to(vec[6:7, :], fed.shape)
    step = 512
    per_half = weights["up"].shape[2] // step

    def feed(index, carry):
        half, chunk = index // per_half, index % per_half
        cols = pl.ds(pl.multiple_of(chunk * step, step), step)
        pre = dot(normed_two[...], weights["up"][half, :, cols]) + up_bias[half, :, cols]
        phi = 0.5 + 0.5 * lax.erf(pre * math.sqrt(0.5))
        act = (pre * phi).astype(BF)
        if "G" in keep:
            keep["G"][half, :, cols] = act
            density = jnp.exp(pre * pre * -0.5) * (1.0 / math.sqrt(2.0 * math.pi))
            keep["D"][half, :, cols] = (phi + pre * density).astype(BF)
        fed[...] += dot(act, weights["down"][half, cols, :])
        return carry

    lax.fori_loop(0, 2 * per_half, feed, 0)

    keep.ready("G", "D", "F")

    def finish(rows):
        result_fn(rows, hidden[rows, :] + vec[5:6, :] * fed[rows, :])

    row_loop(row_count, finish)


def backward(rows_all, ctx, out_grad_fn, vec, weights, keep, grads, work, sums, up_bias_grad):
    width = rows_all.shape[1]
    row_count = rows_all.shape[0] - ctx
    local = width // 2
    grad_in = work["dH"]
    for at in range(8):
        sums[at] = jnp.zeros((8, width), F32)

    def enter(rows):
        grad = out_grad_fn(rows)
        grad_in[rows, :] = grad
        branch = vec[5:6, :] * grad
        sums[5] += fold_rows(grad * keep["F"][rows, :].astype(F32))
        sums[6] += fold_rows(branch)
        grads["dF"][rows, :] = branch.astype(BF)

    keep.need("F")
    row_loop(row_count, enter)
    grads.ready("dF")
    keep.need("D")
    weights.wait("down")
    weights.wait("up")
    grad_mid = work["dM"]
    grad_mid[...] = jnp.zeros_like(grad_mid)
    step = 512
    per_half = weights["up"].shape[2] // step

    def feed(index, carry):
        half, chunk = index // per_half, index % per_half
        cols = pl.ds(pl.multiple_of(chunk * step, step), step)
        act_grad = dot(grads["dF"][...], weights["down"][half, cols, :], NT)
        pre_grad = act_grad * keep["D"][half, :, cols].astype(F32)
        up_bias_grad[half, :, cols] = jnp.sum(pre_grad, 0, keepdims=True)
        pre_grad = pre_grad.astype(BF)
        grads["dU"][half, :, cols] = pre_grad
        grad_mid[...] += dot(pre_grad, weights["up"][half, :, cols], NT)
        return carry

    lax.fori_loop(0, 2 * per_half, feed, 0)

    def middle(rows):
        scaled, inv_std = standardize(keep["H"][rows, :])
        grad = grad_mid[rows, :]
        sums[1] += fold_rows(grad * scaled)
        sums[3] += fold_rows(grad)
        hidden_grad = grad_in[rows, :] + norm_back(grad, scaled, inv_std, vec[1:2, :])
        grad_in[rows, :] = hidden_grad
        sums[4] += fold_rows(hidden_grad * keep["A"][rows, :].astype(F32))
        grads["dA"][rows, :] = (vec[4:5, :] * hidden_grad).astype(BF)

    grads.ready("dU")
    keep.need("H", "A")
    row_loop(row_count, middle)
    grads.ready("dA")
    weights.wait("out")
    mix_grad = work["dO"]

    def unmix(half, cols):
        mix_grad[:, cols] = dot(grads["dA"][...], weights["out"][half], NT).astype(BF)

    halves_loop(local, unmix)
    masks = head_masks()

    def attend(pair, carry):
        cols = pl.ds(pl.multiple_of(pair * 128, 128), 128)
        query, key, value = keep["Q"][:, cols], keep["K"][:, cols], keep["V"][:, cols]
        out_grad = mix_grad[:, cols]
        key_t = key.T
        value_grad = key_grad = None
        query_grads = []
        for at in range(2):
            prob = keep["P"][2 * pair + at]
            own_grad = out_grad * masks[at]
            part = dot(prob, own_grad)
            value_grad = part if value_grad is None else value_grad + part
            prob_grad = dot(value, own_grad, NT)
            wide = prob.astype(F32)
            product = wide * prob_grad
            score_grad = (product - wide * jnp.sum(product, 0, keepdims=True)).astype(BF)
            part = dot(score_grad, query * masks[at])
            key_grad = part if key_grad is None else key_grad + part
            query_grads.append(dot(key_t[64 * at : 64 * at + 64], score_grad))
        grads["dV"][:, cols] = value_grad.astype(BF)
        grads["dK"][:, cols] = key_grad.astype(BF)
        grads["dQ"][:, cols] = (jnp.concatenate(query_grads, 0).T * 0.125).astype(BF)
        return carry

    keep.need("P", "Q", "K", "V")
    lax.fori_loop(0, HEADS // 2, attend, 0)
    grads.ready("dQ", "dK", "dV")
    weights.wait("qkv")
    grad_all = work["dN"]
    qkv = weights["qkv"]
    grad_all[...] = jnp.zeros_like(grad_all)

    def unproject(half, cols):
        grad_all[...] += dot(grads["dK"][:, cols], qkv[half, 1], NT) + dot(
            grads["dV"][:, cols], qkv[half, 2], NT
        )
        grad_all[ctx:, :] += dot(grads["dQ"][:, cols], qkv[half, 0], NT)

    halves_loop(local, unproject)

    def leave(rows):
        scaled, inv_std = standardize(rows_all[rows, :].astype(F32))
        grad = grad_all[rows, :]
        sums[0] += fold_rows(grad * scaled)
        sums[2] += fold_rows(grad)
        grad_all[rows, :] = norm_back(grad, scaled, inv_std, vec[0:1, :])

    keep.need("X")
    row_loop(rows_all.shape[0], leave)


def write_sums(sums, target):
    for at in range(8):
        target[at : at + 1, :] = jnp.sum(sums[at], 0, keepdims=True)


def pick_rows(order_column, patches):
    places = lax.broadcasted_iota(jnp.int32, (order_column.shape[0], patches.shape[0]), 1)
    return dot((places == order_column).astype(F32).astype(BF), patches)


READ_BACK = ("F", "D", "H", "A", "P", "Q", "K", "V", "X")
KEPT = ("X", "N", "Q", "K", "V", "P", "O", "A", "H", "M", "G", "D", "F")
GRADS = ("dF", "dU", "dA", "dQ", "dK", "dV")
OPERANDS = ("dF", "G", "dU", "M", "dA", "O", "dQ", "dK", "dV", "N")


def kept_shapes(rows, keys, width, hidden):
    return {
        "X": ((rows, width), BF),
        "N": ((keys, width), BF),
        "Q": ((rows, width), BF),
        "K": ((keys, width), BF),
        "V": ((keys, width), BF),
        "P": ((HEADS, keys, rows), BF),
        "O": ((rows, width), BF),
        "A": ((rows, width), BF),
        "H": ((rows, width), F32),
        "M": ((rows, width), BF),
        "G": ((2, rows, hidden), BF),
        "D": ((2, rows, hidden), BF),
        "F": ((rows, width), F32),
    }


def grad_shapes(rows, keys, width, hidden):
    return {
        "dF": ((rows, width), BF),
        "dU": ((2, rows, hidden), BF),
        "dA": ((rows, width), BF),
        "dQ": ((rows, width), BF),
        "dK": ((keys, width), BF),
        "dV": ((keys, width), BF),
    }


def vmem(shape_type):
    return pltpu.VMEM(*shape_type)


ONCE = pl.Buffered(1)


def whole(shape):
    return pl.BlockSpec(tuple(shape), lambda _: (0,) * len(shape), pipeline_mode=ONCE)


def image_of(array, image):
    return pl.BlockSpec(
        (None,) + array.shape[1:],
        lambda _: (image,) + (0,) * (array.ndim - 1),
        pipeline_mode=ONCE,
    )


ANY = pl.BlockSpec(memory_space=pl.ANY)


def shape_of(shape_type):
    return jax.ShapeDtypeStruct(*shape_type)


def nothing(shapes):
    return pl.pallas_call(
        lambda *refs: None,
        out_shape=[shape_of(s) for s in shapes],
        out_specs=[ANY] * len(shapes),
        name="no_values",
    )()


def params_of(**extra):
    return pltpu.CompilerParams(vmem_limit_bytes=VMEM_BYTES, **extra)


def block_cost(rows, keys, width, hidden, passes):
    flops = 2 * rows * width * (2 * width + 4 * hidden) + 4 * keys * width * width
    flops += 4 * rows * keys * width
    return pl.CostEstimate(flops=passes * flops, bytes_accessed=24_000_000, transcendentals=0)


def encoder_forward(image, which, patches, order_column, vec, up_bias, matrices, save):
    images, places, width = patches.shape
    rows = places // 2
    hidden = matrices[4].shape[1]
    local = width // 2
    shapes = kept_shapes(rows, rows, width, hidden)
    names = [n for n in KEPT]
    own = names if save else [n for n in names if n not in ("X", "G", "D")]

    def kernel(patch_ref, order_ref, vec_ref, bias_ref, *refs):
        sources, refs = refs[:8], refs[8:]
        result, refs = refs[0], refs[1:]
        if save:
            targets, refs = refs[: len(names)], refs[len(names) :]
        keep = Held(zip(own, refs))
        refs = refs[len(own) :]
        rows_ref, refs = refs[0], refs[1:]
        weights = Weights(sources, refs[:4], refs[4], first_only=not save)
        weights.start(("qkv", "out", "up", "down"))
        rows_ref[...] = pick_rows(order_ref[...], patch_ref[...])
        if save:
            keep.copy_out(names, targets, refs[5])
            keep["X"][...] = rows_ref[...].astype(BF)
            keep.ready("X")

        def result_fn(rows_at, value):
            result[rows_at, :] = value.astype(BF)

        forward(rows_ref, 0, vec_ref, bias_ref, weights, keep, result_fn)
        keep.finish()

    out_shapes = [((rows, width), BF)] + ([shapes[n] for n in names] if save else [])
    out_specs = [whole(out_shapes[0][0])] + [ANY] * (len(out_shapes) - 1)
    patch_spec = image_of(patches, image)
    scratch = [vmem(shapes[n]) for n in own] + [pltpu.VMEM((rows, width), F32)]
    scratch += weight_scratch(width, local, hidden) + [pltpu.SemaphoreType.DMA((len(names),))]
    order_spec = pl.BlockSpec(
        (None, rows, 1), lambda _: (image, which, 0), pipeline_mode=ONCE
    )
    if not save:
        out_shapes = [((images, rows, width), BF)]
        out_specs = [pl.BlockSpec((None, rows, width), lambda i: (i, 0, 0))]
        patch_spec = pl.BlockSpec((None, places, width), lambda i: (i, 0, 0))
        order_spec = pl.BlockSpec((None, rows, 1), lambda i: (i, which, 0))
    return pl.pallas_call(
        kernel,
        grid=(1 if save else images,),
        out_shape=[shape_of(s) for s in out_shapes],
        in_specs=[patch_spec, order_spec, whole(vec.shape), whole(up_bias.shape)] + [ANY] * 8,
        out_specs=out_specs,
        scratch_shapes=scratch,
        compiler_params=params_of(),
        cost_estimate=block_cost(rows, rows, width, hidden, 1),
        name="encoder_forward" if save else "encoder_targets",
    )(patches, order_column, vec, up_bias, *matrices)


def encoder_backward(image, latent_grad, cotangent, order_row, kept, vec, matrices):
    rows, width = latent_grad.shape
    hidden = matrices[4].shape[1]
    local = width // 2
    shapes = grad_shapes(rows, rows, width, hidden)
    names = list(GRADS)
    kept = [dict(zip(KEPT, kept))[name] for name in READ_BACK]

    def kernel(back_ref, cot_ref, order_ref, vec_ref, *refs):
        sources, refs = refs[:8], refs[8:]
        saved, refs = refs[: len(READ_BACK)], refs[len(READ_BACK) :]
        input_grad, vec_grad, bias_grad, refs = refs[0], refs[1], refs[2], refs[3:]
        targets, refs = refs[: len(names)], refs[len(names) :]
        keep = Held(zip(READ_BACK, refs))
        grads = Held(zip(names, refs[len(READ_BACK) :]))
        refs = refs[len(READ_BACK) + len(names) :]
        d_hidden, d_mid, d_out, d_norm, sums = refs[:5]
        weights = Weights(sources, refs[5:9], refs[9])
        keep.copy_in(READ_BACK[:2], saved, refs[11])
        weights.start(("down", "up"))
        keep.copy_in(READ_BACK[2:], saved[2:], refs[12])
        weights.start(("out", "qkv"))
        grads.copy_out(names, targets, refs[13])
        work = {"dH": d_hidden, "dM": d_mid, "dO": d_out, "dN": d_norm}

        def out_grad_fn(rows_at):
            return cot_ref[rows_at, :].astype(F32) + back_ref[rows_at, :].astype(F32)

        backward(
            keep["X"], 0, out_grad_fn, vec_ref, weights, keep, grads, work, sums, bias_grad
        )
        write_sums(sums, vec_grad)

        def join(rows_at):
            total = d_norm[rows_at, :] + d_hidden[rows_at, :]
            high = total.astype(BF)
            d_out[rows_at, :] = high
            grads_low[rows_at, :] = (total - high.astype(F32)).astype(BF)

        grads_low = refs[10]
        row_loop(rows, join)

        def place(index, carry):
            first = pl.multiple_of(index * 128, 128)
            places = lax.broadcasted_iota(jnp.int32, (128, rows), 0) + first
            hot = (places == order_ref[...]).astype(F32).astype(BF)
            input_grad[pl.ds(first, 128), :] = dot(hot, d_out[...]) + dot(hot, grads_low[...])
            return carry

        lax.fori_loop(0, input_grad.shape[0] // 128, place, 0)
        grads.finish()

    out_shapes = [((2 * rows, width), F32), ((8, width), F32), ((2, 1, hidden), F32)]
    out_shapes += [shapes[n] for n in names]
    forms = kept_shapes(rows, rows, width, hidden)
    scratch = [vmem(forms[n]) for n in READ_BACK] + [vmem(shapes[n]) for n in names]
    scratch += [
        pltpu.VMEM((rows, width), F32),
        pltpu.VMEM((rows, width), F32),
        pltpu.VMEM((rows, width), BF),
        pltpu.VMEM((rows, width), F32),
        pltpu.VMEM((8, 8, width), F32),
    ]
    scratch += weight_scratch(width, local, hidden) + [pltpu.VMEM((rows, width), BF)]
    scratch += [
        pltpu.SemaphoreType.DMA((2,)),
        pltpu.SemaphoreType.DMA((len(READ_BACK) - 2,)),
        pltpu.SemaphoreType.DMA((len(names),)),
    ]
    order_spec = pl.BlockSpec((None, 1, rows), lambda _: (image, 0, 0), pipeline_mode=ONCE)
    outs = pl.pallas_call(
        kernel,
        grid=(1,),
        out_shape=[shape_of(s) for s in out_shapes],
        in_specs=[whole(latent_grad.shape), image_of(cotangent, image), order_spec, whole(vec.shape)]
        + [ANY] * (8 + len(kept)),
        out_specs=[whole(s[0]) for s in out_shapes[:3]] + [ANY] * len(names),
        scratch_shapes=scratch,
        compiler_params=params_of(),
        cost_estimate=block_cost(rows, rows, width, hidden, 1),
        name="encoder_backward",
    )(latent_grad, cotangent, order_row, vec, *matrices, *kept)
    return tuple(outs)


def operand_shapes(rows, keys, width, hidden):
    shapes = dict(grad_shapes(rows, keys, width, hidden))
    shapes.update(kept_shapes(rows, keys, width, hidden))
    return [shapes[n] for n in OPERANDS]


def regressor_block(image, latent, codes, token, cotangent, vec, up_bias, matrices):
    ctx, width = latent.shape
    rows = codes.shape[1] - ctx
    keys = rows + ctx
    hidden = matrices[4].shape[1]
    local = width // 2
    kept = kept_shapes(rows, keys, width, hidden)
    shapes = grad_shapes(rows, keys, width, hidden)
    own = [n for n in KEPT if n != "X" and n not in OPERANDS]

    def kernel(latent_ref, code_ref, token_ref, cot_ref, vec_ref, bias_ref, *refs):
        sources, refs = refs[:8], refs[8:]
        result, back, input_grad, vec_grad, bias_grad = refs[:5]
        refs = refs[5:]
        targets, refs = refs[: len(OPERANDS)], refs[len(OPERANDS) :]
        held = OPERANDS + tuple(own)
        keep = Held(zip(held, refs))
        refs = refs[len(held) :]
        keep.copy_out(OPERANDS, targets, refs[10])
        rows_ref, d_hidden, d_mid, d_out, sums = refs[:5]
        weights = Weights(sources, refs[5:9], refs[9])
        weights.start(("qkv", "out", "up", "down"))

        def fill(rows_at):
            rows_ref[rows_at, :] = latent_ref[rows_at, :].astype(F32) + code_ref[rows_at, :]
            lower = pl.ds(rows_at.start + ctx, ROWS_AT_ONCE)
            rows_ref[lower, :] = token_ref[...] + code_ref[lower, :]

        row_loop(ctx, fill)

        def result_fn(rows_at, value):
            result[rows_at, :] = value.astype(BF)

        forward(rows_ref, ctx, vec_ref, bias_ref, weights, keep, result_fn)
        work = {"dH": d_hidden, "dM": d_mid, "dO": d_out, "dN": input_grad}

        def out_grad_fn(rows_at):
            return cot_ref[rows_at, :].astype(F32)

        weights.wait = lambda name: None
        backward(
            rows_ref, ctx, out_grad_fn, vec_ref, weights, keep, keep, work, sums, bias_grad
        )

        def leave(rows_at):
            back[rows_at, :] = input_grad[rows_at, :].astype(BF)
            lower = pl.ds(rows_at.start + ctx, ROWS_AT_ONCE)
            total = input_grad[lower, :] + d_hidden[rows_at, :]
            input_grad[lower, :] = total
            sums[7] += fold_rows(total)

        row_loop(rows, leave)
        write_sums(sums, vec_grad)
        keep.finish()

    out_shapes = [
        ((rows, width), BF),
        ((ctx, width), BF),
        ((keys, width), F32),
        ((8, width), F32),
        ((2, 1, hidden), F32),
    ] + operand_shapes(rows, keys, width, hidden)
    scratch = [vmem(one) for one in operand_shapes(rows, keys, width, hidden)]
    scratch += [vmem(kept[n]) for n in own]
    scratch += [
        pltpu.VMEM((keys, width), F32),
        pltpu.VMEM((rows, width), F32),
        pltpu.VMEM((rows, width), F32),
        pltpu.VMEM((rows, width), BF),
        pltpu.VMEM((8, 8, width), F32),
    ]
    scratch += weight_scratch(width, local, hidden)
    scratch += [pltpu.SemaphoreType.DMA((len(OPERANDS),))]
    outs = pl.pallas_call(
        kernel,
        grid=(1,),
        out_shape=[shape_of(s) for s in out_shapes],
        in_specs=[
            whole(latent.shape),
            image_of(codes, image),
            whole(token.shape),
            image_of(cotangent, image),
            whole(vec.shape),
            whole(up_bias.shape),
        ]
        + [ANY] * 8,
        out_specs=[whole(s[0]) for s in out_shapes[:5]] + [ANY] * len(OPERANDS),
        scratch_shapes=scratch,
        compiler_params=params_of(),
        cost_estimate=block_cost(rows, keys, width, hidden, 2),
        name="regressor_block",
    )(latent, codes, token, cotangent, vec, up_bias, *matrices)
    return outs


def weight_grad(name, lefts, rights, first_rows, split_left, step, halves):
    images = len(lefts)
    wide = (lefts if split_left else rights)[0]
    other = (rights if split_left else lefts)[0]
    if wide.ndim == 3:
        blocks = (wide.shape[0], wide.shape[2] // step)
        wide_spec = pl.BlockSpec((None, wide.shape[1], step), lambda h, c: (h, 0, c))
        width = wide.shape[2]
    else:
        blocks = (halves, wide.shape[1] // halves // step)
        wide_spec = pl.BlockSpec(
            (wide.shape[0], step), lambda h, c: (0, h * blocks[1] + c)
        )
        width = wide.shape[1] // halves
    other_spec = pl.BlockSpec(other.shape, lambda h, c: (0, 0))
    if split_left:
        out = ((halves, width, other.shape[1]), BF)
        out_spec = pl.BlockSpec((None, step, other.shape[1]), lambda h, c: (h, c, 0))
    else:
        out = ((halves, other.shape[1], width), BF)
        out_spec = pl.BlockSpec((None, other.shape[1], step), lambda h, c: (h, 0, c))

    def kernel(*refs):
        total = None
        for at in range(images):
            left, right = refs[at][...], refs[images + at][...]
            if first_rows:
                left = left[first_rows:]
            part = dot(left, right, TN)
            total = part if total is None else total + part
        refs[-1][...] = total.astype(BF)

    specs = ([wide_spec] * images + [other_spec] * images) if split_left else (
        [other_spec] * images + [wide_spec] * images
    )
    rows = rights[0].shape[-2]
    return pl.pallas_call(
        kernel,
        grid=blocks,
        out_shape=shape_of(out),
        in_specs=specs,
        out_specs=out_spec,
        compiler_params=params_of(),
        cost_estimate=pl.CostEstimate(
            flops=2 * images * rows * halves * width * other.shape[1],
            bytes_accessed=8_000_000,
            transcendentals=0,
        ),
        name=name,
    )(*lefts, *rights)


def matrix_grads(operands, ctx):
    named = [dict(zip(OPERANDS, one)) for one in operands]

    def column(name):
        return [one[name] for one in named]

    down = weight_grad("down_grad", column("G"), column("dF"), 0, True, 512, 2)
    up = weight_grad("up_grad", column("M"), column("dU"), 0, False, 512, 2)
    out = weight_grad("out_grad", column("O"), column("dA"), 0, True, 384, 2)
    query = weight_grad("query_grad", column("N"), column("dQ"), ctx, False, 384, 2)
    key = weight_grad("key_grad", column("N"), column("dK"), 0, False, 384, 2)
    value = weight_grad("value_grad", column("N"), column("dV"), 0, False, 384, 2)
    return down, up, out, query, key, value


UNIT = 128
LAG = 2
GIVE = 16


class Exchange:
    LINE = 4
    WIDE = 20
    DEEP = 16
    UNITS = 2 * WIDE + 2 * DEEP


def exchange_kernel(images, *refs):
    count = len(OPERANDS)
    sources = []
    for _ in range(2):
        sources.append([dict(zip(OPERANDS, refs[at * count :])) for at in range(images)])
        refs = refs[images * count :]
    vec_refs, bias_refs, refs = refs[:images], refs[images : 2 * images], refs[2 * images :]
    down_ref, up_ref, out_ref, qkv_ref = (ref.at[0] for ref in refs[:4])
    totals_ref, other_ref = refs[4:6]
    refs = refs[6:]
    held = dict(zip(OPERANDS, refs[:count]))
    acc, gives = refs[count : count + 2]
    refs = refs[count + 2 :]
    total, own_half, from_column, from_line, from_deep, from_side, done = refs[:7]
    small_ref, small_own, small_half, small_side, small_line = refs[7:12]
    (load_sem, half_send, half_recv, x1_send, x1_recv, x2_send, x2_recv, z1_send, z1_recv) = refs[12:21]
    (z2_send, z2_recv, ax_send, ax_recv, a2_send, a2_recv, a1_send, a1_recv) = refs[21:29]
    (a4_send, a4_recv, out_sem, s_send, s_recv) = refs[29:34]
    line, wide, deep = Exchange.LINE, Exchange.WIDE, Exchange.DEEP
    dp = lax.axis_index("dp")
    place, column = dp // 2, dp % 2
    side = {"dp": place * 2 + 1 - column}
    partner = {"head": 1 - lax.axis_index("head")}
    mirror = {"stream": 1 - lax.axis_index("stream")}

    def along(direction, ahead):
        return {"dp": dp + 2 * (2 * direction - 1) * ahead}

    ranks = (line - 1 - place, place)

    stream = lax.axis_index("stream")
    rows, width = held["M"].shape[1:]
    hidden = held["G"].shape[3]
    local = width // 2

    def load(names, method):
        for which in range(2):

            @pl.when(stream == which)
            def _():
                for image, source in enumerate(sources[which]):
                    for name in names:
                        at = OPERANDS.index(name)
                        target = held[name].at[image]
                        if source[name].shape != target.shape:
                            target = target.at[pl.ds(0, source[name].shape[0]), :]
                        copy = pltpu.make_async_copy(source[name], target, load_sem.at[at, image])
                        getattr(copy, method)()

    soon = ("G", "dF", "M", "dU")
    rest = tuple(name for name in OPERANDS if name not in soon)
    load(soon[:2], "start")
    load(soon[2:], "start")
    load(rest, "start")

    def unit(buffer, at):
        return buffer.at[pl.ds(pl.multiple_of(at * UNIT, UNIT), UNIT), :]

    def remote(source, target, send, recv, device):
        return pltpu.make_async_remote_copy(
            src_ref=source,
            dst_ref=target,
            send_sem=send,
            recv_sem=recv,
            device_id=device,
            device_id_type=pl.DeviceIdType.MESH,
        )

    barrier = pltpu.get_barrier_semaphore()

    def greet(device):
        pl.semaphore_signal(barrier, inc=1, device_id=device, device_id_type=pl.DeviceIdType.MESH)

    for device in (partner, side, mirror):
        greet(device)
    for ahead in range(1, line):
        greet({"dp": ((place + ahead) % line) * 2 + column})
    pl.semaphore_wait(barrier, 2 + line)

    small_ref[...] = jnp.zeros_like(small_ref)
    small_ref[0:8, :] = sum(ref[...] for ref in vec_refs)
    for half in range(2):
        for at in range(hidden // width):
            row = 8 * (half + 1) + at
            cols = slice(at * width, (at + 1) * width)
            small_ref[row : row + 1, :] = sum(ref[half, :, cols] for ref in bias_refs)
    small_out = remote(small_ref, small_half, s_send.at[1], s_recv.at[0], partner)
    small_out.start()

    counts = (
        2 * hidden // UNIT,
        2 * hidden // UNIT,
        2 * local // UNIT,
        width // UNIT,
        width // UNIT,
        width // UNIT,
    )
    bounds = [sum(counts[:at]) for at in range(len(counts) + 1)]

    def by_kind(at, bodies):
        for kind, one in enumerate(bodies):

            @pl.when((at >= bounds[kind]) & (at < bounds[kind + 1]))
            def _():
                one(at - bounds[kind])

    def block(at, size=UNIT):
        return pl.ds(pl.multiple_of(at * size, size), size)

    def summed(one):
        parts = [one(image) for image in range(images)]
        return functools.reduce(jnp.add, parts)

    def product(at, half):
        cols = pl.ds(pl.multiple_of(half * local, local), local)
        query_rows = pl.ds(pl.multiple_of(stream * rows, rows), rows)

        def down(index):
            acc[...] = summed(
                lambda i: dot(
                    held["G"][i, half, :, block(index // 2)],
                    held["dF"][i, :, block(index % 2, local)],
                    TN,
                )
            )

        def up(index):
            per = width // UNIT
            acc[...] = summed(
                lambda i: dot(
                    held["M"][i, :, block(index % per)],
                    held["dU"][i, half, :, block(index // per, local)],
                    TN,
                )
            )

        def out(index):
            acc[...] = summed(
                lambda i: dot(
                    held["O"][i, :, block(half * (local // UNIT) + index // 2)],
                    held["dA"][i, :, block(index % 2, local)],
                    TN,
                )
            )

        def over_keys(name):
            def part(index, keys):
                return summed(
                    lambda i: dot(held["N"][i, keys, block(index)], held[name][i, keys, cols], TN)
                )

            def run(index):
                acc[...] = part(index, slice(0, rows))

                @pl.when(stream == 1)
                def _():
                    acc[...] += part(index, slice(rows, None))

            return run

        def query(index):
            acc[...] = summed(
                lambda i: dot(held["N"][i, query_rows, block(index)], held["dQ"][i, :, cols], TN)
            )

        by_kind(at, (down, up, out, over_keys("dK"), over_keys("dV"), query))

    def chunks(body):
        def step(index, carry):
            body(pl.multiple_of(index * 32, 32))
            return carry

        lax.fori_loop(0, UNIT // 32, step, 0)

    def half_copy(slot, at):
        return remote(
            unit(gives, slot), unit(own_half, at), half_send.at[slot], half_recv.at[at], partner
        )

    def unit_of(step, index):
        second = index * (3 - index) // 2
        own = index // 2
        wide_unit = 2 * step + 1 - column + own * (2 * column - 1)
        return wide_unit + second * (2 * wide + 2 * step + own - wide_unit), second

    def make(now):
        def body(turn, carry):
            index, mine = turn % 4, turn // 4
            step = now + 1 - mine
            at, second = unit_of(step, index)

            @pl.when((now == -1) & (turn == 1))
            def _():
                load(soon[2:], "wait")

            @pl.when((step >= 0) & (step < wide) & (second * step < deep))
            def _():
                product(at, 1 - mine)

                @pl.when(mine == 0)
                def _():
                    slot = (4 * step + index) % GIVE

                    @pl.when(4 * step >= GIVE)
                    def _():
                        half_copy(slot, at).wait_send()

                    def convert(offset):
                        gives[pl.ds(pl.multiple_of(slot * UNIT + offset, 32), 32), :] = acc[
                            pl.ds(offset, 32), :
                        ].astype(BF)

                    chunks(convert)
                    half_copy(slot, at).start()

                @pl.when(mine == 1)
                def _():
                    half_copy(0, at).wait_recv()

                    def join(offset):
                        where = pl.ds(pl.multiple_of(at * UNIT + offset, 32), 32)
                        total[where, :] = (
                            acc[pl.ds(offset, 32), :] + own_half[where, :].astype(F32)
                        ).astype(BF)

                    chunks(join)

                    @pl.when(index == 0)
                    def _():
                        x1(step).start()

                    for direction in range(2):

                        @pl.when((index == 1 + direction) & (ranks[direction] == 0))
                        def _():
                            z1(direction, step).start()

            return carry

        lax.fori_loop(0, 8, body, 0)

    def add(target, at, first, first_at, second, second_at):
        def body(index, carry):
            offset = index * 32
            left = first[pl.ds(pl.multiple_of(first_at * UNIT + offset, 32), 32), :]
            right = second[pl.ds(pl.multiple_of(second_at * UNIT + offset, 32), 32), :]
            target[pl.ds(pl.multiple_of(at * UNIT + offset, 32), 32), :] = (
                left.astype(F32) + right.astype(F32)
            ).astype(BF)
            return carry

        lax.fori_loop(0, UNIT // 32, body, 0)

    def x1(at):
        return remote(
            unit(total, 2 * at + 1 - column), unit(from_column, at), x1_send.at[at], x1_recv.at[at], side
        )

    def x2(direction, at, ahead=1):
        slot = direction * (wide // 2) + at
        return remote(
            unit(total, 4 * at + 2 * direction + column),
            unit(from_line, slot),
            x2_send.at[slot],
            x2_recv.at[slot],
            along(direction, ahead),
        )

    def z1(direction, at):
        slot = direction * deep + at
        return remote(
            unit(total, 2 * wide + 2 * at + direction),
            unit(from_deep, slot),
            z1_send.at[slot],
            z1_recv.at[slot],
            along(direction, 1),
        )

    def z2(direction, at):
        return remote(
            unit(total, 2 * wide + 2 * at + direction),
            unit(from_side, at // 2),
            z2_send.at[at // 2],
            z2_recv.at[at // 2],
            side,
        )

    def finished(at, send, recv, slot, device):
        return remote(unit(done, at), unit(done, at), send.at[slot], recv.at[slot], device)

    def ax(at, sent):
        parity = column if sent else 1 - column
        return finished(2 * at + parity, ax_send, ax_recv, at, side)

    def a2(direction, at):
        slot = direction * (wide // 2) + at
        return finished(
            4 * at + 2 * direction + column, a2_send, a2_recv, slot, along(direction, -1)
        )

    def a1(direction, at):
        slot = direction * deep + at
        return finished(
            2 * wide + 2 * at + direction, a1_send, a1_recv, slot, along(direction, -1)
        )

    def a4(direction, at):
        return finished(2 * wide + 2 * at + direction, a4_send, a4_recv, at // 2, side)

    def put(at):
        def send(target):
            pltpu.make_async_copy(unit(done, at), target, out_sem.at[at]).start()

        def by_rows(ref):
            return lambda index: send(ref.at[block(index // 2), block(index % 2, local)])

        def up(index):
            per = width // UNIT
            send(up_ref.at[block(index % per), block(index // per, local)])

        def part(which):
            return lambda index: send(qkv_ref.at[which, block(index), :])

        by_kind(at, (by_rows(down_ref), up, by_rows(out_ref), part(1), part(2), part(0)))

    def small_phase(step):
        @pl.when(step == 2)
        def _():
            small_out.wait_recv()
            small_own[0:8, :] = small_ref[0:8, :] + small_half[0:8, :]
            small_own[8:16, :] = small_ref[8:16, :] + small_half[16:24, :]
            small_side_copy().start()

        @pl.when(step == 4)
        def _():
            small_side_copy().wait_recv()
            small_line[place] = small_own[...] + small_side[...]
            for ahead in range(1, line):
                small_line_copy(ahead).start()

        @pl.when(step == 8)
        def _():
            for ahead in range(1, line):
                small_line_copy(ahead).wait_recv()
            summed = small_line[0]
            for at in range(1, line):
                summed = summed + small_line[at]
            totals_ref[...] = summed
            small_mirror_copy().start()

    def small_side_copy():
        return remote(small_own, small_side, s_send.at[2], s_recv.at[1], side)

    def small_line_copy(ahead):
        there = (place + ahead) % line
        return remote(
            small_line.at[place],
            small_line.at[place],
            s_send.at[2 + ahead],
            s_recv.at[1 + ahead],
            {"dp": there * 2 + column},
        )

    def small_mirror_copy():
        return remote(
            totals_ref, other_ref, s_send.at[2 + line], s_recv.at[1 + line], mirror
        )

    def step_body(step, carry):
        @pl.when(step == 3)
        def _():
            load(rest, "wait")

        make(step)

        at = step - LAG

        @pl.when((at >= 0) & (at < wide))
        def _():
            x1(at).wait_recv()
            add(total, 2 * at + column, total, 2 * at + column, from_column, at)
            for direction in range(2):

                @pl.when((at % 2 == direction) & (ranks[direction] == 0))
                def _():
                    x2(direction, at // 2).start()

        for direction in range(2):
            rank = ranks[direction]
            at = step - LAG * rank

            @pl.when((rank >= 1) & (at >= 0) & (at < deep))
            def _():
                where = 2 * wide + 2 * at + direction
                z1(direction, at).wait_recv()
                add(total, where, total, where, from_deep, direction * deep + at)

                @pl.when(rank < line - 1)
                def _():
                    z1(direction, at).start()

                @pl.when((rank == line - 1) & (at % 2 != column))
                def _():
                    z2(direction, at).start()

            twice = step - LAG - LAG * rank - direction

            @pl.when((rank >= 1) & (twice >= 0) & (twice < wide) & (twice % 2 == 0))
            def _():
                at = twice // 2
                where = 4 * at + 2 * direction + column
                x2(direction, at).wait_recv()
                slot = direction * (wide // 2) + at

                @pl.when(rank < line - 1)
                def _():
                    add(total, where, total, where, from_line, slot)
                    x2(direction, at).start()

                @pl.when(rank == line - 1)
                def _():
                    add(done, where, total, where, from_line, slot)
                    a2(direction, at).start()
                    ax(2 * at + direction, True).start()
                    put(where)

            at = step - LAG * line

            @pl.when((rank == line - 1) & (at >= 0) & (at < deep) & (at % 2 == column))
            def _():
                where = 2 * wide + 2 * at + direction
                z2(direction, at).wait_recv()
                add(done, where, total, where, from_side, at // 2)
                a1(direction, at).start()
                a4(direction, at).start()
                put(where)

            later = step - LAG * line - LAG

            @pl.when((rank == line - 1) & (later >= 0) & (later < deep) & (later % 2 != column))
            def _():
                a4(direction, later).wait_recv()
                a1(direction, later).start()
                put(2 * wide + 2 * later + direction)

            back = LAG * (line - 1 - rank)
            twice = step - LAG * line - back - direction

            @pl.when((rank < line - 1) & (twice >= 0) & (twice < wide) & (twice % 2 == 0))
            def _():
                at = twice // 2
                a2(direction, at).wait_recv()

                @pl.when(rank > 0)
                def _():
                    a2(direction, at).start()

                ax(2 * at + direction, True).start()
                put(4 * at + 2 * direction + column)

            for other in range(2):
                at = step - LAG * line - back - LAG * other

                @pl.when(
                    (rank < line - 1)
                    & (at >= 0)
                    & (at < deep)
                    & ((at + column) % 2 == other)
                )
                def _():
                    a1(direction, at).wait_recv()

                    @pl.when(rank > 0)
                    def _():
                        a1(direction, at).start()

                    put(2 * wide + 2 * at + direction)

            twice = step - LAG * line - back - direction - LAG

            @pl.when((twice >= 0) & (twice < wide) & (twice % 2 == 0))
            def _():
                at = twice + direction
                ax(at, False).wait_recv()
                put(2 * at + 1 - column)

        small_phase(step)
        return carry

    steps = wide - 1 + LAG * line + LAG * (line - 1) + LAG + 1
    load(soon[:2], "wait")
    lax.fori_loop(-1, steps, step_body, 0)

    small_mirror_copy().wait()
    small_out.wait_send()
    small_side_copy().wait_send()
    for ahead in range(1, line):
        small_line_copy(ahead).wait_send()

    def drain(at, carry):
        pltpu.make_async_copy(unit(done, at), unit(done, at), out_sem.at[at]).wait()
        return carry

    lax.fori_loop(0, Exchange.UNITS, drain, 0)

    def drain_give(slot, carry):
        half_copy(slot, 0).wait_send()
        return carry

    lax.fori_loop(0, GIVE, drain_give, 0)

    def drain_wide(at, carry):
        x1(at).wait_send()
        ax(at, True).wait_send()
        return carry

    lax.fori_loop(0, wide, drain_wide, 0)
    for direction in range(2):
        rank = ranks[direction]

        def drain_line(at, carry):
            @pl.when(rank < line - 1)
            def _():
                x2(direction, at).wait_send()

            @pl.when(rank > 0)
            def _():
                a2(direction, at).wait_send()

            return carry

        lax.fori_loop(0, wide // 2, drain_line, 0)

        def drain_deep(at, carry):
            @pl.when(rank < line - 1)
            def _():
                z1(direction, at).wait_send()

            @pl.when(rank > 0)
            def _():
                a1(direction, at).wait_send()

            @pl.when((rank == line - 1) & (at % 2 != column))
            def _():
                z2(direction, at).wait_send()

            @pl.when((rank == line - 1) & (at % 2 == column))
            def _():
                a4(direction, at).wait_send()

            return carry

        lax.fori_loop(0, deep, drain_deep, 0)


def exchange(enc_operands, reg_operands, vec_grads, bias_grads, width, local, hidden):
    units, wide, deep = Exchange.UNITS, Exchange.WIDE, Exchange.DEEP
    images = len(enc_operands)

    def buffer(count, dtype=BF):
        return pltpu.VMEM((count * UNIT, local), dtype)

    def sems(*counts):
        return [pltpu.SemaphoreType.DMA((count,)) for count in counts]

    line = Exchange.LINE
    vspec = pl.BlockSpec(memory_space=pltpu.VMEM)
    return pl.pallas_call(
        functools.partial(exchange_kernel, images),
        out_shape=[
            jax.ShapeDtypeStruct((1, hidden, width), BF),
            jax.ShapeDtypeStruct((1, width, hidden), BF),
            jax.ShapeDtypeStruct((1, local, width), BF),
            jax.ShapeDtypeStruct((1, 3, width, local), BF),
            jax.ShapeDtypeStruct((16, width), F32),
            jax.ShapeDtypeStruct((16, width), F32),
        ],
        in_specs=[ANY] * (2 * images * len(OPERANDS)) + [vspec] * (2 * images),
        out_specs=[ANY] * 4 + [vspec, vspec],
        scratch_shapes=[pltpu.VMEM((images,) + one.shape, BF) for one in reg_operands[0]]
        + [
            buffer(1, F32),
            buffer(GIVE),
            buffer(units),
            buffer(units),
            buffer(wide),
            buffer(wide),
            buffer(2 * deep),
            buffer(deep // 2),
            buffer(units),
            pltpu.VMEM((24, width), F32),
            pltpu.VMEM((16, width), F32),
            pltpu.VMEM((24, width), F32),
            pltpu.VMEM((16, width), F32),
            pltpu.VMEM((line, 16, width), F32),
            pltpu.SemaphoreType.DMA((len(OPERANDS), images)),
        ]
        + sems(GIVE, units, wide, wide, wide, wide, 2 * deep, 2 * deep)
        + sems(deep // 2, deep // 2, wide, wide, wide, wide, 2 * deep, 2 * deep)
        + sems(deep // 2, deep // 2, units, 3 + line, 2 + line),
        compiler_params=params_of(collective_id=0, has_side_effects=True),
        cost_estimate=pl.CostEstimate(flops=0, bytes_accessed=200_000_000, transcendentals=0),
        name="gradient_exchange",
    )(*sum(enc_operands, []), *sum(reg_operands, []), *vec_grads, *bias_grads)


def finish_results(sums, inputs, totals, other, bias_blocks):
    steps = 8
    down, up, out, qkv = sums
    rows, width = inputs[0].shape
    hidden = down.shape[1]

    def rows_spec(array, axis):
        block = list(array.shape)
        block[axis] //= steps
        return pl.BlockSpec(
            tuple(block), lambda i: tuple(i if at == axis else 0 for at in range(len(block)))
        )

    specs = [rows_spec(one, 1) for one in (down, up, out)] + [rows_spec(qkv, 2)]
    stacked = jax.ShapeDtypeStruct((1, len(inputs), rows, width), F32)
    small = [(1, 2, width)] * 3 + [(1, hidden), (1, width), (width,)]

    def fixed(shape):
        return pl.BlockSpec(shape, lambda i: (0,) * len(shape))

    def kernel(*refs):
        sum_refs, input_refs = refs[:4], refs[4 : 4 + len(inputs)]
        refs = refs[4 + len(inputs) :]
        totals_ref, other_ref, refs = refs[0], refs[1], refs[2:]
        for source, target in zip(sum_refs, refs[:4]):
            target[...] = source[...].astype(F32)
        for at, source in enumerate(input_refs):
            refs[4][0, at] = source[...]
        gains, biases, scales, bias, down_bias, token = refs[5:]

        @pl.when(pl.program_id(0) == 0)
        def _():
            for at, target in enumerate((gains, biases, scales)):
                target[0] = totals_ref[2 * at : 2 * at + 2, :]
            for at in range(bias_blocks):
                bias[:, at * width : (at + 1) * width] = totals_ref[8 + at : 9 + at, :]
            down_bias[...] = totals_ref[6:7, :]

            @pl.when(lax.axis_index("stream") == 0)
            def _():
                token[...] = other_ref[7, :]

            @pl.when(lax.axis_index("stream") == 1)
            def _():
                token[...] = totals_ref[7, :]

    return pl.pallas_call(
        kernel,
        grid=(steps,),
        out_shape=[jax.ShapeDtypeStruct(one.shape, F32) for one in sums]
        + [stacked]
        + [jax.ShapeDtypeStruct(one, F32) for one in small],
        in_specs=specs
        + [rows_spec(one, 0) for one in inputs]
        + [fixed(totals.shape), fixed(other.shape)],
        out_specs=specs + [rows_spec(stacked, 2)] + [fixed(one) for one in small],
        compiler_params=params_of(),
        name="finish_results",
    )(*sums, *inputs, totals, other)


def place_code(positions, model_width):
    half_width = model_width // 2
    frequency = jnp.exp(
        jnp.arange(half_width, dtype=F32) * (-math.log(10000.0) / half_width)
    )
    angles = positions.astype(F32)[..., None] * frequency
    return jnp.sin(jnp.concatenate([angles, angles + 0.5 * math.pi], -1))


def shards(
    patches,
    order,
    cotangent,
    norm_gains,
    norm_biases,
    layer_scales,
    qkv_weight,
    out_weight,
    up_weight,
    up_bias,
    down_weight,
    down_bias,
    mask_token,
):
    images, places, width = patches.shape
    rows = places // 2
    hidden = up_weight.shape[2]
    local = width // 2
    encoder = lax.axis_index("stream") == 0

    def swapped(value):
        return lax.ppermute(value, "head", SWAP)

    own = (qkv_weight[0], out_weight[0], up_weight[0], down_weight[0])
    matrices = []
    for value in own:
        matrices += [value, swapped(value)]
    bias_pair = jnp.stack([up_bias[0], swapped(up_bias[0])]).astype(F32)[:, None, :]
    vec = jnp.concatenate(
        [
            norm_gains[0],
            norm_biases[0],
            layer_scales[0],
            down_bias[0][None],
            jnp.zeros((1, width), F32),
        ]
    )
    token = mask_token[None]
    cotangent = cotangent[0]
    order_column = order[:, :, None]
    order_row = order[:, None, :]

    kept_list = list(kept_shapes(rows, rows, width, hidden).values())
    row_shape = ((rows, width), BF)
    code_shape = ((images, places, width), F32)
    grad_list = list(grad_shapes(rows, rows, width, hidden).values())
    operand_list = operand_shapes(rows, places, width, hidden)

    kept, latents = [], []
    codes = None
    for image in range(images):

        def run_encoder():
            outs = encoder_forward(
                image, 0, patches, order_column, vec, up_bias=bias_pair, matrices=matrices, save=True
            )
            return tuple(outs) + ((nothing([code_shape])[0],) if image == 0 else ())

        def run_other():
            outs = nothing([row_shape] + kept_list)
            return tuple(outs) + ((place_code(order, width),) if image == 0 else ())

        outs = lax.cond(encoder, run_encoder, run_other)
        if image == 0:
            codes = outs[-1]
            outs = outs[:-1]
        latents.append(outs[0])
        kept.append(outs[1:])
    arrived = [lax.ppermute(one, "stream", [(0, 1)]) for one in latents]

    features, returned, reg_inputs, reg_vecs, reg_biases, reg_operands = [], [], [], [], [], []
    for image in range(images):

        def run_targets():
            rest = tuple(
                nothing(
                    [row_shape, row_shape, ((places, width), F32)]
                    + [((8, width), F32), ((2, 1, hidden), F32)]
                    + operand_list
                )
            )
            if image == 0:
                rest += tuple(
                    encoder_forward(
                        None, 1, patches, order_column, vec, bias_pair, matrices, save=False
                    )
                )
            return rest

        def run_regressor():
            outs = regressor_block(
                image, arrived[image], codes, token, cotangent, vec, bias_pair, matrices
            )
            if image == 0:
                outs = tuple(outs) + tuple(nothing([((images, rows, width), BF)]))
            return tuple(outs)

        outs = lax.cond(encoder, run_targets, run_regressor)
        if image == 0:
            targets = outs[-1]
            outs = outs[:-1]
        features.append(outs[0])
        returned.append(lax.ppermute(outs[1], "stream", [(1, 0)]))
        reg_inputs.append(outs[2])
        reg_vecs.append(outs[3])
        reg_biases.append(outs[4])
        reg_operands.append(list(outs[5:]))

    input_grads, vec_grads, bias_grads, enc_operands = [], [], [], []
    for image in range(images):

        def run_backward():
            return encoder_backward(
                image, returned[image], cotangent, order_row, kept[image], vec, matrices
            )

        def run_pass():
            return (reg_inputs[image], reg_vecs[image], reg_biases[image]) + tuple(
                nothing(grad_list)
            )

        outs = lax.cond(encoder, run_backward, run_pass)
        input_grads.append(outs[0])
        vec_grads.append(outs[1])
        bias_grads.append(outs[2])
        named = dict(zip(KEPT, kept[image]))
        named.update(zip(GRADS, outs[3:]))
        enc_operands.append([named[name] for name in OPERANDS])

    if lax.axis_size("dp") == 2 * Exchange.LINE and width == 768 and hidden == 1536:
        down, up, out, qkv, totals, other = exchange(
            enc_operands, reg_operands, vec_grads, bias_grads, width, local, hidden
        )
        outs = finish_results(
            (down, up, out, qkv), input_grads, totals, other, hidden // width
        )
        down, up, out, qkv, input_grad = outs[:5]
        gains, biases, scales, bias_total, down_bias_total, token_grad = outs[5:]
    else:
        parts = lax.cond(
            encoder,
            lambda: matrix_grads(enc_operands, 0),
            lambda: matrix_grads(reg_operands, rows),
        )
        vec_grad = sum(vec_grads)
        bias_grad = sum(bias_grads)[:, 0]

        def reduced(value):
            mine = value[0].astype(F32) + swapped(value[1]).astype(F32)
            part = lax.psum_scatter(mine.astype(BF), "dp", scatter_dimension=0, tiled=True)
            return lax.all_gather(part, "dp", axis=0, tiled=True).astype(F32)

        down, up, out, query, key, value = (reduced(one) for one in parts)
        qkv = jnp.stack([query, key, value])
        qkv, out, up, down = (one[None] for one in (qkv, out, up, down))
        bias_total = lax.psum(bias_grad[0] + swapped(bias_grad[1]), "dp")
        totals = lax.psum(vec_grad, ("dp", "head"))
        token_grad = lax.psum(jnp.where(encoder, 0.0, totals[7]), "stream")
        bias_total = bias_total[None]
        input_grad = jnp.stack(input_grads)[None]
        gains, biases, scales = (totals[at : at + 2][None] for at in (0, 2, 4))
        down_bias_total = totals[6][None]

    latent_out = jnp.where(encoder, jnp.stack(latents), jnp.stack(arrived))
    return (
        latent_out,
        jnp.where(encoder, targets, jnp.stack(features))[None],
        input_grad,
        gains,
        biases,
        scales,
        qkv,
        out,
        up,
        bias_total,
        down,
        down_bias_total,
        token_grad,
    )


def solution(mesh):
    in_specs = (
        P(("dp", "head"), None, None),
        P(("dp", "head"), None),
        P("stream", ("dp", "head"), None, None),
        P("stream", None, None),
        P("stream", None, None),
        P("stream", None, None),
        P("stream", None, None, "head"),
        P("stream", "head", None),
        P("stream", None, "head"),
        P("stream", "head"),
        P("stream", "head", None),
        P("stream", None),
        P(),
    )
    out_specs = (
        P(("dp", "head"), None, None),
        P("stream", ("dp", "head"), None, None),
        P("stream", ("dp", "head"), None, None),
        P("stream", None, None),
        P("stream", None, None),
        P("stream", None, None),
        P("stream", None, None, "head"),
        P("stream", "head", None),
        P("stream", None, "head"),
        P("stream", "head"),
        P("stream", "head", None),
        P("stream", None),
        P(),
    )
    return jax.shard_map(shards, mesh=mesh, in_specs=in_specs, out_specs=out_specs, check_vma=False)
```

```python
import functools
import math

import jax
import jax.numpy as jnp
from jax import lax
from jax.experimental import pallas as pl
from jax.experimental.pallas import tpu as pltpu
from jax.sharding import PartitionSpec as P

HEADS = 12
EPSILON = 1e-06
BF = jnp.bfloat16
F32 = jnp.float32
ROWS_AT_ONCE = 64
NN = ((1,), (0,))
NT = ((1,), (1,))
TN = ((0,), (0,))
SWAP = ((0, 1), (1, 0))
VMEM_BYTES = 60 * 1024 * 1024


def dot(left, right, dims=NN):
    return lax.dot_general(left, right, (dims, ((), ())), preferred_element_type=F32)


def row_loop(rows, body):
    def step(index, carry):
        body(pl.ds(pl.multiple_of(index * ROWS_AT_ONCE, ROWS_AT_ONCE), ROWS_AT_ONCE))
        return carry

    lax.fori_loop(0, rows // ROWS_AT_ONCE, step, 0)


def halves_loop(size, body):
    def step(half, carry):
        body(half, pl.ds(pl.multiple_of(half * size, size), size))
        return carry

    lax.fori_loop(0, 2, step, 0)


def standardize(values):
    centred = values - jnp.mean(values, -1, keepdims=True)
    inv_std = lax.rsqrt(jnp.mean(centred * centred, -1, keepdims=True) + EPSILON)
    return centred * inv_std, inv_std


def norm_into(source, target, gain, bias):
    def body(rows):
        scaled, _ = standardize(source[rows, :])
        target[rows, :] = (scaled * gain + bias).astype(BF)

    row_loop(source.shape[0], body)


def fold_rows(values):
    return jnp.sum(values.reshape(-1, 8, values.shape[-1]), 0)


def norm_back(grad, scaled, inv_std, gain):
    scaled_grad = grad * gain
    return inv_std * (
        scaled_grad
        - jnp.mean(scaled_grad, -1, keepdims=True)
        - scaled * jnp.mean(scaled_grad * scaled, -1, keepdims=True)
    )


class Weights:
    NAMES = ("qkv", "out", "up", "down")

    def __init__(self, sources, buffers, sems, names=NAMES, first_only=False):
        self.first_only = first_only
        self.buffers = dict(zip(self.NAMES, buffers))
        self.copies = {}
        for at, name in enumerate(self.NAMES):
            if name not in names:
                continue
            for half in range(2):
                self.copies[name, half] = pltpu.make_async_copy(
                    sources[2 * at + half], self.buffers[name].at[half], sems.at[at, half]
                )

    def each(self, names, method):
        def run():
            for name in names:
                for half in range(2):
                    getattr(self.copies[name, half], method)()

        if self.first_only:
            pl.when(pl.program_id(0) == 0)(run)
        else:
            run()

    def start(self, order):
        self.each(order, "start")

    def wait(self, name):
        self.each((name,), "wait")

    def __getitem__(self, name):
        return self.buffers[name]


class Held(dict):
    def __init__(self, buffers):
        super().__init__(buffers)
        self.coming, self.going = {}, {}

    def copy_in(self, names, sources, sems):
        for at, (name, source) in enumerate(zip(names, sources)):
            self.coming[name] = pltpu.make_async_copy(source, self[name], sems.at[at])
            self.coming[name].start()

    def copy_out(self, names, targets, sems):
        for at, (name, target) in enumerate(zip(names, targets)):
            self.going[name] = pltpu.make_async_copy(self[name], target, sems.at[at])

    def need(self, *names):
        for name in names:
            if name in self.coming:
                self.coming[name].wait()

    def ready(self, *names):
        for name in names:
            if name in self.going:
                self.going[name].start()

    def finish(self):
        for copy in self.going.values():
            copy.wait()


def weight_scratch(width, local, hidden):
    return [
        pltpu.VMEM((2, 3, width, local), BF),
        pltpu.VMEM((2, local, width), BF),
        pltpu.VMEM((2, width, hidden), BF),
        pltpu.VMEM((2, hidden, width), BF),
        pltpu.SemaphoreType.DMA((4, 2)),
    ]


def head_masks():
    lanes = lax.broadcasted_iota(jnp.int32, (1, 128), 1)
    low = (lanes < 64).astype(F32)
    return low.astype(BF), (1.0 - low).astype(BF)


def forward(rows_all, ctx, vec, up_bias, weights, keep, result_fn):
    width = rows_all.shape[1]
    row_count = rows_all.shape[0] - ctx
    normed, queries, keys, values, probs, mixed = (
        keep[name] for name in ("N", "Q", "K", "V", "P", "O")
    )
    norm_into(rows_all, normed, vec[0:1, :], vec[2:3, :])
    keep.ready("N")
    weights.wait("qkv")
    local = weights["qkv"].shape[3]

    def project(half, cols):
        queries[:, cols] = (dot(normed[ctx:, :], weights["qkv"][half, 0]) * 0.125).astype(BF)
        keys[:, cols] = dot(normed[...], weights["qkv"][half, 1]).astype(BF)
        values[:, cols] = dot(normed[...], weights["qkv"][half, 2]).astype(BF)

    halves_loop(local, project)
    keep.ready("Q", "K", "V")
    masks = head_masks()

    def attend(pair, carry):
        cols = pl.ds(pl.multiple_of(pair * 128, 128), 128)
        query, key = queries[:, cols], keys[:, cols]
        value_t = values[:, cols].T
        outs = []
        for at in range(2):
            scores = dot(key, query * masks[at], NT)
            weight = jnp.exp(scores - jnp.max(scores, 0, keepdims=True))
            prob = (weight * (1.0 / jnp.sum(weight, 0, keepdims=True))).astype(BF)
            probs[2 * pair + at] = prob
            outs.append(dot(value_t[64 * at : 64 * at + 64], prob))
        mixed[:, cols] = jnp.concatenate(outs, 0).T.astype(BF)
        return carry

    lax.fori_loop(0, HEADS // 2, attend, 0)
    keep.ready("P", "O")
    weights.wait("out")
    attended = dot(mixed[:, :local], weights["out"][0]) + dot(mixed[:, local:], weights["out"][1])
    hidden, normed_two = keep["H"], keep["M"]
    keep["A"][...] = attended.astype(keep["A"].dtype)
    hidden[...] = rows_all[ctx:, :] + vec[4:5, :] * attended
    norm_into(hidden, normed_two, vec[1:2, :], vec[3:4, :])
    keep.ready("A", "H", "M")
    weights.wait("up")
    weights.wait("down")
    fed = keep["F"]
    fed[...] = jnp.broadcast_to(vec[6:7, :], fed.shape)
    step = 768
    per_half = weights["up"].shape[2] // step

    def feed(index, carry):
        half, chunk = index // per_half, index % per_half
        cols = pl.ds(pl.multiple_of(chunk * step, step), step)
        pre = dot(normed_two[...], weights["up"][half, :, cols]) + up_bias[half, :, cols]
        phi = 0.5 + 0.5 * lax.erf(pre * math.sqrt(0.5))
        act = (pre * phi).astype(BF)
        if "G" in keep:
            keep["G"][half, :, cols] = act
            density = jnp.exp(pre * pre * -0.5) * (1.0 / math.sqrt(2.0 * math.pi))
            keep["D"][half, :, cols] = (phi + pre * density).astype(BF)
        fed[...] += dot(act, weights["down"][half, cols, :])
        return carry

    lax.fori_loop(0, 2 * per_half, feed, 0)

    keep.ready("G", "D", "F")

    def finish(rows):
        result_fn(rows, hidden[rows, :] + vec[5:6, :] * fed[rows, :])

    row_loop(row_count, finish)


def backward(rows_all, ctx, out_grad_fn, vec, weights, keep, grads, work, sums, up_bias_grad):
    width = rows_all.shape[1]
    row_count = rows_all.shape[0] - ctx
    local = width // 2
    grad_in = work["dH"]
    for at in range(8):
        sums[at] = jnp.zeros((8, width), F32)

    def enter(rows):
        grad = out_grad_fn(rows)
        grad_in[rows, :] = grad
        branch = vec[5:6, :] * grad
        sums[5] += fold_rows(grad * keep["F"][rows, :].astype(F32))
        sums[6] += fold_rows(branch)
        grads["dF"][rows, :] = branch.astype(BF)

    keep.need("F")
    row_loop(row_count, enter)
    grads.ready("dF")
    keep.need("D")
    weights.wait("down")
    weights.wait("up")
    grad_mid = work["dM"]
    grad_mid[...] = jnp.zeros_like(grad_mid)
    step = 768
    per_half = weights["up"].shape[2] // step

    def feed(index, carry):
        half, chunk = index // per_half, index % per_half
        cols = pl.ds(pl.multiple_of(chunk * step, step), step)
        act_grad = dot(grads["dF"][...], weights["down"][half, cols, :], NT)
        pre_grad = act_grad * keep["D"][half, :, cols].astype(F32)
        up_bias_grad[half, :, cols] = jnp.sum(pre_grad, 0, keepdims=True)
        pre_grad = pre_grad.astype(BF)
        grads["dU"][half, :, cols] = pre_grad
        grad_mid[...] += dot(pre_grad, weights["up"][half, :, cols], NT)
        return carry

    lax.fori_loop(0, 2 * per_half, feed, 0)

    def middle(rows):
        scaled, inv_std = standardize(keep["H"][rows, :])
        grad = grad_mid[rows, :]
        sums[1] += fold_rows(grad * scaled)
        sums[3] += fold_rows(grad)
        hidden_grad = grad_in[rows, :] + norm_back(grad, scaled, inv_std, vec[1:2, :])
        grad_in[rows, :] = hidden_grad
        sums[4] += fold_rows(hidden_grad * keep["A"][rows, :].astype(F32))
        grads["dA"][rows, :] = (vec[4:5, :] * hidden_grad).astype(BF)

    grads.ready("dU")
    keep.need("H", "A")
    row_loop(row_count, middle)
    grads.ready("dA")
    weights.wait("out")
    mix_grad = work["dO"]

    def unmix(half, cols):
        mix_grad[:, cols] = dot(grads["dA"][...], weights["out"][half], NT).astype(BF)

    halves_loop(local, unmix)
    masks = head_masks()

    def attend(pair, carry):
        cols = pl.ds(pl.multiple_of(pair * 128, 128), 128)
        query, key, value = keep["Q"][:, cols], keep["K"][:, cols], keep["V"][:, cols]
        out_grad = mix_grad[:, cols]
        key_t = key.T
        value_grad = key_grad = None
        query_grads = []
        for at in range(2):
            prob = keep["P"][2 * pair + at]
            own_grad = out_grad * masks[at]
            part = dot(prob, own_grad)
            value_grad = part if value_grad is None else value_grad + part
            prob_grad = dot(value, own_grad, NT)
            wide = prob.astype(F32)
            product = wide * prob_grad
            score_grad = (product - wide * jnp.sum(product, 0, keepdims=True)).astype(BF)
            part = dot(score_grad, query * masks[at])
            key_grad = part if key_grad is None else key_grad + part
            query_grads.append(dot(key_t[64 * at : 64 * at + 64], score_grad))
        grads["dV"][:, cols] = value_grad.astype(BF)
        grads["dK"][:, cols] = key_grad.astype(BF)
        grads["dQ"][:, cols] = (jnp.concatenate(query_grads, 0).T * 0.125).astype(BF)
        return carry

    keep.need("P", "Q", "K", "V")
    lax.fori_loop(0, HEADS // 2, attend, 0)
    grads.ready("dQ", "dK", "dV")
    weights.wait("qkv")
    grad_all = work["dN"]
    qkv = weights["qkv"]
    grad_all[...] = jnp.zeros_like(grad_all)

    def unproject(half, cols):
        grad_all[...] += dot(grads["dK"][:, cols], qkv[half, 1], NT) + dot(
            grads["dV"][:, cols], qkv[half, 2], NT
        )
        grad_all[ctx:, :] += dot(grads["dQ"][:, cols], qkv[half, 0], NT)

    halves_loop(local, unproject)

    def leave(rows):
        scaled, inv_std = standardize(rows_all[rows, :].astype(F32))
        grad = grad_all[rows, :]
        sums[0] += fold_rows(grad * scaled)
        sums[2] += fold_rows(grad)
        grad_all[rows, :] = norm_back(grad, scaled, inv_std, vec[0:1, :])

    keep.need("X")
    row_loop(rows_all.shape[0], leave)


def write_sums(sums, target):
    for at in range(8):
        target[at : at + 1, :] = jnp.sum(sums[at], 0, keepdims=True)


def pick_rows(order_column, patches):
    places = lax.broadcasted_iota(jnp.int32, (order_column.shape[0], patches.shape[0]), 1)
    return dot((places == order_column).astype(F32).astype(BF), patches)


READ_BACK = ("F", "D", "H", "A", "P", "Q", "K", "V", "X")
KEPT = ("X", "N", "Q", "K", "V", "P", "O", "A", "H", "M", "G", "D", "F")
GRADS = ("dF", "dU", "dA", "dQ", "dK", "dV")
OPERANDS = ("dF", "G", "dU", "M", "dA", "O", "dQ", "dK", "dV", "N")


def kept_shapes(rows, keys, width, hidden):
    return {
        "X": ((rows, width), BF),
        "N": ((keys, width), BF),
        "Q": ((rows, width), BF),
        "K": ((keys, width), BF),
        "V": ((keys, width), BF),
        "P": ((HEADS, keys, rows), BF),
        "O": ((rows, width), BF),
        "A": ((rows, width), BF),
        "H": ((rows, width), F32),
        "M": ((rows, width), BF),
        "G": ((2, rows, hidden), BF),
        "D": ((2, rows, hidden), BF),
        "F": ((rows, width), F32),
    }


def grad_shapes(rows, keys, width, hidden):
    return {
        "dF": ((rows, width), BF),
        "dU": ((2, rows, hidden), BF),
        "dA": ((rows, width), BF),
        "dQ": ((rows, width), BF),
        "dK": ((keys, width), BF),
        "dV": ((keys, width), BF),
    }


def vmem(shape_type):
    return pltpu.VMEM(*shape_type)


ONCE = pl.Buffered(1)


def whole(shape):
    return pl.BlockSpec(tuple(shape), lambda _: (0,) * len(shape), pipeline_mode=ONCE)


def image_of(array, image):
    return pl.BlockSpec(
        (None,) + array.shape[1:],
        lambda _: (image,) + (0,) * (array.ndim - 1),
        pipeline_mode=ONCE,
    )


ANY = pl.BlockSpec(memory_space=pl.ANY)


def shape_of(shape_type):
    return jax.ShapeDtypeStruct(*shape_type)


def nothing(shapes):
    return pl.pallas_call(
        lambda *refs: None,
        out_shape=[shape_of(s) for s in shapes],
        out_specs=[ANY] * len(shapes),
        name="no_values",
    )()


def params_of(**extra):
    return pltpu.CompilerParams(vmem_limit_bytes=VMEM_BYTES, **extra)


def block_cost(rows, keys, width, hidden, passes):
    flops = 2 * rows * width * (2 * width + 4 * hidden) + 4 * keys * width * width
    flops += 4 * rows * keys * width
    return pl.CostEstimate(flops=passes * flops, bytes_accessed=24_000_000, transcendentals=0)


def encoder_forward(image, which, patches, order_column, vec, up_bias, matrices, save):
    images, places, width = patches.shape
    rows = places // 2
    hidden = matrices[4].shape[1]
    local = width // 2
    shapes = kept_shapes(rows, rows, width, hidden)
    names = [n for n in KEPT]
    own = names if save else [n for n in names if n not in ("X", "G", "D")]

    def kernel(patch_ref, order_ref, vec_ref, bias_ref, *refs):
        sources, refs = refs[:8], refs[8:]
        result, refs = refs[0], refs[1:]
        if save:
            targets, refs = refs[: len(names)], refs[len(names) :]
        keep = Held(zip(own, refs))
        refs = refs[len(own) :]
        rows_ref, refs = refs[0], refs[1:]
        weights = Weights(sources, refs[:4], refs[4], first_only=not save)
        weights.start(("qkv", "out", "up", "down"))
        rows_ref[...] = pick_rows(order_ref[...], patch_ref[...])
        if save:
            keep.copy_out(names, targets, refs[5])
            keep["X"][...] = rows_ref[...].astype(BF)
            keep.ready("X")

        def result_fn(rows_at, value):
            result[rows_at, :] = value.astype(BF)

        forward(rows_ref, 0, vec_ref, bias_ref, weights, keep, result_fn)
        keep.finish()

    out_shapes = [((rows, width), BF)] + ([shapes[n] for n in names] if save else [])
    out_specs = [whole(out_shapes[0][0])] + [ANY] * (len(out_shapes) - 1)
    patch_spec = image_of(patches, image)
    scratch = [vmem(shapes[n]) for n in own] + [pltpu.VMEM((rows, width), F32)]
    scratch += weight_scratch(width, local, hidden) + [pltpu.SemaphoreType.DMA((len(names),))]
    order_spec = pl.BlockSpec(
        (None, rows, 1), lambda _: (image, which, 0), pipeline_mode=ONCE
    )
    if not save:
        out_shapes = [((images, rows, width), BF)]
        out_specs = [pl.BlockSpec((None, rows, width), lambda i: (i, 0, 0))]
        patch_spec = pl.BlockSpec((None, places, width), lambda i: (i, 0, 0))
        order_spec = pl.BlockSpec((None, rows, 1), lambda i: (i, which, 0))
    return pl.pallas_call(
        kernel,
        grid=(1 if save else images,),
        out_shape=[shape_of(s) for s in out_shapes],
        in_specs=[patch_spec, order_spec, whole(vec.shape), whole(up_bias.shape)] + [ANY] * 8,
        out_specs=out_specs,
        scratch_shapes=scratch,
        compiler_params=params_of(),
        cost_estimate=block_cost(rows, rows, width, hidden, 1),
        name="encoder_forward" if save else "encoder_targets",
    )(patches, order_column, vec, up_bias, *matrices)


def encoder_backward(image, latent_grad, cotangent, order_row, kept, vec, matrices):
    rows, width = latent_grad.shape
    hidden = matrices[4].shape[1]
    local = width // 2
    shapes = grad_shapes(rows, rows, width, hidden)
    names = list(GRADS)
    kept = [dict(zip(KEPT, kept))[name] for name in READ_BACK]

    def kernel(back_ref, cot_ref, order_ref, vec_ref, *refs):
        sources, refs = refs[:8], refs[8:]
        saved, refs = refs[: len(READ_BACK)], refs[len(READ_BACK) :]
        input_grad, vec_grad, bias_grad, refs = refs[0], refs[1], refs[2], refs[3:]
        targets, refs = refs[: len(names)], refs[len(names) :]
        keep = Held(zip(READ_BACK, refs))
        grads = Held(zip(names, refs[len(READ_BACK) :]))
        refs = refs[len(READ_BACK) + len(names) :]
        d_hidden, d_mid, d_out, d_norm, sums = refs[:5]
        weights = Weights(sources, refs[5:9], refs[9])
        keep.copy_in(READ_BACK[:2], saved, refs[11])
        weights.start(("down", "up"))
        keep.copy_in(READ_BACK[2:], saved[2:], refs[12])
        weights.start(("out", "qkv"))
        grads.copy_out(names, targets, refs[13])
        work = {"dH": d_hidden, "dM": d_mid, "dO": d_out, "dN": d_norm}

        def out_grad_fn(rows_at):
            return cot_ref[rows_at, :].astype(F32) + back_ref[rows_at, :].astype(F32)

        backward(
            keep["X"], 0, out_grad_fn, vec_ref, weights, keep, grads, work, sums, bias_grad
        )
        write_sums(sums, vec_grad)

        def join(rows_at):
            total = d_norm[rows_at, :] + d_hidden[rows_at, :]
            high = total.astype(BF)
            d_out[rows_at, :] = high
            grads_low[rows_at, :] = (total - high.astype(F32)).astype(BF)

        grads_low = refs[10]
        row_loop(rows, join)

        def place(index, carry):
            first = pl.multiple_of(index * 128, 128)
            places = lax.broadcasted_iota(jnp.int32, (128, rows), 0) + first
            hot = (places == order_ref[...]).astype(F32).astype(BF)
            input_grad[pl.ds(first, 128), :] = dot(hot, d_out[...]) + dot(hot, grads_low[...])
            return carry

        lax.fori_loop(0, input_grad.shape[0] // 128, place, 0)
        grads.finish()

    out_shapes = [((2 * rows, width), F32), ((8, width), F32), ((2, 1, hidden), F32)]
    out_shapes += [shapes[n] for n in names]
    forms = kept_shapes(rows, rows, width, hidden)
    scratch = [vmem(forms[n]) for n in READ_BACK] + [vmem(shapes[n]) for n in names]
    scratch += [
        pltpu.VMEM((rows, width), F32),
        pltpu.VMEM((rows, width), F32),
        pltpu.VMEM((rows, width), BF),
        pltpu.VMEM((rows, width), F32),
        pltpu.VMEM((8, 8, width), F32),
    ]
    scratch += weight_scratch(width, local, hidden) + [pltpu.VMEM((rows, width), BF)]
    scratch += [
        pltpu.SemaphoreType.DMA((2,)),
        pltpu.SemaphoreType.DMA((len(READ_BACK) - 2,)),
        pltpu.SemaphoreType.DMA((len(names),)),
    ]
    order_spec = pl.BlockSpec((None, 1, rows), lambda _: (image, 0, 0), pipeline_mode=ONCE)
    outs = pl.pallas_call(
        kernel,
        grid=(1,),
        out_shape=[shape_of(s) for s in out_shapes],
        in_specs=[whole(latent_grad.shape), image_of(cotangent, image), order_spec, whole(vec.shape)]
        + [ANY] * (8 + len(kept)),
        out_specs=[whole(s[0]) for s in out_shapes[:3]] + [ANY] * len(names),
        scratch_shapes=scratch,
        compiler_params=params_of(),
        cost_estimate=block_cost(rows, rows, width, hidden, 1),
        name="encoder_backward",
    )(latent_grad, cotangent, order_row, vec, *matrices, *kept)
    return tuple(outs)


def operand_shapes(rows, keys, width, hidden):
    shapes = dict(grad_shapes(rows, keys, width, hidden))
    shapes.update(kept_shapes(rows, keys, width, hidden))
    return [shapes[n] for n in OPERANDS]


def regressor_block(image, latent, codes, token, cotangent, vec, up_bias, matrices):
    ctx, width = latent.shape
    rows = codes.shape[1] - ctx
    keys = rows + ctx
    hidden = matrices[4].shape[1]
    local = width // 2
    kept = kept_shapes(rows, keys, width, hidden)
    shapes = grad_shapes(rows, keys, width, hidden)
    own = [n for n in KEPT if n != "X" and n not in OPERANDS]

    def kernel(latent_ref, code_ref, token_ref, cot_ref, vec_ref, bias_ref, *refs):
        sources, refs = refs[:8], refs[8:]
        result, back, input_grad, vec_grad, bias_grad = refs[:5]
        refs = refs[5:]
        targets, refs = refs[: len(OPERANDS)], refs[len(OPERANDS) :]
        held = OPERANDS + tuple(own)
        keep = Held(zip(held, refs))
        refs = refs[len(held) :]
        keep.copy_out(OPERANDS, targets, refs[10])
        rows_ref, d_hidden, d_mid, d_out, sums = refs[:5]
        weights = Weights(sources, refs[5:9], refs[9])
        weights.start(("qkv", "out", "up", "down"))

        def fill(rows_at):
            rows_ref[rows_at, :] = latent_ref[rows_at, :].astype(F32) + code_ref[rows_at, :]
            lower = pl.ds(rows_at.start + ctx, ROWS_AT_ONCE)
            rows_ref[lower, :] = token_ref[...] + code_ref[lower, :]

        row_loop(ctx, fill)

        def result_fn(rows_at, value):
            result[rows_at, :] = value.astype(BF)

        forward(rows_ref, ctx, vec_ref, bias_ref, weights, keep, result_fn)
        work = {"dH": d_hidden, "dM": d_mid, "dO": d_out, "dN": input_grad}

        def out_grad_fn(rows_at):
            return cot_ref[rows_at, :].astype(F32)

        weights.wait = lambda name: None
        backward(
            rows_ref, ctx, out_grad_fn, vec_ref, weights, keep, keep, work, sums, bias_grad
        )

        def leave(rows_at):
            back[rows_at, :] = input_grad[rows_at, :].astype(BF)
            lower = pl.ds(rows_at.start + ctx, ROWS_AT_ONCE)
            total = input_grad[lower, :] + d_hidden[rows_at, :]
            input_grad[lower, :] = total
            sums[7] += fold_rows(total)

        row_loop(rows, leave)
        write_sums(sums, vec_grad)
        keep.finish()

    out_shapes = [
        ((rows, width), BF),
        ((ctx, width), BF),
        ((keys, width), F32),
        ((8, width), F32),
        ((2, 1, hidden), F32),
    ] + operand_shapes(rows, keys, width, hidden)
    scratch = [vmem(one) for one in operand_shapes(rows, keys, width, hidden)]
    scratch += [vmem(kept[n]) for n in own]
    scratch += [
        pltpu.VMEM((keys, width), F32),
        pltpu.VMEM((rows, width), F32),
        pltpu.VMEM((rows, width), F32),
        pltpu.VMEM((rows, width), BF),
        pltpu.VMEM((8, 8, width), F32),
    ]
    scratch += weight_scratch(width, local, hidden)
    scratch += [pltpu.SemaphoreType.DMA((len(OPERANDS),))]
    outs = pl.pallas_call(
        kernel,
        grid=(1,),
        out_shape=[shape_of(s) for s in out_shapes],
        in_specs=[
            whole(latent.shape),
            image_of(codes, image),
            whole(token.shape),
            image_of(cotangent, image),
            whole(vec.shape),
            whole(up_bias.shape),
        ]
        + [ANY] * 8,
        out_specs=[whole(s[0]) for s in out_shapes[:5]] + [ANY] * len(OPERANDS),
        scratch_shapes=scratch,
        compiler_params=params_of(),
        cost_estimate=block_cost(rows, keys, width, hidden, 2),
        name="regressor_block",
    )(latent, codes, token, cotangent, vec, up_bias, *matrices)
    return outs


def weight_grad(name, lefts, rights, first_rows, split_left, step, halves):
    images = len(lefts)
    wide = (lefts if split_left else rights)[0]
    other = (rights if split_left else lefts)[0]
    if wide.ndim == 3:
        blocks = (wide.shape[0], wide.shape[2] // step)
        wide_spec = pl.BlockSpec((None, wide.shape[1], step), lambda h, c: (h, 0, c))
        width = wide.shape[2]
    else:
        blocks = (halves, wide.shape[1] // halves // step)
        wide_spec = pl.BlockSpec(
            (wide.shape[0], step), lambda h, c: (0, h * blocks[1] + c)
        )
        width = wide.shape[1] // halves
    other_spec = pl.BlockSpec(other.shape, lambda h, c: (0, 0))
    if split_left:
        out = ((halves, width, other.shape[1]), BF)
        out_spec = pl.BlockSpec((None, step, other.shape[1]), lambda h, c: (h, c, 0))
    else:
        out = ((halves, other.shape[1], width), BF)
        out_spec = pl.BlockSpec((None, other.shape[1], step), lambda h, c: (h, 0, c))

    def kernel(*refs):
        total = None
        for at in range(images):
            left, right = refs[at][...], refs[images + at][...]
            if first_rows:
                left = left[first_rows:]
            part = dot(left, right, TN)
            total = part if total is None else total + part
        refs[-1][...] = total.astype(BF)

    specs = ([wide_spec] * images + [other_spec] * images) if split_left else (
        [other_spec] * images + [wide_spec] * images
    )
    rows = rights[0].shape[-2]
    return pl.pallas_call(
        kernel,
        grid=blocks,
        out_shape=shape_of(out),
        in_specs=specs,
        out_specs=out_spec,
        compiler_params=params_of(),
        cost_estimate=pl.CostEstimate(
            flops=2 * images * rows * halves * width * other.shape[1],
            bytes_accessed=8_000_000,
            transcendentals=0,
        ),
        name=name,
    )(*lefts, *rights)


def matrix_grads(operands, ctx):
    named = [dict(zip(OPERANDS, one)) for one in operands]

    def column(name):
        return [one[name] for one in named]

    down = weight_grad("down_grad", column("G"), column("dF"), 0, True, 512, 2)
    up = weight_grad("up_grad", column("M"), column("dU"), 0, False, 512, 2)
    out = weight_grad("out_grad", column("O"), column("dA"), 0, True, 384, 2)
    query = weight_grad("query_grad", column("N"), column("dQ"), ctx, False, 384, 2)
    key = weight_grad("key_grad", column("N"), column("dK"), 0, False, 384, 2)
    value = weight_grad("value_grad", column("N"), column("dV"), 0, False, 384, 2)
    return down, up, out, query, key, value


UNIT = 128
LAG = 2
GIVE = 16


class Exchange:
    LINE = 4
    WIDE = 20
    DEEP = 16
    UNITS = 2 * WIDE + 2 * DEEP


def exchange_kernel(images, *refs):
    count = len(OPERANDS)
    sources = []
    for _ in range(2):
        sources.append([dict(zip(OPERANDS, refs[at * count :])) for at in range(images)])
        refs = refs[images * count :]
    vec_refs, bias_refs, refs = refs[:images], refs[images : 2 * images], refs[2 * images :]
    down_ref, up_ref, out_ref, qkv_ref = (ref.at[0] for ref in refs[:4])
    totals_ref, other_ref = refs[4:6]
    refs = refs[6:]
    held = dict(zip(OPERANDS, refs[:count]))
    acc, gives = refs[count : count + 2]
    refs = refs[count + 2 :]
    total, own_half, from_column, from_line, from_deep, from_side, done = refs[:7]
    small_ref, small_own, small_half, small_side, small_line = refs[7:12]
    (load_sem, half_send, half_recv, x1_send, x1_recv, x2_send, x2_recv, z1_send, z1_recv) = refs[12:21]
    (z2_send, z2_recv, ax_send, ax_recv, a2_send, a2_recv, a1_send, a1_recv) = refs[21:29]
    (a4_send, a4_recv, out_sem, s_send, s_recv) = refs[29:34]
    line, wide, deep = Exchange.LINE, Exchange.WIDE, Exchange.DEEP
    dp = lax.axis_index("dp")
    place, column = dp // 2, dp % 2
    side = {"dp": place * 2 + 1 - column}
    partner = {"head": 1 - lax.axis_index("head")}
    mirror = {"stream": 1 - lax.axis_index("stream")}

    def along(direction, ahead):
        return {"dp": dp + 2 * (2 * direction - 1) * ahead}

    ranks = (line - 1 - place, place)

    stream = lax.axis_index("stream")
    rows, width = held["M"].shape[1:]
    hidden = held["G"].shape[3]
    local = width // 2

    def load(names, method):
        for which in range(2):

            @pl.when(stream == which)
            def _():
                for image, source in enumerate(sources[which]):
                    for name in names:
                        at = OPERANDS.index(name)
                        target = held[name].at[image]
                        if source[name].shape != target.shape:
                            target = target.at[pl.ds(0, source[name].shape[0]), :]
                        copy = pltpu.make_async_copy(source[name], target, load_sem.at[at, image])
                        getattr(copy, method)()

    soon = ("G", "dF", "M", "dU")
    rest = tuple(name for name in OPERANDS if name not in soon)
    load(soon[:2], "start")
    load(soon[2:], "start")
    load(rest, "start")

    def unit(buffer, at):
        return buffer.at[pl.ds(pl.multiple_of(at * UNIT, UNIT), UNIT), :]

    def remote(source, target, send, recv, device):
        return pltpu.make_async_remote_copy(
            src_ref=source,
            dst_ref=target,
            send_sem=send,
            recv_sem=recv,
            device_id=device,
            device_id_type=pl.DeviceIdType.MESH,
        )

    barrier = pltpu.get_barrier_semaphore()

    def greet(device):
        pl.semaphore_signal(barrier, inc=1, device_id=device, device_id_type=pl.DeviceIdType.MESH)

    for device in (partner, side, mirror):
        greet(device)
    for ahead in range(1, line):
        greet({"dp": ((place + ahead) % line) * 2 + column})
    pl.semaphore_wait(barrier, 2 + line)

    small_ref[...] = jnp.zeros_like(small_ref)
    small_ref[0:8, :] = sum(ref[...] for ref in vec_refs)
    for half in range(2):
        for at in range(hidden // width):
            row = 8 * (half + 1) + at
            cols = slice(at * width, (at + 1) * width)
            small_ref[row : row + 1, :] = sum(ref[half, :, cols] for ref in bias_refs)
    small_out = remote(small_ref, small_half, s_send.at[1], s_recv.at[0], partner)
    small_out.start()

    counts = (
        2 * hidden // UNIT,
        2 * hidden // UNIT,
        2 * local // UNIT,
        width // UNIT,
        width // UNIT,
        width // UNIT,
    )
    bounds = [sum(counts[:at]) for at in range(len(counts) + 1)]

    def by_kind(at, bodies):
        for kind, one in enumerate(bodies):

            @pl.when((at >= bounds[kind]) & (at < bounds[kind + 1]))
            def _():
                one(at - bounds[kind])

    def block(at, size=UNIT):
        return pl.ds(pl.multiple_of(at * size, size), size)

    def summed(one):
        parts = [one(image) for image in range(images)]
        return functools.reduce(jnp.add, parts)

    def product(at, half):
        cols = pl.ds(pl.multiple_of(half * local, local), local)
        query_rows = pl.ds(pl.multiple_of(stream * rows, rows), rows)

        def down(index):
            acc[...] = summed(
                lambda i: dot(
                    held["G"][i, half, :, block(index // 2)],
                    held["dF"][i, :, block(index % 2, local)],
                    TN,
                )
            )

        def up(index):
            per = width // UNIT
            acc[...] = summed(
                lambda i: dot(
                    held["M"][i, :, block(index % per)],
                    held["dU"][i, half, :, block(index // per, local)],
                    TN,
                )
            )

        def out(index):
            acc[...] = summed(
                lambda i: dot(
                    held["O"][i, :, block(half * (local // UNIT) + index // 2)],
                    held["dA"][i, :, block(index % 2, local)],
                    TN,
                )
            )

        def over_keys(name):
            def part(index, keys):
                return summed(
                    lambda i: dot(held["N"][i, keys, block(index)], held[name][i, keys, cols], TN)
                )

            def run(index):
                acc[...] = part(index, slice(0, rows))

                @pl.when(stream == 1)
                def _():
                    acc[...] += part(index, slice(rows, None))

            return run

        def query(index):
            acc[...] = summed(
                lambda i: dot(held["N"][i, query_rows, block(index)], held["dQ"][i, :, cols], TN)
            )

        by_kind(at, (down, up, out, over_keys("dK"), over_keys("dV"), query))

    def chunks(body):
        def step(index, carry):
            body(pl.multiple_of(index * 32, 32))
            return carry

        lax.fori_loop(0, UNIT // 32, step, 0)

    def half_copy(slot, at):
        return remote(
            unit(gives, slot), unit(own_half, at), half_send.at[slot], half_recv.at[at], partner
        )

    def unit_of(step, index):
        second = index * (3 - index) // 2
        own = index // 2
        wide_unit = 2 * step + 1 - column + own * (2 * column - 1)
        return wide_unit + second * (2 * wide + 2 * step + own - wide_unit), second

    def make(now):
        def body(turn, carry):
            index, mine = turn % 4, turn // 4
            step = now + 1 - mine
            at, second = unit_of(step, index)

            @pl.when((now == -1) & (turn == 1))
            def _():
                load(soon[2:], "wait")

            @pl.when((step >= 0) & (step < wide) & (second * step < deep))
            def _():
                product(at, 1 - mine)

                @pl.when(mine == 0)
                def _():
                    slot = (4 * step + index) % GIVE

                    @pl.when(4 * step >= GIVE)
                    def _():
                        half_copy(slot, at).wait_send()

                    def convert(offset):
                        gives[pl.ds(pl.multiple_of(slot * UNIT + offset, 32), 32), :] = acc[
                            pl.ds(offset, 32), :
                        ].astype(BF)

                    chunks(convert)
                    half_copy(slot, at).start()

                @pl.when(mine == 1)
                def _():
                    half_copy(0, at).wait_recv()

                    def join(offset):
                        where = pl.ds(pl.multiple_of(at * UNIT + offset, 32), 32)
                        total[where, :] = (
                            acc[pl.ds(offset, 32), :] + own_half[where, :].astype(F32)
                        ).astype(BF)

                    chunks(join)

                    @pl.when(index == 0)
                    def _():
                        x1(step).start()

                    for direction in range(2):

                        @pl.when((index == 1 + direction) & (ranks[direction] == 0))
                        def _():
                            z1(direction, step).start()

            return carry

        lax.fori_loop(0, 8, body, 0)

    def add(target, at, first, first_at, second, second_at):
        def body(index, carry):
            offset = index * 32
            left = first[pl.ds(pl.multiple_of(first_at * UNIT + offset, 32), 32), :]
            right = second[pl.ds(pl.multiple_of(second_at * UNIT + offset, 32), 32), :]
            target[pl.ds(pl.multiple_of(at * UNIT + offset, 32), 32), :] = (
                left.astype(F32) + right.astype(F32)
            ).astype(BF)
            return carry

        lax.fori_loop(0, UNIT // 32, body, 0)

    def x1(at):
        return remote(
            unit(total, 2 * at + 1 - column), unit(from_column, at), x1_send.at[at], x1_recv.at[at], side
        )

    def x2(direction, at, ahead=1):
        slot = direction * (wide // 2) + at
        return remote(
            unit(total, 4 * at + 2 * direction + column),
            unit(from_line, slot),
            x2_send.at[slot],
            x2_recv.at[slot],
            along(direction, ahead),
        )

    def z1(direction, at):
        slot = direction * deep + at
        return remote(
            unit(total, 2 * wide + 2 * at + direction),
            unit(from_deep, slot),
            z1_send.at[slot],
            z1_recv.at[slot],
            along(direction, 1),
        )

    def z2(direction, at):
        return remote(
            unit(total, 2 * wide + 2 * at + direction),
            unit(from_side, at // 2),
            z2_send.at[at // 2],
            z2_recv.at[at // 2],
            side,
        )

    def finished(at, send, recv, slot, device):
        return remote(unit(done, at), unit(done, at), send.at[slot], recv.at[slot], device)

    def ax(at, sent):
        parity = column if sent else 1 - column
        return finished(2 * at + parity, ax_send, ax_recv, at, side)

    def a2(direction, at):
        slot = direction * (wide // 2) + at
        return finished(
            4 * at + 2 * direction + column, a2_send, a2_recv, slot, along(direction, -1)
        )

    def a1(direction, at):
        slot = direction * deep + at
        return finished(
            2 * wide + 2 * at + direction, a1_send, a1_recv, slot, along(direction, -1)
        )

    def a4(direction, at):
        return finished(2 * wide + 2 * at + direction, a4_send, a4_recv, at // 2, side)

    def put(at):
        def send(target):
            pltpu.make_async_copy(unit(done, at), target, out_sem.at[at]).start()

        def by_rows(ref):
            return lambda index: send(ref.at[block(index // 2), block(index % 2, local)])

        def up(index):
            per = width // UNIT
            send(up_ref.at[block(index % per), block(index // per, local)])

        def part(which):
            return lambda index: send(qkv_ref.at[which, block(index), :])

        by_kind(at, (by_rows(down_ref), up, by_rows(out_ref), part(1), part(2), part(0)))

    def small_phase(step):
        @pl.when(step == 2)
        def _():
            small_out.wait_recv()
            small_own[0:8, :] = small_ref[0:8, :] + small_half[0:8, :]
            small_own[8:16, :] = small_ref[8:16, :] + small_half[16:24, :]
            small_side_copy().start()

        @pl.when(step == 4)
        def _():
            small_side_copy().wait_recv()
            small_line[place] = small_own[...] + small_side[...]
            for ahead in range(1, line):
                small_line_copy(ahead).start()

        @pl.when(step == 8)
        def _():
            for ahead in range(1, line):
                small_line_copy(ahead).wait_recv()
            summed = small_line[0]
            for at in range(1, line):
                summed = summed + small_line[at]
            totals_ref[...] = summed
            small_mirror_copy().start()

    def small_side_copy():
        return remote(small_own, small_side, s_send.at[2], s_recv.at[1], side)

    def small_line_copy(ahead):
        there = (place + ahead) % line
        return remote(
            small_line.at[place],
            small_line.at[place],
            s_send.at[2 + ahead],
            s_recv.at[1 + ahead],
            {"dp": there * 2 + column},
        )

    def small_mirror_copy():
        return remote(
            totals_ref, other_ref, s_send.at[2 + line], s_recv.at[1 + line], mirror
        )

    def step_body(step, carry):
        @pl.when(step == 3)
        def _():
            load(rest, "wait")

        make(step)

        at = step - LAG

        @pl.when((at >= 0) & (at < wide))
        def _():
            x1(at).wait_recv()
            add(total, 2 * at + column, total, 2 * at + column, from_column, at)
            for direction in range(2):

                @pl.when((at % 2 == direction) & (ranks[direction] == 0))
                def _():
                    x2(direction, at // 2).start()

        for direction in range(2):
            rank = ranks[direction]
            at = step - LAG * rank

            @pl.when((rank >= 1) & (at >= 0) & (at < deep))
            def _():
                where = 2 * wide + 2 * at + direction
                z1(direction, at).wait_recv()
                add(total, where, total, where, from_deep, direction * deep + at)

                @pl.when(rank < line - 1)
                def _():
                    z1(direction, at).start()

                @pl.when((rank == line - 1) & (at % 2 != column))
                def _():
                    z2(direction, at).start()

            twice = step - LAG - LAG * rank - direction

            @pl.when((rank >= 1) & (twice >= 0) & (twice < wide) & (twice % 2 == 0))
            def _():
                at = twice // 2
                where = 4 * at + 2 * direction + column
                x2(direction, at).wait_recv()
                slot = direction * (wide // 2) + at

                @pl.when(rank < line - 1)
                def _():
                    add(total, where, total, where, from_line, slot)
                    x2(direction, at).start()

                @pl.when(rank == line - 1)
                def _():
                    add(done, where, total, where, from_line, slot)
                    a2(direction, at).start()
                    ax(2 * at + direction, True).start()
                    put(where)

            at = step - LAG * line

            @pl.when((rank == line - 1) & (at >= 0) & (at < deep) & (at % 2 == column))
            def _():
                where = 2 * wide + 2 * at + direction
                z2(direction, at).wait_recv()
                add(done, where, total, where, from_side, at // 2)
                a1(direction, at).start()
                a4(direction, at).start()
                put(where)

            later = step - LAG * line - LAG

            @pl.when((rank == line - 1) & (later >= 0) & (later < deep) & (later % 2 != column))
            def _():
                a4(direction, later).wait_recv()
                a1(direction, later).start()
                put(2 * wide + 2 * later + direction)

            back = LAG * (line - 1 - rank)
            twice = step - LAG * line - back - direction

            @pl.when((rank < line - 1) & (twice >= 0) & (twice < wide) & (twice % 2 == 0))
            def _():
                at = twice // 2
                a2(direction, at).wait_recv()

                @pl.when(rank > 0)
                def _():
                    a2(direction, at).start()

                ax(2 * at + direction, True).start()
                put(4 * at + 2 * direction + column)

            for other in range(2):
                at = step - LAG * line - back - LAG * other

                @pl.when(
                    (rank < line - 1)
                    & (at >= 0)
                    & (at < deep)
                    & ((at + column) % 2 == other)
                )
                def _():
                    a1(direction, at).wait_recv()

                    @pl.when(rank > 0)
                    def _():
                        a1(direction, at).start()

                    put(2 * wide + 2 * at + direction)

            twice = step - LAG * line - back - direction - LAG

            @pl.when((twice >= 0) & (twice < wide) & (twice % 2 == 0))
            def _():
                at = twice + direction
                ax(at, False).wait_recv()
                put(2 * at + 1 - column)

        small_phase(step)
        return carry

    steps = wide - 1 + LAG * line + LAG * (line - 1) + LAG + 1
    load(soon[:2], "wait")
    lax.fori_loop(-1, steps, step_body, 0)

    small_mirror_copy().wait()
    small_out.wait_send()
    small_side_copy().wait_send()
    for ahead in range(1, line):
        small_line_copy(ahead).wait_send()

    def drain(at, carry):
        pltpu.make_async_copy(unit(done, at), unit(done, at), out_sem.at[at]).wait()
        return carry

    lax.fori_loop(0, Exchange.UNITS, drain, 0)

    def drain_give(slot, carry):
        half_copy(slot, 0).wait_send()
        return carry

    lax.fori_loop(0, GIVE, drain_give, 0)

    def drain_wide(at, carry):
        x1(at).wait_send()
        ax(at, True).wait_send()
        return carry

    lax.fori_loop(0, wide, drain_wide, 0)
    for direction in range(2):
        rank = ranks[direction]

        def drain_line(at, carry):
            @pl.when(rank < line - 1)
            def _():
                x2(direction, at).wait_send()

            @pl.when(rank > 0)
            def _():
                a2(direction, at).wait_send()

            return carry

        lax.fori_loop(0, wide // 2, drain_line, 0)

        def drain_deep(at, carry):
            @pl.when(rank < line - 1)
            def _():
                z1(direction, at).wait_send()

            @pl.when(rank > 0)
            def _():
                a1(direction, at).wait_send()

            @pl.when((rank == line - 1) & (at % 2 != column))
            def _():
                z2(direction, at).wait_send()

            @pl.when((rank == line - 1) & (at % 2 == column))
            def _():
                a4(direction, at).wait_send()

            return carry

        lax.fori_loop(0, deep, drain_deep, 0)


def exchange(enc_operands, reg_operands, vec_grads, bias_grads, width, local, hidden):
    units, wide, deep = Exchange.UNITS, Exchange.WIDE, Exchange.DEEP
    images = len(enc_operands)

    def buffer(count, dtype=BF):
        return pltpu.VMEM((count * UNIT, local), dtype)

    def sems(*counts):
        return [pltpu.SemaphoreType.DMA((count,)) for count in counts]

    line = Exchange.LINE
    vspec = pl.BlockSpec(memory_space=pltpu.VMEM)
    return pl.pallas_call(
        functools.partial(exchange_kernel, images),
        out_shape=[
            jax.ShapeDtypeStruct((1, hidden, width), BF),
            jax.ShapeDtypeStruct((1, width, hidden), BF),
            jax.ShapeDtypeStruct((1, local, width), BF),
            jax.ShapeDtypeStruct((1, 3, width, local), BF),
            jax.ShapeDtypeStruct((16, width), F32),
            jax.ShapeDtypeStruct((16, width), F32),
        ],
        in_specs=[ANY] * (2 * images * len(OPERANDS)) + [vspec] * (2 * images),
        out_specs=[ANY] * 4 + [vspec, vspec],
        scratch_shapes=[pltpu.VMEM((images,) + one.shape, BF) for one in reg_operands[0]]
        + [
            buffer(1, F32),
            buffer(GIVE),
            buffer(units),
            buffer(units),
            buffer(wide),
            buffer(wide),
            buffer(2 * deep),
            buffer(deep // 2),
            buffer(units),
            pltpu.VMEM((24, width), F32),
            pltpu.VMEM((16, width), F32),
            pltpu.VMEM((24, width), F32),
            pltpu.VMEM((16, width), F32),
            pltpu.VMEM((line, 16, width), F32),
            pltpu.SemaphoreType.DMA((len(OPERANDS), images)),
        ]
        + sems(GIVE, units, wide, wide, wide, wide, 2 * deep, 2 * deep)
        + sems(deep // 2, deep // 2, wide, wide, wide, wide, 2 * deep, 2 * deep)
        + sems(deep // 2, deep // 2, units, 3 + line, 2 + line),
        compiler_params=params_of(collective_id=0, has_side_effects=True),
        cost_estimate=pl.CostEstimate(flops=0, bytes_accessed=200_000_000, transcendentals=0),
        name="gradient_exchange",
    )(*sum(enc_operands, []), *sum(reg_operands, []), *vec_grads, *bias_grads)


def finish_results(sums, inputs, totals, other, bias_blocks):
    steps = 8
    down, up, out, qkv = sums
    rows, width = inputs[0].shape
    hidden = down.shape[1]

    def rows_spec(array, axis):
        block = list(array.shape)
        block[axis] //= steps
        return pl.BlockSpec(
            tuple(block), lambda i: tuple(i if at == axis else 0 for at in range(len(block)))
        )

    specs = [rows_spec(one, 1) for one in (down, up, out)] + [rows_spec(qkv, 2)]
    stacked = jax.ShapeDtypeStruct((1, len(inputs), rows, width), F32)
    small = [(1, 2, width)] * 3 + [(1, hidden), (1, width), (width,)]

    def fixed(shape):
        return pl.BlockSpec(shape, lambda i: (0,) * len(shape))

    def kernel(*refs):
        sum_refs, input_refs = refs[:4], refs[4 : 4 + len(inputs)]
        refs = refs[4 + len(inputs) :]
        totals_ref, other_ref, refs = refs[0], refs[1], refs[2:]
        for source, target in zip(sum_refs, refs[:4]):
            target[...] = source[...].astype(F32)
        for at, source in enumerate(input_refs):
            refs[4][0, at] = source[...]
        gains, biases, scales, bias, down_bias, token = refs[5:]

        @pl.when(pl.program_id(0) == 0)
        def _():
            for at, target in enumerate((gains, biases, scales)):
                target[0] = totals_ref[2 * at : 2 * at + 2, :]
            for at in range(bias_blocks):
                bias[:, at * width : (at + 1) * width] = totals_ref[8 + at : 9 + at, :]
            down_bias[...] = totals_ref[6:7, :]

            @pl.when(lax.axis_index("stream") == 0)
            def _():
                token[...] = other_ref[7, :]

            @pl.when(lax.axis_index("stream") == 1)
            def _():
                token[...] = totals_ref[7, :]

    return pl.pallas_call(
        kernel,
        grid=(steps,),
        out_shape=[jax.ShapeDtypeStruct(one.shape, F32) for one in sums]
        + [stacked]
        + [jax.ShapeDtypeStruct(one, F32) for one in small],
        in_specs=specs
        + [rows_spec(one, 0) for one in inputs]
        + [fixed(totals.shape), fixed(other.shape)],
        out_specs=specs + [rows_spec(stacked, 2)] + [fixed(one) for one in small],
        compiler_params=params_of(),
        name="finish_results",
    )(*sums, *inputs, totals, other)


def place_code(positions, model_width):
    half_width = model_width // 2
    frequency = jnp.exp(
        jnp.arange(half_width, dtype=F32) * (-math.log(10000.0) / half_width)
    )
    angles = positions.astype(F32)[..., None] * frequency
    return jnp.sin(jnp.concatenate([angles, angles + 0.5 * math.pi], -1))


def shards(
    patches,
    order,
    cotangent,
    norm_gains,
    norm_biases,
    layer_scales,
    qkv_weight,
    out_weight,
    up_weight,
    up_bias,
    down_weight,
    down_bias,
    mask_token,
):
    images, places, width = patches.shape
    rows = places // 2
    hidden = up_weight.shape[2]
    local = width // 2
    encoder = lax.axis_index("stream") == 0

    def swapped(value):
        return lax.ppermute(value, "head", SWAP)

    own = (qkv_weight[0], out_weight[0], up_weight[0], down_weight[0])
    matrices = []
    for value in own:
        matrices += [value, swapped(value)]
    bias_pair = jnp.stack([up_bias[0], swapped(up_bias[0])]).astype(F32)[:, None, :]
    vec = jnp.concatenate(
        [
            norm_gains[0],
            norm_biases[0],
            layer_scales[0],
            down_bias[0][None],
            jnp.zeros((1, width), F32),
        ]
    )
    token = mask_token[None]
    cotangent = cotangent[0]
    order_column = order[:, :, None]
    order_row = order[:, None, :]

    kept_list = list(kept_shapes(rows, rows, width, hidden).values())
    row_shape = ((rows, width), BF)
    code_shape = ((images, places, width), F32)
    grad_list = list(grad_shapes(rows, rows, width, hidden).values())
    operand_list = operand_shapes(rows, places, width, hidden)

    kept, latents = [], []
    codes = None
    for image in range(images):

        def run_encoder():
            outs = encoder_forward(
                image, 0, patches, order_column, vec, up_bias=bias_pair, matrices=matrices, save=True
            )
            return tuple(outs) + ((nothing([code_shape])[0],) if image == 0 else ())

        def run_other():
            outs = nothing([row_shape] + kept_list)
            return tuple(outs) + ((place_code(order, width),) if image == 0 else ())

        outs = lax.cond(encoder, run_encoder, run_other)
        if image == 0:
            codes = outs[-1]
            outs = outs[:-1]
        latents.append(outs[0])
        kept.append(outs[1:])
    arrived = [lax.ppermute(one, "stream", [(0, 1)]) for one in latents]

    features, returned, reg_inputs, reg_vecs, reg_biases, reg_operands = [], [], [], [], [], []
    for image in range(images):

        def run_targets():
            rest = tuple(
                nothing(
                    [row_shape, row_shape, ((places, width), F32)]
                    + [((8, width), F32), ((2, 1, hidden), F32)]
                    + operand_list
                )
            )
            if image == 0:
                rest += tuple(
                    encoder_forward(
                        None, 1, patches, order_column, vec, bias_pair, matrices, save=False
                    )
                )
            return rest

        def run_regressor():
            outs = regressor_block(
                image, arrived[image], codes, token, cotangent, vec, bias_pair, matrices
            )
            if image == 0:
                outs = tuple(outs) + tuple(nothing([((images, rows, width), BF)]))
            return tuple(outs)

        outs = lax.cond(encoder, run_targets, run_regressor)
        if image == 0:
            targets = outs[-1]
            outs = outs[:-1]
        features.append(outs[0])
        returned.append(lax.ppermute(outs[1], "stream", [(1, 0)]))
        reg_inputs.append(outs[2])
        reg_vecs.append(outs[3])
        reg_biases.append(outs[4])
        reg_operands.append(list(outs[5:]))

    input_grads, vec_grads, bias_grads, enc_operands = [], [], [], []
    for image in range(images):

        def run_backward():
            return encoder_backward(
                image, returned[image], cotangent, order_row, kept[image], vec, matrices
            )

        def run_pass():
            return (reg_inputs[image], reg_vecs[image], reg_biases[image]) + tuple(
                nothing(grad_list)
            )

        outs = lax.cond(encoder, run_backward, run_pass)
        input_grads.append(outs[0])
        vec_grads.append(outs[1])
        bias_grads.append(outs[2])
        named = dict(zip(KEPT, kept[image]))
        named.update(zip(GRADS, outs[3:]))
        enc_operands.append([named[name] for name in OPERANDS])

    if lax.axis_size("dp") == 2 * Exchange.LINE and width == 768 and hidden == 1536:
        down, up, out, qkv, totals, other = exchange(
            enc_operands, reg_operands, vec_grads, bias_grads, width, local, hidden
        )
        outs = finish_results(
            (down, up, out, qkv), input_grads, totals, other, hidden // width
        )
        down, up, out, qkv, input_grad = outs[:5]
        gains, biases, scales, bias_total, down_bias_total, token_grad = outs[5:]
    else:
        parts = lax.cond(
            encoder,
            lambda: matrix_grads(enc_operands, 0),
            lambda: matrix_grads(reg_operands, rows),
        )
        vec_grad = sum(vec_grads)
        bias_grad = sum(bias_grads)[:, 0]

        def reduced(value):
            mine = value[0].astype(F32) + swapped(value[1]).astype(F32)
            part = lax.psum_scatter(mine.astype(BF), "dp", scatter_dimension=0, tiled=True)
            return lax.all_gather(part, "dp", axis=0, tiled=True).astype(F32)

        down, up, out, query, key, value = (reduced(one) for one in parts)
        qkv = jnp.stack([query, key, value])
        qkv, out, up, down = (one[None] for one in (qkv, out, up, down))
        bias_total = lax.psum(bias_grad[0] + swapped(bias_grad[1]), "dp")
        totals = lax.psum(vec_grad, ("dp", "head"))
        token_grad = lax.psum(jnp.where(encoder, 0.0, totals[7]), "stream")
        bias_total = bias_total[None]
        input_grad = jnp.stack(input_grads)[None]
        gains, biases, scales = (totals[at : at + 2][None] for at in (0, 2, 4))
        down_bias_total = totals[6][None]

    latent_out = jnp.where(encoder, jnp.stack(latents), jnp.stack(arrived))
    return (
        latent_out,
        jnp.where(encoder, targets, jnp.stack(features))[None],
        input_grad,
        gains,
        biases,
        scales,
        qkv,
        out,
        up,
        bias_total,
        down,
        down_bias_total,
        token_grad,
    )


def solution(mesh):
    in_specs = (
        P(("dp", "head"), None, None),
        P(("dp", "head"), None),
        P("stream", ("dp", "head"), None, None),
        P("stream", None, None),
        P("stream", None, None),
        P("stream", None, None),
        P("stream", None, None, "head"),
        P("stream", "head", None),
        P("stream", None, "head"),
        P("stream", "head"),
        P("stream", "head", None),
        P("stream", None),
        P(),
    )
    out_specs = (
        P(("dp", "head"), None, None),
        P("stream", ("dp", "head"), None, None),
        P("stream", ("dp", "head"), None, None),
        P("stream", None, None),
        P("stream", None, None),
        P("stream", None, None),
        P("stream", None, None, "head"),
        P("stream", "head", None),
        P("stream", None, "head"),
        P("stream", "head"),
        P("stream", "head", None),
        P("stream", None),
        P(),
    )
    return jax.shard_map(shards, mesh=mesh, in_specs=in_specs, out_specs=out_specs, check_vma=False)
```
